32 devices in a mesh: wide: 8 (over z, y), narrow: 4 (over x, core).
Axes of the slice: x: 2, y: 2, z: 4, core: 2. Of those that a mesh axis runs over, the one named last changes fastest.
Arguments:
- tokens: bfloat16 [12288, 768], P(('wide', 'narrow')), may hold values from -6 to 6
- buckets: int32 [12288], P(('wide', 'narrow')), may hold values from 0 to 255
- lengths: int32 [8, 3], P('wide'), may hold values from 1 to 1024, 1536 in all within a row
- type_table: bfloat16 [256, 768], replicated, may hold values from -3 to 3
- query_weight: bfloat16 [2, 768, 768], P(None, None, 'narrow'), may hold values from -0.3125 to 0.3125
- query_bias: bfloat16 [2, 768], P(None, 'narrow'), may hold values from -2 to 2
- key_weight: bfloat16 [2, 768, 768], P(None, None, 'narrow'), may hold values from -0.21875 to 0.21875
- value_weight: bfloat16 [2, 768, 768], P(None, None, 'narrow'), may hold values from -0.21875 to 0.21875
- value_bias: bfloat16 [2, 768], P(None, 'narrow'), may hold values from -2 to 2
- output_weight: bfloat16 [2, 768, 768], P(None, 'narrow'), may hold values from -1.25 to 1.25
- output_bias: bfloat16 [2, 768], replicated, may hold values from -2 to 2
- attention_gain: bfloat16 [2, 768], replicated, may hold values from 0.5 to 1.5
- attention_shift: bfloat16 [2, 768], replicated, may hold values from -2 to 2
- up_weight: bfloat16 [2, 768, 3072], P(None, None, 'narrow'), may hold values from -0.21875 to 0.21875
- up_bias: bfloat16 [2, 3072], P(None, 'narrow'), may hold values from -2 to 2
- down_weight: bfloat16 [2, 3072, 768], P(None, 'narrow'), may hold values from -0.109375 to 0.109375
- down_bias: bfloat16 [2, 768], replicated, may hold values from -2 to 2
- feed_gain: bfloat16 [2, 768], replicated, may hold values from 0.5 to 1.5
- feed_shift: bfloat16 [2, 768], replicated, may hold values from -2 to 2
- cotangent: bfloat16 [12288, 768], P(('wide', 'narrow')), may hold values from -6 to 6
Outputs:
- encoded: bfloat16 [12288, 768], P(('wide', 'narrow'))
- tokens_grad: float32 [12288, 768], P(('wide', 'narrow'))
- table_grad: float32 [256, 768], replicated
- query_weight_grad: float32 [2, 768, 768], P(None, None, 'narrow')
- query_bias_grad: float32 [2, 768], P(None, 'narrow')
- key_weight_grad: float32 [2, 768, 768], P(None, None, 'narrow')
- value_weight_grad: float32 [2, 768, 768], P(None, None, 'narrow')
- value_bias_grad: float32 [2, 768], P(None, 'narrow')
- output_weight_grad: float32 [2, 768, 768], P(None, 'narrow')
- output_bias_grad: float32 [2, 768], replicated
- attention_gain_grad: float32 [2, 768], replicated
- attention_shift_grad: float32 [2, 768], replicated
- up_weight_grad: float32 [2, 768, 3072], P(None, None, 'narrow')
- up_bias_grad: float32 [2, 3072], P(None, 'narrow')
- down_weight_grad: float32 [2, 3072, 768], P(None, 'narrow')
- down_bias_grad: float32 [2, 768], replicated
- feed_gain_grad: float32 [2, 768], replicated
- feed_shift_grad: float32 [2, 768], replicated
The draws below stay inside these ranges and needn't reach their ends.
Inputs may be any that keep to these rules, and one draw needn't show every extreme that they name: In each row the lengths sum to 1536 and the largest is exactly 1024.
All inputs are finite; a program needn't handle non-finite values.
Results may differ from the reference program's by a relative error of at most 0.035.
Values may be sent and summed in bfloat16 or wider, within the bound.
No kernel may reach another device: no remote copies, remote signals or barrier semaphores. Data moves between devices by JAX's collectives and lax.ppermute only.
A program may use at most 128 MiB of HBM per device.

```python
import math
import jax
import jax.numpy as jnp
import numpy as np
from jax import lax

D = 768
HEADS = 12
HEAD_DIM = 64
FF = 3072
BUCKETS = 256
LAYERS = 2
MAXLEN = 1024
ITEMS_DEV = 3
TOK_DEV = 1536
TOKENS = 12288
N_WIDE = 8


def touch_ends(values, key, low, high):
    longest = values.shape.index(max(values.shape))
    spots = []
    for shift in (0, 1):
        where = [jax.random.randint(jax.random.fold_in(key, axis), (), 0, length) for axis, length in enumerate(values.shape)]
        where[longest] = (where[longest] + shift) % values.shape[longest]
        spots.append(tuple(where))
    return values.at[spots[0]].set(low).at[spots[1]].set(high)


def shard_levels(stream_key, dims, split, low, largest):
    def one(position, blocks):
        heights = jax.random.uniform(jax.random.fold_in(jax.random.fold_in(stream_key, 6), position), (blocks,), jnp.float32, low / len(split), largest / len(split))
        return jnp.repeat(jnp.exp(heights), dims[position] // blocks).reshape((-1,) + (1,) * (len(dims) - position - 1))

    level = one(*split[0])
    for cut in split[1:]:
        level = level * one(*cut)
    return level


def split_up(amount, total, limit, slope):
    loads = [(1 << 20) // math.isqrt(standing ** slope) + 1 for standing in range(2, amount + 1)]
    spare, given = total - limit - (amount - 1), [1] * (amount - 1)
    while spare > 0:
        free = [i for i in range(amount - 1) if given[i] < limit]
        mass, left = sum([loads[i] for i in free]), spare
        for i in free:
            addition = min(limit - given[i], max(1, left * loads[i] // mass), spare)
            given[i] = given[i] + addition
            spare = spare - addition
    return np.array([limit] + given)


def uneven_parts(rng, count, total, reach, slope):
    if count == 2:
        one = jax.random.randint(rng, (), max(1, total - reach), min(reach, total - 1) + 1)
        return jnp.stack([one, total - one])
    tallies = jnp.asarray(split_up(count, total, reach, slope), jnp.int32)
    couples = (count - 1) // 2
    giver, sink = tallies[1:1 + 2 * couples:2], tallies[2:2 + 2 * couples:2]
    slack = jnp.minimum(giver - 1, reach - sink)
    moved = jax.random.randint(jax.random.fold_in(rng, 1), (couples,), 0, 1 << 20) % (slack + 1)
    tallies = tallies.at[1:1 + 2 * couples:2].set(giver - moved).at[2:2 + 2 * couples:2].set(sink + moved)
    return tallies[jax.random.permutation(jax.random.fold_in(rng, 2), count)]


def scatter_about(key, extent, scale, limit, cuts=(), kind=jnp.bfloat16):
    values = jax.random.normal(key, extent, jnp.float32) * scale
    if len(cuts) > 0:
        values = shard_levels(key, extent, cuts, -0.22, 0.18) * values
    return jnp.clip(values, min=-limit, max=limit).astype(kind)


def setup_inputs(seed: int = 0) -> dict:
    splits = jax.random.split(jax.random.key(seed), 21)
    return {
        "tokens": scatter_about(splits[0], (TOKENS, D), 1.0, 6.0, ((0, 32),)),
        "buckets": touch_ends(jax.random.randint(splits[1], (TOKENS,), 0, BUCKETS), jax.random.fold_in(splits[1], 1), 0, BUCKETS - 1).astype(jnp.int32),
        "lengths": jax.vmap(lambda own: uneven_parts(own, ITEMS_DEV, TOK_DEV, MAXLEN, 2))(jax.random.split(splits[2], N_WIDE)).reshape((N_WIDE, ITEMS_DEV)).astype(jnp.int32),
        "type_table": scatter_about(splits[3], (BUCKETS, D), 0.5, 3.0),
        "query_weight": scatter_about(splits[4], (LAYERS, D, D), (D // 2) ** -0.5, 0.3125, ((2, 4),)),
        "query_bias": scatter_about(splits[5], (LAYERS, D), 0.3, 2.0, ((1, 4),)),
        "key_weight": scatter_about(splits[6], (LAYERS, D, D), D ** -0.5, 0.21875, ((2, 4),)),
        "value_weight": scatter_about(splits[7], (LAYERS, D, D), D ** -0.5, 0.21875, ((2, 4),)),
        "value_bias": scatter_about(splits[8], (LAYERS, D), 0.3, 2.0, ((1, 4),)),
        "output_weight": scatter_about(splits[9], (LAYERS, D, D), (D // 32) ** -0.5, 1.25, ((1, 4),)),
        "output_bias": scatter_about(splits[10], (LAYERS, D), 0.3, 2.0),
        "attention_gain": jnp.clip(1.0 + 0.1 * jax.random.normal(splits[11], (LAYERS, D), jnp.float32), 0.5, 1.5).astype(jnp.bfloat16),
        "attention_shift": scatter_about(splits[12], (LAYERS, D), 0.3, 2.0),
        "up_weight": scatter_about(splits[13], (LAYERS, D, FF), D ** -0.5, 0.21875, ((2, 4),)),
        "up_bias": scatter_about(splits[14], (LAYERS, FF), 0.3, 2.0, ((1, 4),)),
        "down_weight": scatter_about(splits[15], (LAYERS, FF, D), FF ** -0.5, 0.109375, ((1, 4),)),
        "down_bias": scatter_about(splits[16], (LAYERS, D), 0.3, 2.0),
        "feed_gain": jnp.clip(1.0 + 0.1 * jax.random.normal(splits[17], (LAYERS, D), jnp.float32), 0.5, 1.5).astype(jnp.bfloat16),
        "feed_shift": scatter_about(splits[18], (LAYERS, D), 0.3, 2.0),
        "cotangent": scatter_about(splits[19], (TOKENS, D), 1.0, 6.0, ((0, 32),)),
    }


@jax.custom_vjp
def low(v):
    return lax.optimization_barrier(v.astype(jnp.bfloat16)).astype(jnp.float32)

@jax.custom_vjp
def low_back(v):
    return v

def low_keep(v):
    return (low(v), None)

def low_pass(kept, grad):
    return (grad,)

def back_keep(v):
    return (v, None)

def back_low(kept, grad):
    return (low(grad),)
low.defvjp(low_keep, low_pass)
low_back.defvjp(back_keep, back_low)
EPS = 1e-12
ROOT_HALF = 0.7071067811865476
NEG = -1e+30

def round_both(value):
    return low(low_back(value))

def product(left_side, right_side):
    return jnp.dot(left_side, right_side, precision=lax.Precision.HIGHEST)

def layer_norm(summed, gain_row, shift_row):
    row_mean = lax.optimization_barrier(jnp.mean(summed, -1, keepdims=True))
    centred = summed - row_mean
    spread = lax.optimization_barrier(jnp.mean(centred * centred, -1, keepdims=True))
    return centred * lax.rsqrt(spread + EPS) * gain_row + shift_row

def gelu_exact(preact):
    return 0.5 * preact * (1.0 + jax.scipy.special.erf(preact * ROOT_HALF))

def group_attention(pieces):
    queries, key_rows, values, labels = pieces
    scores = low_back(jnp.einsum('qhd,khd->hqk', queries, key_rows, precision=lax.Precision.HIGHEST))
    same_item = labels[:, None] == labels[None, :]
    scores = jnp.where(same_item[None], scores, NEG)
    probability = low(jax.nn.softmax(scores, axis=-1))
    return jnp.einsum('hqk,khd->qhd', probability, values, precision=lax.Precision.HIGHEST)

def encoder_layer(stream, weights, labels):
    query_weight, query_bias, key_weight, value_weight, value_bias, output_weight, output_bias, attention_gain, attention_shift, up_weight, up_bias, down_weight, down_bias, feed_gain, feed_shift = weights
    query_scale = HEAD_DIM ** (-0.5)
    low_in = low(stream)
    queries = round_both((product(low_in, query_weight) + query_bias) * query_scale)
    key_rows = round_both(product(low_in, key_weight))
    values = round_both(product(low_in, value_weight) + value_bias)
    shaped = (N_WIDE, TOK_DEV, HEADS, HEAD_DIM)
    context = lax.map(jax.checkpoint(group_attention), (queries.reshape(shaped), key_rows.reshape(shaped), values.reshape(shaped), labels))
    context = round_both(context.reshape(N_WIDE * TOK_DEV, HEADS * HEAD_DIM))
    summed = stream + low_back(product(context, output_weight)) + output_bias
    middle = layer_norm(summed, attention_gain, attention_shift)
    up_values = low_back(product(low(middle), up_weight) + up_bias)
    activation = low(gelu_exact(up_values))
    second = middle + low_back(product(activation, down_weight)) + down_bias
    return layer_norm(second, feed_gain, feed_shift)

def reference(tokens, buckets, lengths, type_table, query_weight, query_bias, key_weight, value_weight, value_bias, output_weight, output_bias, attention_gain, attention_shift, up_weight, up_bias, down_weight, down_bias, feed_gain, feed_shift, cotangent):
    item_ends = jnp.cumsum(lengths, axis=1, dtype=jnp.int32)
    places = jnp.arange(TOK_DEV, dtype=jnp.int32)
    labels = lax.optimization_barrier(jnp.sum((places[None, :, None] >= item_ends[:, None, :]).astype(jnp.int32), axis=2, dtype=jnp.int32))
    floats = [array.astype(jnp.float32) for array in (tokens, type_table, query_weight, query_bias, key_weight, value_weight, value_bias, output_weight, output_bias, attention_gain, attention_shift, up_weight, up_bias, down_weight, down_bias, feed_gain, feed_shift)]

    def forward(*arrays):
        stream = arrays[0] + arrays[1][buckets]
        for layer_index in range(LAYERS):
            stream = encoder_layer(stream, [weight[layer_index] for weight in arrays[2:]], labels)
        return stream
    result, pullback = jax.vjp(forward, *floats)
    grads = pullback(cotangent.astype(jnp.float32))
    return (result.astype(jnp.bfloat16), grads[0], grads[1], grads[2], grads[3], grads[4], grads[5], grads[6], grads[7], grads[8], grads[9], grads[10], grads[11], grads[12], grads[13], grads[14], grads[15], grads[16])
```

```python
import functools

import jax
import jax.numpy as jnp
from jax import lax
from jax.experimental import pallas as pl
from jax.experimental.pallas import tpu as pltpu
from jax.sharding import PartitionSpec as P

HEAD_DIM = 64
LAYERS = 2
CHUNK = 256
EPS = 1e-12
ROOT_HALF = 0.7071067811865476
DENSITY = 0.3989422804014327
NEG = -1e30
F32 = jnp.float32
BF16 = jnp.bfloat16
MIB = 1 << 20
CORE_SWAP = [(0, 1), (1, 0), (2, 3), (3, 2)]
CHIP_SWAP = [(0, 2), (2, 0), (1, 3), (3, 1)]


def over_core(value):
    return lax.ppermute(value, "narrow", CORE_SWAP)


def over_chip(value):
    return lax.ppermute(value, "narrow", CHIP_SWAP)


def dot(left, right, left_axis=1, right_axis=0):
    return lax.dot_general(
        left, right, (((left_axis,), (right_axis,)), ((), ())), preferred_element_type=F32
    )


def norm_parts(summed):
    row_mean = jnp.mean(summed, -1, keepdims=True)
    centred = summed - row_mean
    spread = jnp.mean(centred * centred, -1, keepdims=True)
    inverse = lax.rsqrt(spread + EPS)
    return centred * inverse, inverse


def norm_back(upstream, unit_rows, inverse, gain_row):
    scaled = upstream * gain_row
    return inverse * (
        scaled
        - jnp.mean(scaled, -1, keepdims=True)
        - unit_rows * jnp.mean(scaled * unit_rows, -1, keepdims=True)
    )


def gelu_parts(preact):
    size = jnp.abs(preact) * ROOT_HALF
    bell = jnp.exp(-(size * size))
    step = 1.0 / (1.0 + 0.3275911 * size)
    series = step * (
        0.254829592
        + step * (-0.284496736 + step * (1.421413741 + step * (-1.453152027 + step * 1.061405429)))
    )
    tail = 0.5 * series * bell
    cdf = jnp.where(preact >= 0.0, 1.0 - tail, tail)
    return preact * cdf, cdf + preact * DENSITY * bell


def whole(shape):
    zeros = (0,) * len(shape)
    return pl.BlockSpec(shape, lambda *ids: zeros)


def call(kernel, grid, inputs, outputs, scratch=(), flops=0, moved=0, limit=40):
    arrays = [array for array, spec in inputs]
    specs = [spec for array, spec in inputs]
    aliases = {}
    for place, (shape, dtype, spec, buffer) in enumerate(outputs):
        if buffer is not None:
            aliases[len(arrays)] = place
            arrays.append(buffer)
            specs.append(pl.BlockSpec(memory_space=pl.ANY))
    given, extra, out_count = len(inputs), len(aliases), len(outputs)

    def body(*refs):
        kernel(*refs[:given], *refs[given + extra :])

    return pl.pallas_call(
        body,
        grid=grid,
        in_specs=specs,
        out_specs=[spec for shape, dtype, spec, buffer in outputs],
        out_shape=[
            jax.ShapeDtypeStruct(shape, dtype) for shape, dtype, spec, buffer in outputs
        ],
        scratch_shapes=list(scratch),
        input_output_aliases=aliases,
        compiler_params=pltpu.CompilerParams(vmem_limit_bytes=limit * MIB),
        cost_estimate=pl.CostEstimate(flops=flops, bytes_accessed=moved, transcendentals=0),
    )(*arrays)


def gather_kernel(own_ref, other_ref, rows_ref, turned_ref):
    place = pl.program_id(0)
    half = pl.num_programs(0) // 2

    def put(source):
        tile = source[0]
        rows_ref[0] = tile
        turned_ref[0] = tile.astype(F32).T.astype(BF16)

    @pl.when(place < half)
    def _():
        put(own_ref)

    @pl.when(place >= half)
    def _():
        put(other_ref)


def split_pairs(pair_block, target, head_count):
    lanes = lax.broadcasted_iota(jnp.int32, (CHUNK, 2 * HEAD_DIM), 1)
    low_half = lanes < HEAD_DIM
    for head in range(head_count):
        pair = pair_block[:, (head // 2) * 128 : (head // 2) * 128 + 128]
        keep = low_half if head % 2 == 0 else jnp.logical_not(low_half)
        target[head] = jnp.where(keep, pair, jnp.zeros_like(pair))


def attend_kernel(
    head_count,
    place,
    bits_ref,
    q_ref,
    kv_ref,
    turned_ref,
    q_label_ref,
    k_label_ref,
    out_weight_ref,
    context_ref,
    exact_ref,
    logsum_ref,
    share_ref,
    masked_q,
    total,
    top,
    mass,
):
    width = head_count * HEAD_DIM
    split_pairs(q_ref[...], masked_q, head_count)
    top[...] = jnp.full_like(top, NEG)
    mass[...] = jnp.zeros_like(mass)
    total[...] = jnp.zeros_like(total)
    tiles = kv_ref.shape[0]
    q_bits = bits_ref[tiles + place]

    def one_tile(tile, carry):
        @pl.when((bits_ref[tile] & q_bits) != 0)
        def _():
            hide = jnp.where(k_label_ref[tile] == q_label_ref[...], 0.0, NEG)
            for head in range(head_count):
                pair = (head // 2) * 128
                scores = dot(kv_ref[tile, :, pair : pair + 128], masked_q[head], 1, 1) + hide
                old_top = top[head : head + 1, :]
                new_top = jnp.maximum(old_top, jnp.max(scores, 0, keepdims=True))
                weights = jnp.exp(scores - new_top)
                fade = jnp.exp(old_top - new_top)
                top[head : head + 1, :] = new_top
                mass[head : head + 1, :] = mass[head : head + 1, :] * fade + jnp.sum(
                    weights, 0, keepdims=True
                )
                rows = slice(head * HEAD_DIM, (head + 1) * HEAD_DIM)
                total[rows, :] = total[rows, :] * fade + dot(
                    turned_ref[tile, width + head * HEAD_DIM : width + (head + 1) * HEAD_DIM, :],
                    weights.astype(BF16),
                )

        return carry

    lax.fori_loop(0, tiles, one_tile, 0)
    for head in range(head_count):
        rows = slice(head * HEAD_DIM, (head + 1) * HEAD_DIM)
        total[rows, :] = total[rows, :] / mass[head : head + 1, :]
    exact = total[...].T
    exact_ref[...] = exact
    context = exact.astype(BF16)
    context_ref[...] = context
    live = slice(0, head_count)
    logsum_ref[0] = jnp.zeros_like(logsum_ref[0])
    logsum_ref[0, live, :] = top[live, :] + jnp.log(mass[live, :])
    share_ref[...] = dot(context, out_weight_ref[0]).astype(BF16)


def attend_back_kernel(
    head_count,
    bits_ref,
    q_ref,
    kv_ref,
    turned_ref,
    q_label_ref,
    k_label_ref,
    grad_ref,
    exact_ref,
    logsum_ref,
    q_grad_ref,
    own_ref,
    other_ref,
    masked_q,
    masked_grad,
    centre,
    q_total,
    kv_total,
):
    place = pl.program_id(0)
    width = head_count * HEAD_DIM
    tiles = kv_ref.shape[0]

    @pl.when(place == 0)
    def _():
        kv_total[...] = jnp.zeros_like(kv_total)

    split_pairs(q_ref[...], masked_q, head_count)
    split_pairs(grad_ref[...], masked_grad, head_count)
    crossed = (grad_ref[...].astype(F32) * exact_ref[...]).T
    for head in range(head_count):
        rows = slice(head * HEAD_DIM, (head + 1) * HEAD_DIM)
        centre[head : head + 1, :] = jnp.sum(crossed[rows, :], 0, keepdims=True)
    q_total[...] = jnp.zeros_like(q_total)
    q_bits = bits_ref[tiles + place]

    def one_tile(tile, carry):
        @pl.when((bits_ref[tile] & q_bits) != 0)
        def _():
            hide = jnp.where(k_label_ref[tile] == q_label_ref[0], 0.0, NEG)
            for pair in range(head_count // 2):
                lanes = slice(pair * 128, pair * 128 + 128)
                v_lanes = slice(width + pair * 128, width + pair * 128 + 128)
                key_part = None
                value_part = None
                for head in (2 * pair, 2 * pair + 1):
                    scores = dot(kv_ref[tile, :, lanes], masked_q[head], 1, 1) + hide
                    weights = jnp.exp(scores - logsum_ref[0, head : head + 1, :])
                    weight_grad = dot(kv_ref[tile, :, v_lanes], masked_grad[head], 1, 1)
                    score_grad = (weights * (weight_grad - centre[head : head + 1, :])).astype(
                        BF16
                    )
                    value_now = dot(weights.astype(BF16), masked_grad[head])
                    key_now = dot(score_grad, masked_q[head])
                    value_part = value_now if value_part is None else value_part + value_now
                    key_part = key_now if key_part is None else key_part + key_now
                    rows = slice(head * HEAD_DIM, (head + 1) * HEAD_DIM)
                    q_total[rows, :] += dot(turned_ref[tile, rows, :], score_grad)
                kv_total[tile, :, lanes] += key_part
                kv_total[tile, :, v_lanes] += value_part

        return carry

    lax.fori_loop(0, tiles, one_tile, 0)
    q_grad_ref[...] = q_total[...].T.astype(BF16) * jnp.asarray(HEAD_DIM**-0.5, BF16)

    @pl.when(place == pl.num_programs(0) - 1)
    def _():
        own_ref[...] = kv_total[: tiles // 2]
        other_ref[...] = kv_total[tiles // 2 :].astype(BF16)


def feed_kernel(
    steps,
    unit_ref,
    share_ref,
    recv_ref,
    vec_ref,
    up_own_ref,
    up_other_ref,
    bias_ref,
    down_own_ref,
    down_other_ref,
    new_unit_ref,
    inverse_ref,
    low_ref,
    act_ref,
    slope_ref,
    part_ref,
    low_rows,
    total,
):
    step = pl.program_id(0)

    @pl.when(step == 0)
    def _():
        stream = unit_ref[...] * vec_ref[0, 6:7, :] + vec_ref[0, 7:8, :]
        attention = share_ref[...].astype(F32) + recv_ref[...].astype(F32)
        unit, inverse = norm_parts(stream + attention + vec_ref[0, 0:1, :])
        new_unit_ref[...] = unit
        inverse_ref[...] = inverse
        low = (unit * vec_ref[0, 1:2, :] + vec_ref[0, 2:3, :]).astype(BF16)
        low_ref[...] = low
        low_rows[...] = low
        total[...] = jnp.zeros_like(total)

    def half(up_ref, down_ref):
        act, slope = gelu_parts(dot(low_rows[...], up_ref[0]) + bias_ref[0])
        low_act = act.astype(BF16)
        act_ref[...] = low_act
        slope_ref[...] = slope.astype(BF16)
        total[...] += dot(low_act, down_ref[0])

    @pl.when(step < steps // 2)
    def _():
        half(up_own_ref, down_own_ref)

    @pl.when(step >= steps // 2)
    def _():
        half(up_other_ref, down_other_ref)

    @pl.when(step == steps - 1)
    def _():
        part_ref[...] = total[...].astype(BF16)


def project_kernel(
    unit_ref,
    share_ref,
    recv_ref,
    vec_ref,
    q_weight_ref,
    kv_weight_ref,
    q_bias_ref,
    kv_bias_ref,
    new_unit_ref,
    inverse_ref,
    low_ref,
    q_ref,
    kv_ref,
):
    middle = unit_ref[...] * vec_ref[0, 1:2, :] + vec_ref[0, 2:3, :]
    feed = share_ref[...].astype(F32) + recv_ref[...].astype(F32)
    unit, inverse = norm_parts(middle + feed + vec_ref[0, 3:4, :])
    new_unit_ref[...] = unit
    inverse_ref[...] = inverse
    low = (unit * vec_ref[0, 4:5, :] + vec_ref[0, 5:6, :]).astype(BF16)
    low_ref[...] = low
    kv_ref[0] = (dot(low, kv_weight_ref[0]) + kv_bias_ref[0]).astype(BF16)
    q_ref[...] = ((dot(low, q_weight_ref[0]) + q_bias_ref[0]) * HEAD_DIM**-0.5).astype(BF16)


def feed_back_kernel(
    steps,
    top_layer,
    up_ref,
    unit_ref,
    inverse_ref,
    share_ref,
    recv_ref,
    vec_ref,
    slope_ref,
    up_own_ref,
    up_other_ref,
    down_own_ref,
    down_other_ref,
    encoded_ref,
    total_ref,
    low_ref,
    grad_ref,
    bias_ref,
    sums_ref,
    part_ref,
    low_rows,
    total,
):
    step = pl.program_id(0)

    @pl.when(step == 0)
    def _():
        added = share_ref[...].astype(F32) + recv_ref[...].astype(F32)
        if top_layer:
            middle = unit_ref[...] * vec_ref[0, 1:2, :] + vec_ref[0, 2:3, :]
            unit, inverse = norm_parts(middle + added + vec_ref[0, 3:4, :])
            encoded_ref[...] = (unit * vec_ref[0, 4:5, :] + vec_ref[0, 5:6, :]).astype(BF16)
            upstream = up_ref[...].astype(F32)
        else:
            unit = unit_ref[...]
            inverse = inverse_ref[...]
            upstream = up_ref[...] + added
        second = norm_back(upstream, unit, inverse, vec_ref[0, 4:5, :])
        sums_ref[...] = jnp.zeros_like(sums_ref)
        sums_ref[0:1, :] = jnp.sum(upstream * unit, 0, keepdims=True)
        sums_ref[1:2, :] = jnp.sum(upstream, 0, keepdims=True)
        sums_ref[2:3, :] = jnp.sum(second, 0, keepdims=True)
        total_ref[...] = second
        low = second.astype(BF16)
        low_ref[...] = low
        low_rows[...] = low
        total[...] = jnp.zeros_like(total)

    def half(up_weight_ref, down_ref):
        grad = (dot(low_rows[...], down_ref[0], 1, 1) * slope_ref[...].astype(F32)).astype(BF16)
        grad_ref[...] = grad
        bias_ref[...] = jnp.sum(grad.astype(F32), 0, keepdims=True)
        total[...] += dot(grad, up_weight_ref[0], 1, 1)

    @pl.when(step < steps // 2)
    def _():
        half(up_own_ref, down_own_ref)

    @pl.when(step >= steps // 2)
    def _():
        half(up_other_ref, down_other_ref)

    @pl.when(step == steps - 1)
    def _():
        part_ref[...] = total[...].astype(BF16)


def context_back_kernel(
    second_ref,
    share_ref,
    recv_ref,
    unit_ref,
    inverse_ref,
    vec_ref,
    out_weight_ref,
    total_ref,
    low_ref,
    grad_ref,
    sums_ref,
):
    added = share_ref[...].astype(F32) + recv_ref[...].astype(F32)
    upstream = second_ref[...] + added
    unit = unit_ref[...]
    first = norm_back(upstream, unit, inverse_ref[...], vec_ref[0, 1:2, :])
    sums_ref[...] = jnp.zeros_like(sums_ref)
    sums_ref[0:1, :] = jnp.sum(upstream * unit, 0, keepdims=True)
    sums_ref[1:2, :] = jnp.sum(upstream, 0, keepdims=True)
    sums_ref[2:3, :] = jnp.sum(first, 0, keepdims=True)
    total_ref[...] = first
    low = first.astype(BF16)
    low_ref[...] = low
    grad_ref[...] = dot(low, out_weight_ref[0], 1, 1).astype(BF16)


def joint_back_kernel(
    q_grad_ref, own_ref, recv_ref, q_weight_ref, kv_weight_ref, joint_ref, bias_ref, part_ref
):
    width = q_grad_ref.shape[1]
    q_grad = q_grad_ref[...]
    kv_grad = (own_ref[0] + recv_ref[0].astype(F32)).astype(BF16)
    joint_ref[:, :width] = q_grad
    joint_ref[:, width:] = kv_grad
    bias_ref[...] = jnp.zeros_like(bias_ref)
    bias_ref[0:1, :] = jnp.sum(q_grad.astype(F32), 0, keepdims=True)
    bias_ref[1:2, :] = jnp.sum(kv_grad[:, width:].astype(F32), 0, keepdims=True)
    part_ref[...] = (dot(q_grad, q_weight_ref[0], 1, 1) + dot(kv_grad, kv_weight_ref[0], 1, 1)).astype(
        BF16
    )


def wide_pairs(wide):
    steps = []
    reach = 1
    while reach < wide:
        steps.append([(index, index ^ reach) for index in range(wide)])
        reach *= 2
    return steps


def on_device(wide, *arguments):
    (
        tokens,
        buckets,
        lengths,
        type_table,
        query_weight,
        query_bias,
        key_weight,
        value_weight,
        value_bias,
        output_weight,
        output_bias,
        attention_gain,
        attention_shift,
        up_weight,
        up_bias,
        down_weight,
        down_bias,
        feed_gain,
        feed_shift,
        cotangent,
    ) = arguments
    share, model = tokens.shape
    lane = 2 * share
    chunks = lane // CHUNK
    local = query_weight.shape[2]
    width = 2 * local
    head_count = width // HEAD_DIM
    units = up_weight.shape[2]
    place = lax.axis_index("narrow")
    chip, core = place // 2, place % 2
    first_chip, first_core = chip == 0, core == 0

    def by_core(own, other, axis):
        return jnp.where(
            first_core,
            jnp.concatenate([own, other], axis),
            jnp.concatenate([other, own], axis),
        )

    def by_chip(own, other):
        return jnp.where(
            first_chip, jnp.concatenate([own, other], 0), jnp.concatenate([other, own], 0)
        )

    def own_rows(rows):
        return jnp.where(first_chip, rows[:share], rows[share:])

    def other_rows(rows):
        return jnp.where(first_chip, rows[share:], rows[:share])

    lane_tokens = by_chip(tokens, over_chip(tokens))
    lane_buckets = by_chip(buckets, over_chip(buckets))
    lane_cotangent = by_chip(cotangent, over_chip(cotangent))

    qw = by_core(query_weight, over_core(query_weight), 2)
    kw = by_core(key_weight, over_core(key_weight), 2)
    vw = by_core(value_weight, over_core(value_weight), 2)
    ow = by_core(output_weight, over_core(output_weight), 1)
    kvw = jnp.concatenate([kw, vw], 2)
    up_other = over_core(up_weight)
    down_other = over_core(down_weight)
    small = jnp.concatenate([query_bias, value_bias, up_bias], 1)
    small_other = over_core(small)
    q_bias = by_core(query_bias, small_other[:, :local], 1).astype(F32)[:, None, :]
    v_bias = by_core(value_bias, small_other[:, local:width], 1).astype(F32)
    kv_bias = jnp.concatenate([jnp.zeros_like(v_bias), v_bias], 1)[:, None, :]
    unit_bias = jnp.concatenate([up_bias, small_other[:, width:]], 1).astype(F32)[:, None, :]
    ones = jnp.ones((1, model), F32)
    rows = [
        value.astype(F32)
        for value in (
            output_bias,
            attention_gain,
            attention_shift,
            down_bias,
            feed_gain,
            feed_shift,
        )
    ]
    rows.append(jnp.concatenate([ones, rows[4][: LAYERS - 1]], 0))
    rows.append(jnp.concatenate([0.0 * ones, rows[5][: LAYERS - 1]], 0))
    vec = jnp.stack(rows, 1)

    ends = jnp.cumsum(lengths[0], dtype=jnp.int32)
    offsets = lax.iota(jnp.int32, share)
    spots = jnp.concatenate(
        [
            offsets + (block * 2 + which) * share
            for which in (core, 1 - core)
            for block in range(2)
        ]
    )
    labels = jnp.sum((spots[:, None] >= ends[None, :]).astype(jnp.int32), 1, dtype=jnp.int32)
    tiles = 2 * chunks
    tile_labels = labels.reshape(tiles, CHUNK)
    present = jnp.any(
        tile_labels[:, :, None] == lax.iota(jnp.int32, lengths.shape[1])[None, None, :], axis=1
    )
    bits = jnp.sum(
        jnp.where(present, jnp.left_shift(1, lax.iota(jnp.int32, lengths.shape[1]))[None, :], 0),
        axis=1,
        dtype=jnp.int32,
    )
    bits = jnp.concatenate([bits, bits[:chunks]])
    k_labels = tile_labels[:, :, None]
    q_labels = tile_labels[:chunks, None, :]

    block = (CHUNK, model)
    smem = pl.BlockSpec(memory_space=pltpu.SMEM)

    def layer_spec(layer, shape):
        return pl.BlockSpec((1,) + shape, lambda *ids: (layer,) + (0,) * len(shape))

    def rows_at(index, columns):
        return pl.BlockSpec((CHUNK, columns), lambda *ids: (index, 0))

    steps = 2 * units // CHUNK
    half_steps = steps // 2

    def unit_specs(layer):
        def early(step):
            return jnp.minimum(step, half_steps - 1)

        def late(step):
            return jnp.maximum(step - half_steps, 0)

        up_specs = [
            pl.BlockSpec((1, model, CHUNK), lambda step: (layer, 0, early(step))),
            pl.BlockSpec((1, model, CHUNK), lambda step: (layer, 0, late(step))),
        ]
        down_specs = [
            pl.BlockSpec((1, CHUNK, model), lambda step: (layer, early(step), 0)),
            pl.BlockSpec((1, CHUNK, model), lambda step: (layer, late(step), 0)),
        ]
        return up_specs, down_specs

    selector = (lane_buckets[:, None] == lax.iota(jnp.int32, type_table.shape[0])[None, :]).astype(
        BF16
    )
    stream = lane_tokens.astype(F32) + dot(selector, type_table)
    low_first = stream.astype(BF16)
    state = [stream[CHUNK * i : CHUNK * (i + 1)] for i in range(chunks)]
    kept = []
    matmul = 2 * CHUNK * model
    for layer in range(LAYERS):
        keep = {}
        if layer == 0:
            low_in = low_first
            kv = (dot(low_first, kvw[0]) + kv_bias[0]).astype(BF16).reshape(chunks, CHUNK, 2 * width)
            queries = ((dot(low_first, qw[0]) + q_bias[0]) * HEAD_DIM**-0.5).astype(BF16)
        else:
            low_in = queries = kv = None
            units_now = []
            inverses = []
            for i in range(chunks):
                outs = call(
                    project_kernel,
                    (1,),
                    [
                        (state[i], whole(block)),
                        (feed_share[i], whole(block)),
                        (feed_recv[i], whole(block)),
                        (vec, layer_spec(layer - 1, (8, model))),
                        (qw, layer_spec(layer, (model, width))),
                        (kvw, layer_spec(layer, (model, 2 * width))),
                        (q_bias, layer_spec(layer, (1, width))),
                        (kv_bias, layer_spec(layer, (1, 2 * width))),
                    ],
                    [
                        (block, F32, whole(block), None),
                        ((CHUNK, 1), F32, whole((CHUNK, 1)), None),
                        ((lane, model), BF16, rows_at(i, model), low_in),
                        ((lane, width), BF16, rows_at(i, width), queries),
                        (
                            (chunks, CHUNK, 2 * width),
                            BF16,
                            pl.BlockSpec((1, CHUNK, 2 * width), lambda *ids, i=i: (i, 0, 0)),
                            kv,
                        ),
                    ],
                    flops=matmul * 3 * width,
                    moved=6 * MIB,
                )
                units_now.append(outs[0])
                inverses.append(outs[1])
                low_in, queries, kv = outs[2:]
            state = units_now
            kept[layer - 1]["second_unit"] = units_now
            kept[layer - 1]["second_inverse"] = inverses
        kv_other = over_core(kv)
        tile_shape = (1, CHUNK, 2 * width)
        kv_all, turned = call(
            gather_kernel,
            (tiles,),
            [
                (kv, pl.BlockSpec(tile_shape, lambda t: (jnp.minimum(t, chunks - 1), 0, 0))),
                (kv_other, pl.BlockSpec(tile_shape, lambda t: (jnp.maximum(t - chunks, 0), 0, 0))),
            ],
            [
                ((tiles, CHUNK, 2 * width), BF16, pl.BlockSpec(tile_shape, lambda t: (t, 0, 0)), None),
                (
                    (tiles, 2 * width, CHUNK),
                    BF16,
                    pl.BlockSpec((1, 2 * width, CHUNK), lambda t: (t, 0, 0)),
                    None,
                ),
            ],
            moved=7 * MIB,
        )
        context = exact = logsum = None
        shares = []
        for i in range(chunks):
            context, exact, logsum, part = call(
                functools.partial(attend_kernel, head_count, i),
                (1,),
                [
                    (bits, smem),
                    (queries, rows_at(i, width)),
                    (kv_all, whole(kv_all.shape)),
                    (turned, whole(turned.shape)),
                    (q_labels[i], whole((1, CHUNK))),
                    (k_labels, whole(k_labels.shape)),
                    (ow, layer_spec(layer, (width, model))),
                ],
                [
                    ((lane, width), BF16, rows_at(i, width), context),
                    ((lane, width), F32, rows_at(i, width), exact),
                    (
                        (chunks, 8, CHUNK),
                        F32,
                        pl.BlockSpec((1, 8, CHUNK), lambda *ids, i=i: (i, 0, 0)),
                        logsum,
                    ),
                    (block, BF16, whole(block), None),
                ],
                scratch=[
                    pltpu.VMEM((head_count, CHUNK, 128), BF16),
                    pltpu.VMEM((width, CHUNK), F32),
                    pltpu.VMEM((8, CHUNK), F32),
                    pltpu.VMEM((8, CHUNK), F32),
                ],
                flops=4 * CHUNK * tiles * CHUNK * width * 4,
                moved=5 * MIB,
            )
            shares.append(part)
        received = [over_chip(part) for part in shares]
        up_specs, down_specs = unit_specs(layer)
        low_middle = act = slope = None
        first_unit, first_inverse, feed_share = [], [], []
        for i in range(chunks):
            outs = call(
                functools.partial(feed_kernel, steps),
                (steps,),
                [
                    (state[i], whole(block)),
                    (shares[i], whole(block)),
                    (received[i], whole(block)),
                    (vec, layer_spec(layer, (8, model))),
                    (up_weight, up_specs[0]),
                    (up_other, up_specs[1]),
                    (
                        unit_bias,
                        pl.BlockSpec((1, 1, CHUNK), lambda step, layer=layer: (layer, 0, step)),
                    ),
                    (down_weight, down_specs[0]),
                    (down_other, down_specs[1]),
                ],
                [
                    (block, F32, whole(block), None),
                    ((CHUNK, 1), F32, whole((CHUNK, 1)), None),
                    ((lane, model), BF16, rows_at(i, model), low_middle),
                    (
                        (lane, 2 * units),
                        BF16,
                        pl.BlockSpec((CHUNK, CHUNK), lambda step, i=i: (i, step)),
                        act,
                    ),
                    (
                        (lane, 2 * units),
                        BF16,
                        pl.BlockSpec((CHUNK, CHUNK), lambda step, i=i: (i, step)),
                        slope,
                    ),
                    (block, BF16, whole(block), None),
                ],
                scratch=[pltpu.VMEM(block, BF16), pltpu.VMEM(block, F32)],
                flops=matmul * 4 * units,
                moved=8 * MIB,
            )
            first_unit.append(outs[0])
            first_inverse.append(outs[1])
            low_middle, act, slope = outs[2:5]
            feed_share.append(outs[5])
        feed_recv = [over_chip(part) for part in feed_share]
        state = first_unit
        keep.update(
            low_in=low_in,
            queries=queries,
            kv_all=kv_all,
            turned=turned,
            context=context,
            exact=exact,
            logsum=logsum,
            first_unit=first_unit,
            first_inverse=first_inverse,
            low_middle=low_middle,
            act=act,
            slope=slope,
        )
        kept.append(keep)

    def over_wide(value):
        return lax.psum(value, "wide")

    def pair_total(own, other):
        return over_wide((own + over_core(other.astype(BF16)).astype(F32)).astype(BF16))

    def halves(full, axis):
        left, right = jnp.split(full, 2, axis)
        return jnp.where(first_core, left, right), jnp.where(first_core, right, left)

    weight_grads = [None] * LAYERS
    shared = [None] * LAYERS
    split_vectors = [None] * LAYERS
    encoded = None
    for layer in reversed(range(LAYERS)):
        keep = kept[layer]
        top_layer = layer == LAYERS - 1
        up_specs, down_specs = unit_specs(layer)
        low_second = up_grad = None
        second, unit_sums, second_sums, parts = [], [], [], []
        for i in range(chunks):
            if top_layer:
                upstream = (lane_cotangent, rows_at(i, model))
                unit = keep["first_unit"][i]
                inverse = keep["first_inverse"][i]
                added = (feed_share[i], feed_recv[i])
            else:
                upstream = (first_total[i], whole(block))
                unit = keep["second_unit"][i]
                inverse = keep["second_inverse"][i]
                added = (joint_share[i], joint_recv[i])
            outs = call(
                functools.partial(feed_back_kernel, steps, top_layer),
                (steps,),
                [
                    upstream,
                    (unit, whole(block)),
                    (inverse, whole((CHUNK, 1))),
                    (added[0], whole(block)),
                    (added[1], whole(block)),
                    (vec, layer_spec(layer, (8, model))),
                    (
                        keep["slope"],
                        pl.BlockSpec((CHUNK, CHUNK), lambda step, i=i: (i, step)),
                    ),
                    (up_weight, up_specs[0]),
                    (up_other, up_specs[1]),
                    (down_weight, down_specs[0]),
                    (down_other, down_specs[1]),
                ],
                [
                    ((lane, model), BF16, rows_at(i, model), encoded)
                    if top_layer
                    else ((8, 128), BF16, whole((8, 128)), None),
                    (block, F32, whole(block), None),
                    ((lane, model), BF16, rows_at(i, model), low_second),
                    (
                        (lane, 2 * units),
                        BF16,
                        pl.BlockSpec((CHUNK, CHUNK), lambda step, i=i: (i, step)),
                        up_grad,
                    ),
                    ((1, 2 * units), F32, pl.BlockSpec((1, CHUNK), lambda step: (0, step)), None),
                    ((8, model), F32, whole((8, model)), None),
                    (block, BF16, whole(block), None),
                ],
                scratch=[pltpu.VMEM(block, BF16), pltpu.VMEM(block, F32)],
                flops=matmul * 4 * units,
                moved=8 * MIB,
            )
            if top_layer:
                encoded = outs[0]
            second.append(outs[1])
            low_second, up_grad = outs[2:4]
            unit_sums.append(outs[4])
            second_sums.append(outs[5])
            parts.append(outs[6])
        received = [over_chip(part) for part in parts]
        down_grad = pair_total(
            dot(keep["act"][:, :units], low_second, 0, 0),
            dot(keep["act"][:, units:], low_second, 0, 0),
        )
        up_weight_grad = pair_total(
            dot(keep["low_middle"], up_grad[:, :units], 0, 0),
            dot(keep["low_middle"], up_grad[:, units:], 0, 0),
        )
        low_total = context_grad = None
        first_total, first_sums = [], []
        for i in range(chunks):
            outs = call(
                context_back_kernel,
                (1,),
                [
                    (second[i], whole(block)),
                    (parts[i], whole(block)),
                    (received[i], whole(block)),
                    (keep["first_unit"][i], whole(block)),
                    (keep["first_inverse"][i], whole((CHUNK, 1))),
                    (vec, layer_spec(layer, (8, model))),
                    (ow, layer_spec(layer, (width, model))),
                ],
                [
                    (block, F32, whole(block), None),
                    ((lane, model), BF16, rows_at(i, model), low_total),
                    ((lane, width), BF16, rows_at(i, width), context_grad),
                    ((8, model), F32, whole((8, model)), None),
                ],
                flops=matmul * width,
                moved=5 * MIB,
            )
            first_total.append(outs[0])
            low_total, context_grad = outs[1:3]
            first_sums.append(outs[3])
        own, other = halves(dot(keep["context"], low_total, 0, 0), 0)
        out_grad = pair_total(own, other)
        tile_rows = pl.BlockSpec((CHUNK, width), lambda t: (t, 0))
        turned_keys = (tiles, width, CHUNK)
        half_shape = (chunks, CHUNK, 2 * width)
        q_grad, kv_grad, kv_grad_other = call(
            functools.partial(attend_back_kernel, head_count),
            (chunks,),
            [
                (bits, smem),
                (keep["queries"], tile_rows),
                (keep["kv_all"], whole(keep["kv_all"].shape)),
                (keep["turned"], whole(turned_keys)),
                (q_labels, pl.BlockSpec((1, 1, CHUNK), lambda t: (t, 0, 0))),
                (k_labels, whole(k_labels.shape)),
                (context_grad, tile_rows),
                (keep["exact"], tile_rows),
                (keep["logsum"], pl.BlockSpec((1, 8, CHUNK), lambda t: (t, 0, 0))),
            ],
            [
                ((lane, width), BF16, tile_rows, None),
                (half_shape, F32, whole(half_shape), None),
                (half_shape, BF16, whole(half_shape), None),
            ],
            scratch=[
                pltpu.VMEM((head_count, CHUNK, 128), BF16),
                pltpu.VMEM((head_count, CHUNK, 128), BF16),
                pltpu.VMEM((8, CHUNK), F32),
                pltpu.VMEM((width, CHUNK), F32),
                pltpu.VMEM((tiles, CHUNK, 2 * width), F32),
            ],
            flops=10 * lane * tiles * CHUNK * width * 4,
            moved=12 * MIB,
        )
        kv_recv = over_core(kv_grad_other)
        joint_grad = None
        joint_share, bias_sums = [], []
        for i in range(chunks):
            tile_spec = pl.BlockSpec((1, CHUNK, 2 * width), lambda *ids, i=i: (i, 0, 0))
            joint_grad, sums, part = call(
                joint_back_kernel,
                (1,),
                [
                    (q_grad, rows_at(i, width)),
                    (kv_grad, tile_spec),
                    (kv_recv, tile_spec),
                    (qw, layer_spec(layer, (model, width))),
                    (kvw, layer_spec(layer, (model, 2 * width))),
                ],
                [
                    ((lane, 3 * width), BF16, rows_at(i, 3 * width), joint_grad),
                    ((8, width), F32, whole((8, width)), None),
                    (block, BF16, whole(block), None),
                ],
                flops=matmul * 3 * width,
                moved=5 * MIB,
            )
            joint_share.append(part)
            bias_sums.append(sums)
        if layer > 0:
            joint_recv = [over_chip(part) for part in joint_share]
        joint_weight_grad = dot(keep["low_in"], joint_grad, 0, 0)
        pieces = [
            halves(joint_weight_grad[:, width * k : width * (k + 1)], 1) for k in range(3)
        ]
        own = jnp.concatenate([piece[0] for piece in pieces], 1)
        other = jnp.concatenate([piece[1] for piece in pieces], 1)
        joint = pair_total(own, other)
        weight_grads[layer] = (
            joint[:, :local],
            joint[:, local : 2 * local],
            joint[:, 2 * local :],
            out_grad,
            up_weight_grad,
            down_grad,
        )
        second_sum, first_sum = sum(second_sums), sum(first_sums)
        shared[layer] = jnp.concatenate([second_sum[:3], first_sum[:3]], 0)
        unit_sum, bias_sum = sum(unit_sums), sum(bias_sums)
        q_own, q_other = halves(bias_sum[0], 0)
        v_own, v_other = halves(bias_sum[1], 0)
        split_vectors[layer] = (
            jnp.concatenate([q_own, v_own, unit_sum[0, :units]]),
            jnp.concatenate([q_other, v_other, unit_sum[0, units:]]),
        )

    joint_rows = jnp.concatenate(joint_share, 0)
    joint_mine = own_rows(joint_rows).astype(F32)
    joint_theirs = over_chip(other_rows(joint_rows)).astype(F32)
    tokens_grad = own_rows(jnp.concatenate(first_total, 0)) + (joint_mine + joint_theirs)
    own_selector = (buckets[:, None] == lax.iota(jnp.int32, type_table.shape[0])[None, :]).astype(
        BF16
    )
    high = tokens_grad.astype(BF16)
    rest = (tokens_grad - high.astype(F32)).astype(BF16)
    table = dot(own_selector, high, 0, 0) + dot(own_selector, rest, 0, 0)

    def wide_sum(value):
        if wide != 8:
            return lax.psum(value, "wide")
        for pairs in wide_pairs(wide):
            value = value + lax.ppermute(value, "wide", pairs)
        return value

    def summed_in_bf16(value, pairs, axis):
        low = value.astype(BF16)
        return low.astype(F32) + lax.ppermute(low, axis, pairs).astype(F32)

    table_own, table_other = halves(table, 0)
    table_half = table_own + over_core(table_other)
    table_half = summed_in_bf16(table_half, CHIP_SWAP, "narrow")
    if wide == 8:
        for pairs in wide_pairs(wide):
            table_half = summed_in_bf16(table_half, pairs, "wide")
    else:
        table_half = lax.psum(table_half, "wide")
    table_grad = by_core(table_half, over_core(table_half), 0)

    common = jnp.concatenate(shared, 0)
    mine = jnp.stack([value[0] for value in split_vectors])
    theirs = jnp.stack([value[1] for value in split_vectors])
    vectors = jnp.concatenate([common.reshape(-1), mine.reshape(-1)])
    sent = jnp.concatenate([common.reshape(-1), theirs.reshape(-1)])
    vectors = wide_sum((vectors + over_core(sent)).reshape(-1, 128)).reshape(-1)
    common = vectors[: common.size].reshape(LAYERS, 6, model)
    mine = vectors[common.size :].reshape(LAYERS, -1)

    def stacked(member):
        return jnp.stack([weight_grads[layer][member] for layer in range(LAYERS)]).astype(F32)

    return (
        own_rows(encoded),
        tokens_grad,
        table_grad,
        stacked(0),
        mine[:, :local],
        stacked(1),
        stacked(2),
        mine[:, local : 2 * local],
        stacked(3),
        common[:, 5],
        common[:, 3],
        common[:, 4],
        stacked(4),
        mine[:, 2 * local :],
        stacked(5),
        common[:, 2],
        common[:, 0],
        common[:, 1],
    )


def solution(mesh):
    rows = P(("wide", "narrow"), None)
    third = P(None, None, "narrow")
    second = P(None, "narrow")
    middle = P(None, "narrow", None)
    in_specs = (
        rows,
        P(("wide", "narrow")),
        P("wide", None),
        P(),
        third,
        second,
        third,
        third,
        second,
        middle,
        P(),
        P(),
        P(),
        third,
        second,
        middle,
        P(),
        P(),
        P(),
        rows,
    )
    out_specs = (
        rows,
        rows,
        P(),
        third,
        second,
        third,
        third,
        second,
        middle,
        P(),
        P(),
        P(),
        third,
        second,
        middle,
        P(),
        P(),
        P(),
    )
    return jax.shard_map(
        functools.partial(on_device, mesh.shape["wide"]),
        mesh=mesh,
        in_specs=in_specs,
        out_specs=out_specs,
        check_vma=False,
    )
```

```python
import functools

import jax
import jax.numpy as jnp
from jax import lax
from jax.experimental import pallas as pl
from jax.experimental.pallas import tpu as pltpu
from jax.sharding import PartitionSpec as P

HEAD_DIM = 64
LAYERS = 2
CHUNK = 256
EPS = 1e-12
ROOT_HALF = 0.7071067811865476
DENSITY = 0.3989422804014327
NEG = -1e30
F32 = jnp.float32
BF16 = jnp.bfloat16
MIB = 1 << 20
CORE_SWAP = [(0, 1), (1, 0), (2, 3), (3, 2)]
CHIP_SWAP = [(0, 2), (2, 0), (1, 3), (3, 1)]


def over_core(value):
    return lax.ppermute(value, "narrow", CORE_SWAP)


def over_chip(value):
    return lax.ppermute(value, "narrow", CHIP_SWAP)


def dot(left, right, left_axis=1, right_axis=0):
    return lax.dot_general(
        left, right, (((left_axis,), (right_axis,)), ((), ())), preferred_element_type=F32
    )


def norm_parts(summed):
    row_mean = jnp.mean(summed, -1, keepdims=True)
    centred = summed - row_mean
    spread = jnp.mean(centred * centred, -1, keepdims=True)
    inverse = lax.rsqrt(spread + EPS)
    return centred * inverse, inverse


def norm_back(upstream, unit_rows, inverse, gain_row):
    scaled = upstream * gain_row
    return inverse * (
        scaled
        - jnp.mean(scaled, -1, keepdims=True)
        - unit_rows * jnp.mean(scaled * unit_rows, -1, keepdims=True)
    )


def gelu_parts(preact):
    size = jnp.abs(preact) * ROOT_HALF
    bell = jnp.exp(-(size * size))
    step = 1.0 / (1.0 + 0.3275911 * size)
    series = step * (
        0.254829592
        + step * (-0.284496736 + step * (1.421413741 + step * (-1.453152027 + step * 1.061405429)))
    )
    tail = 0.5 * series * bell
    cdf = jnp.where(preact >= 0.0, 1.0 - tail, tail)
    return preact * cdf, cdf + preact * DENSITY * bell


ON_CHIP = pl.BlockSpec(memory_space=pltpu.VMEM)


def whole(shape):
    zeros = (0,) * len(shape)
    return pl.BlockSpec(shape, lambda *ids: zeros)


def call(kernel, grid, inputs, outputs, scratch=(), cost=1, limit=16, after=()):
    arrays = [array for array, spec in inputs]
    specs = [spec for array, spec in inputs]
    aliases = {}
    for place, (shape, dtype, spec, buffer) in enumerate(outputs):
        if buffer is not None:
            aliases[len(arrays)] = place
            arrays.append(buffer)
            specs.append(pl.BlockSpec(memory_space=pl.ANY))
    for array in after:
        arrays.append(array)
        specs.append(pl.BlockSpec(memory_space=pl.ANY))
    given, extra = len(inputs), len(aliases) + len(after)

    def body(*refs):
        kernel(*refs[:given], *refs[given + extra :])

    return pl.pallas_call(
        body,
        **({} if grid is None else {"grid": grid}),
        in_specs=specs,
        out_specs=[spec for shape, dtype, spec, buffer in outputs],
        out_shape=[
            jax.ShapeDtypeStruct(shape, dtype) for shape, dtype, spec, buffer in outputs
        ],
        scratch_shapes=list(scratch),
        input_output_aliases=aliases,
        compiler_params=pltpu.CompilerParams(vmem_limit_bytes=limit * MIB),
        cost_estimate=pl.CostEstimate(flops=cost * 4000000000, bytes_accessed=1, transcendentals=0),
    )(*arrays)


def gather_kernel(*refs):
    sources, (rows_ref, turned_ref) = refs[:-2], refs[-2:]
    for place, source in enumerate(sources):
        tile = source[...]
        rows_ref[place] = tile
        turned_ref[place] = tile.astype(F32).T.astype(BF16)


def split_pairs(pair_block, target, head_count):
    lanes = lax.broadcasted_iota(jnp.int32, (CHUNK, 2 * HEAD_DIM), 1)
    low_half = lanes < HEAD_DIM
    for head in range(head_count):
        pair = pair_block[:, (head // 2) * 128 : (head // 2) * 128 + 128]
        keep = low_half if head % 2 == 0 else jnp.logical_not(low_half)
        target[head] = jnp.where(keep, pair, jnp.zeros_like(pair))


def attend_kernel(
    head_count,
    layer,
    place,
    bits_ref,
    q_ref,
    kv_ref,
    turned_ref,
    q_label_ref,
    k_label_ref,
    out_weight_ref,
    context_ref,
    exact_ref,
    logsum_ref,
    share_ref,
    masked_q,
    total,
    top,
    mass,
    score_tiles,
):
    width = head_count * HEAD_DIM
    split_pairs(q_ref[...], masked_q, head_count)
    top[...] = jnp.full_like(top, NEG)
    mass[...] = jnp.zeros_like(mass)
    total[...] = jnp.zeros_like(total)
    tiles = kv_ref.shape[0]
    q_bits = bits_ref[tiles + place]

    def score_tile(tile, carry):
        @pl.when((bits_ref[tile] & q_bits) != 0)
        def _():
            hide = jnp.where(k_label_ref[tile] == q_label_ref[place], 0.0, NEG)
            for head in range(head_count):
                pair = (head // 2) * 128
                scores = dot(kv_ref[tile, :, pair : pair + 128], masked_q[head], 1, 1) + hide
                score_tiles[head, tile] = scores
                highest = jnp.max(scores.reshape(-1, 8, CHUNK), 0)
                top[head] = jnp.maximum(top[head], highest)

        return carry

    lax.fori_loop(0, tiles, score_tile, 0)
    for head in range(head_count):
        top[head] = jnp.broadcast_to(jnp.max(top[head], 0, keepdims=True), (8, CHUNK))

    def weigh_tile(tile, carry):
        @pl.when((bits_ref[tile] & q_bits) != 0)
        def _():
            for head in range(head_count):
                weights = jnp.exp(score_tiles[head, tile] - top[head, 0:1, :])
                mass[head] += jnp.sum(weights.reshape(-1, 8, CHUNK), 0)
                rows = slice(head * HEAD_DIM, (head + 1) * HEAD_DIM)
                total[rows, :] += dot(
                    turned_ref[tile, width + head * HEAD_DIM : width + (head + 1) * HEAD_DIM, :],
                    weights.astype(BF16),
                )

        return carry

    lax.fori_loop(0, tiles, weigh_tile, 0)
    logsum_ref[...] = jnp.zeros_like(logsum_ref)
    for head in range(head_count):
        rows = slice(head * HEAD_DIM, (head + 1) * HEAD_DIM)
        amount = jnp.sum(mass[head], 0, keepdims=True)
        total[rows, :] = total[rows, :] / amount
        logsum_ref[head : head + 1, :] = top[head, 0:1, :] + jnp.log(amount)
    exact = total[...].T
    exact_ref[...] = exact
    context = exact.astype(BF16)
    context_ref[...] = context
    share_ref[...] = dot(context, out_weight_ref[layer]).astype(BF16)


def attend_back_kernel(pair, head_count, chunks, *refs):
    bits_ref, kv_ref, turned_ref, q_label_ref, k_label_ref = refs[:5]
    q_refs, grad_refs, exact_refs, logsum_refs = (
        refs[5 + chunks * k : 5 + chunks * (k + 1)] for k in range(4)
    )
    q_grad_ref, own_ref, other_ref, masked_q, masked_grad, centre, q_total, kv_total = refs[
        5 + 4 * chunks :
    ]
    tiles = kv_ref.shape[0]
    lanes = slice(pair * 128, pair * 128 + 128)
    v_lanes = slice(head_count * HEAD_DIM + pair * 128, head_count * HEAD_DIM + pair * 128 + 128)
    kv_total[...] = jnp.zeros_like(kv_total)
    for place in range(chunks):
        split_pairs(q_refs[place][:, lanes], masked_q, 2)
        split_pairs(grad_refs[place][:, lanes], masked_grad, 2)
        crossed = (grad_refs[place][:, lanes].astype(F32) * exact_refs[place][:, lanes]).T
        for head in range(2):
            rows = slice(head * HEAD_DIM, (head + 1) * HEAD_DIM)
            centre[head : head + 1, :] = jnp.sum(crossed[rows, :], 0, keepdims=True)
        q_total[...] = jnp.zeros_like(q_total)
        q_bits = bits_ref[tiles + place]
        logsum_ref = logsum_refs[place]

        def one_tile(tile, carry):
            @pl.when((bits_ref[tile] & q_bits) != 0)
            def _():
                hide = jnp.where(k_label_ref[tile] == q_label_ref[place], 0.0, NEG)
                key_part = None
                value_part = None
                for head in range(2):
                    number = 2 * pair + head
                    scores = dot(kv_ref[tile, :, lanes], masked_q[head], 1, 1) + hide
                    weights = jnp.exp(scores - logsum_ref[number : number + 1, :])
                    weight_grad = dot(kv_ref[tile, :, v_lanes], masked_grad[head], 1, 1)
                    score_grad = (weights * (weight_grad - centre[head : head + 1, :])).astype(BF16)
                    value_now = dot(weights.astype(BF16), masked_grad[head])
                    key_now = dot(score_grad, masked_q[head])
                    value_part = value_now if value_part is None else value_part + value_now
                    key_part = key_now if key_part is None else key_part + key_now
                    rows = slice(head * HEAD_DIM, (head + 1) * HEAD_DIM)
                    turned = slice(number * HEAD_DIM, (number + 1) * HEAD_DIM)
                    q_total[rows, :] += dot(turned_ref[tile, turned, :], score_grad)
                kv_total[tile, :, :128] += key_part
                kv_total[tile, :, 128:] += value_part

            return carry

        lax.fori_loop(0, tiles, one_tile, 0)
        q_grad_ref[place * CHUNK : (place + 1) * CHUNK, :] = q_total[...].T.astype(
            BF16
        ) * jnp.asarray(HEAD_DIM**-0.5, BF16)
    own_ref[...] = kv_total[: tiles // 2]
    other_ref[...] = kv_total[tiles // 2 :].astype(BF16)


def weight_grad_kernel(chunks, left_start, right_start, *refs):
    lefts, rights, recv_refs = refs[:chunks], refs[chunks : 2 * chunks], refs[2 * chunks : -1]
    out_ref = refs[-1]
    rows, columns = out_ref.shape
    step = CHUNK if rows % CHUNK == 0 else rows
    for start in range(0, rows, step):
        left_lanes = slice(left_start + start, left_start + start + step)
        right_lanes = slice(right_start, right_start + columns)
        total = None
        for left, right in zip(lefts, rights):
            part = dot(left[:, left_lanes], right[:, right_lanes], 0, 0)
            total = part if total is None else total + part
        for recv_ref in recv_refs:
            total = total + recv_ref[start : start + step, :].astype(F32)
        out_ref[start : start + step, :] = total.astype(out_ref.dtype)


def out_grad_kernel(chunks, core_ref, *refs):
    lefts, rights, (own_ref, other_ref, full) = refs[:chunks], refs[chunks:-3], refs[-3:]
    total = None
    for left, right in zip(lefts, rights):
        part = dot(left[...], right[...], 0, 0)
        total = part if total is None else total + part
    full[...] = total
    local = own_ref.shape[0]
    own_ref[...] = full[pl.ds(pl.multiple_of(core_ref[0] * local, local), local), :]
    other_ref[...] = full[pl.ds(pl.multiple_of((1 - core_ref[0]) * local, local), local), :].astype(
        BF16
    )


def feed_kernel(
    layer,
    place,
    unit_ref,
    share_ref,
    recv_ref,
    vec_ref,
    up_own_ref,
    up_other_ref,
    bias_ref,
    down_own_ref,
    down_other_ref,
    new_unit_ref,
    inverse_ref,
    low_ref,
    act_ref,
    slope_ref,
    part_ref,
):
    stream = unit_ref[...] * vec_ref[layer, 6:7, :] + vec_ref[layer, 7:8, :]
    attention = share_ref[...].astype(F32) + recv_ref[...].astype(F32)
    unit, inverse = norm_parts(stream + attention + vec_ref[layer, 0:1, :])
    new_unit_ref[...] = unit
    inverse_ref[...] = inverse
    low_ref[...] = (unit * vec_ref[layer, 1:2, :] + vec_ref[layer, 2:3, :]).astype(BF16)
    units = up_own_ref.shape[2]
    total = None
    for half, (up_ref, down_ref) in enumerate(
        ((up_own_ref, down_own_ref), (up_other_ref, down_other_ref))
    ):
        lanes = slice(half * units, (half + 1) * units)
        act, slope = gelu_parts(dot(low_ref[...], up_ref[layer]) + bias_ref[layer, :, lanes])
        low_act = act.astype(BF16)
        act_ref[:, lanes] = low_act
        slope_ref[:, lanes] = slope.astype(BF16)
        part = dot(low_act, down_ref[layer])
        total = part if total is None else total + part
    part_ref[...] = total.astype(BF16)


def project_kernel(
    layer,
    place,
    unit_ref,
    share_ref,
    recv_ref,
    vec_ref,
    q_weight_ref,
    kv_weight_ref,
    q_bias_ref,
    kv_bias_ref,
    new_unit_ref,
    inverse_ref,
    low_ref,
    q_ref,
    kv_ref,
):
    old = layer - 1
    middle = unit_ref[...] * vec_ref[old, 1:2, :] + vec_ref[old, 2:3, :]
    feed = share_ref[...].astype(F32) + recv_ref[...].astype(F32)
    unit, inverse = norm_parts(middle + feed + vec_ref[old, 3:4, :])
    new_unit_ref[...] = unit
    inverse_ref[...] = inverse
    low = (unit * vec_ref[old, 4:5, :] + vec_ref[old, 5:6, :]).astype(BF16)
    low_ref[...] = low
    kv_ref[...] = (dot(low, kv_weight_ref[layer], 1, 1) + kv_bias_ref[layer]).astype(BF16)
    q_ref[...] = (
        (dot(low, q_weight_ref[layer], 1, 1) + q_bias_ref[layer]) * HEAD_DIM**-0.5
    ).astype(BF16)


def feed_back_kernel(
    layer,
    place,
    top_layer,
    up_ref,
    unit_ref,
    inverse_ref,
    share_ref,
    recv_ref,
    vec_ref,
    slope_ref,
    up_own_ref,
    up_other_ref,
    down_own_ref,
    down_other_ref,
    encoded_ref,
    total_ref,
    low_ref,
    grad_ref,
    bias_ref,
    sums_ref,
    part_ref,
):
    keep_span = slice(place * CHUNK, (place + 1) * CHUNK)
    added = share_ref[...].astype(F32) + recv_ref[...].astype(F32)
    if top_layer:
        middle = unit_ref[...] * vec_ref[layer, 1:2, :] + vec_ref[layer, 2:3, :]
        unit, inverse = norm_parts(middle + added + vec_ref[layer, 3:4, :])
        encoded_ref[...] = (unit * vec_ref[layer, 4:5, :] + vec_ref[layer, 5:6, :]).astype(BF16)
        upstream = up_ref[keep_span, :].astype(F32)
    else:
        unit = unit_ref[...]
        inverse = inverse_ref[...]
        upstream = up_ref[...] + added
        encoded_ref[...] = jnp.zeros_like(encoded_ref)
    second = norm_back(upstream, unit, inverse, vec_ref[layer, 4:5, :])
    sums_ref[...] = jnp.zeros_like(sums_ref)
    sums_ref[0:1, :] = jnp.sum(upstream * unit, 0, keepdims=True)
    sums_ref[1:2, :] = jnp.sum(upstream, 0, keepdims=True)
    sums_ref[2:3, :] = jnp.sum(second, 0, keepdims=True)
    total_ref[...] = second
    low_ref[...] = second.astype(BF16)
    units = up_own_ref.shape[2]
    total = None
    for half, (up_weight_ref, down_ref) in enumerate(
        ((up_own_ref, down_own_ref), (up_other_ref, down_other_ref))
    ):
        lanes = slice(half * units, (half + 1) * units)
        grad = (
            dot(low_ref[...], down_ref[layer], 1, 1) * slope_ref[:, lanes].astype(F32)
        ).astype(BF16)
        grad_ref[:, lanes] = grad
        bias_ref[:, lanes] = jnp.sum(grad.astype(F32), 0, keepdims=True)
        part = dot(grad, up_weight_ref[layer], 1, 1)
        total = part if total is None else total + part
    part_ref[...] = total.astype(BF16)


def context_back_kernel(
    layer,
    place,
    second_ref,
    share_ref,
    recv_ref,
    unit_ref,
    inverse_ref,
    vec_ref,
    out_weight_ref,
    total_ref,
    low_ref,
    grad_ref,
    sums_ref,
):
    added = share_ref[...].astype(F32) + recv_ref[...].astype(F32)
    upstream = second_ref[...] + added
    unit = unit_ref[...]
    first = norm_back(upstream, unit, inverse_ref[...], vec_ref[layer, 1:2, :])
    sums_ref[...] = jnp.zeros_like(sums_ref)
    sums_ref[0:1, :] = jnp.sum(upstream * unit, 0, keepdims=True)
    sums_ref[1:2, :] = jnp.sum(upstream, 0, keepdims=True)
    sums_ref[2:3, :] = jnp.sum(first, 0, keepdims=True)
    total_ref[...] = first
    low = first.astype(BF16)
    low_ref[...] = low
    grad_ref[...] = dot(low, out_weight_ref[layer], 1, 1).astype(BF16)


def joint_back_kernel(layer, place, core_ref, *refs):
    pairs = (len(refs) - 6) // 3
    q_refs, own_refs, recv_refs = (refs[k * pairs : (k + 1) * pairs] for k in range(3))
    q_weight_ref, kv_weight_ref, mine_ref, theirs_ref, bias_ref, part_ref = refs[3 * pairs :]
    width = 128 * pairs
    local = width // 2
    keep_span = slice(place * CHUNK, (place + 1) * CHUNK)
    q_grad = jnp.concatenate([ref[keep_span, :] for ref in q_refs], 1)
    both = [
        (own[place] + recv[place].astype(F32)).astype(BF16) for own, recv in zip(own_refs, recv_refs)
    ]
    kv_grad = jnp.concatenate(
        [part[:, :128] for part in both] + [part[:, 128:] for part in both], 1
    )
    first = core_ref[0] == 0
    for member, value in enumerate((q_grad, kv_grad[:, :width], kv_grad[:, width:])):
        left, right = value[:, :local].astype(F32), value[:, local:].astype(F32)
        lanes = slice(member * local, (member + 1) * local)
        mine_ref[:, lanes] = jnp.where(first, left, right).astype(BF16)
        theirs_ref[:, lanes] = jnp.where(first, right, left).astype(BF16)
    bias_ref[...] = jnp.zeros_like(bias_ref)
    bias_ref[0:1, :] = jnp.sum(q_grad.astype(F32), 0, keepdims=True)
    bias_ref[1:2, :] = jnp.sum(kv_grad[:, width:].astype(F32), 0, keepdims=True)
    part_ref[...] = (
        dot(q_grad, q_weight_ref[layer]) + dot(kv_grad, kv_weight_ref[layer])
    ).astype(BF16)


def weights_kernel(core_ref, *refs):
    sources, vectors, small_ref, other_ref = refs[:8], refs[8:14], refs[14], refs[15]
    q_ref, kv_ref, out_ref, vec_ref, q_bias_ref, kv_bias_ref, unit_bias_ref = refs[16:]
    local = sources[0].shape[1]
    width = 2 * local
    own_row = pl.multiple_of(core_ref[0] * local, local)
    other_row = pl.multiple_of((1 - core_ref[0]) * local, local)
    for layer in range(LAYERS):
        for member, (target, start) in enumerate(
            ((q_ref, 0), (kv_ref, 0), (kv_ref, width), (out_ref, 0))
        ):
            target[layer, pl.ds(start + own_row, local), :] = sources[2 * member][layer]
            target[layer, pl.ds(start + other_row, local), :] = sources[2 * member + 1][layer]

    first = core_ref[0] == 0
    for layer in range(LAYERS):
        row = slice(layer, layer + 1)
        for member, vector in enumerate(vectors):
            vec_ref[layer, member : member + 1, :] = vector[...].astype(F32)[row]
        if layer == 0:
            vec_ref[layer, 6:7, :] = jnp.ones_like(vec_ref[layer, 6:7, :])
            vec_ref[layer, 7:8, :] = jnp.zeros_like(vec_ref[layer, 7:8, :])
        else:
            vec_ref[layer, 6:8, :] = vec_ref[layer - 1, 4:6, :]
        own = small_ref[...].astype(F32)[row]
        other = other_ref[...].astype(F32)[row]
        kv_bias_ref[layer] = jnp.zeros_like(kv_bias_ref[layer])
        for target, start, lanes in (
            (q_bias_ref, 0, slice(0, local)),
            (kv_bias_ref, width, slice(local, width)),
        ):
            left, right = own[:, lanes], other[:, lanes]
            target[layer, :, start : start + local] = jnp.where(first, left, right)
            target[layer, :, start + local : start + width] = jnp.where(first, right, left)
        units = own.shape[1] - width
        unit_bias_ref[layer, :, :units] = own[:, width:]
        unit_bias_ref[layer, :, units:] = other[:, width:]


def widen_kernel(source_ref, target_ref):
    target_ref[0] = source_ref[...].astype(F32)


def unpack_rows_kernel(place_ref, *refs):
    count = 1 if len(refs) == 2 else 4
    sources, targets = refs[:-count], refs[-count:]
    rows = targets[0].shape[1]
    start = 0
    for number, source in enumerate(sources):
        pieces, size = source.shape[0], source.shape[1]
        for piece in range(pieces):
            target, row = targets[start // rows], start % rows
            target[0, row : row + size, :] = source[piece ^ place_ref[number]].astype(F32)
            start += size


class Wide:
    def __init__(self, size):
        self.small = size == 8
        index = lax.axis_index("wide")
        self.bits = {}
        if self.small:
            for name, reach in (("y", 1), ("near", 2), ("far", 4)):
                self.bits[name] = (
                    (index // reach) % 2,
                    [(number, number ^ reach) for number in range(size)],
                )

    def place(self, order):
        if not self.small:
            return jnp.int32(0)
        first, second, third = (self.bits[name][0] for name in order)
        return (first * 4 + second * 2 + third).astype(jnp.int32)

    def chain(self, value, order):
        return Chain(self, value, order)

    def exchanged(self, value):
        if not self.small:
            return lax.psum(value, "wide")
        for name in ("y", "near", "far"):
            low = value.astype(BF16)
            value = low.astype(F32) + lax.ppermute(low, "wide", self.bits[name][1]).astype(F32)
        return value


def gate(value, *later):
    return lax.optimization_barrier((value,) + later)[0] if later else value


class Chain:
    def __init__(self, wide, value, order):
        self.wide, self.order, self.step = wide, order, 0
        self.addends, self.pieces = [value], None

    def advance(self, *later):
        if not self.wide.small:
            if self.pieces is None:
                value = self.addends[0]
                self.pieces = lax.psum(value, "wide").reshape(8, -1, value.shape[1])
            return self.pieces
        self.step += 1
        if self.step <= 3:
            bit, pairs = self.wide.bits[self.order[self.step - 1]]
            parts = self.addends[:-1] + [gate(self.addends[-1], *later)]
            split = [part.reshape(2, part.shape[0] // 2, part.shape[1]) for part in parts]
            sent = sum(
                lax.dynamic_index_in_dim(part, 1 - bit, 0, False).astype(F32) for part in split
            ).astype(BF16)
            mine = [lax.dynamic_index_in_dim(part, bit, 0, False) for part in split]
            self.addends = mine + [lax.ppermute(sent, "wide", pairs)]
            return sent
        if self.step == 4:
            parts = self.addends[:-1] + [gate(self.addends[-1], *later)]
            sent = sum(part.astype(F32) for part in parts).astype(BF16)[None]
        else:
            sent = jnp.concatenate([self.pieces, gate(self.received, *later)], 0)
        self.pieces = sent
        self.received = lax.ppermute(sent, "wide", self.wide.bits[self.order[6 - self.step]][1])
        return sent

    def finish(self, *later):
        while self.step < 6 and self.wide.small:
            self.advance()
        if not self.wide.small:
            return self.advance()
        return jnp.concatenate([self.pieces, gate(self.received, *later)], 0)


def on_device(wide, *arguments):
    (
        tokens,
        buckets,
        lengths,
        type_table,
        query_weight,
        query_bias,
        key_weight,
        value_weight,
        value_bias,
        output_weight,
        output_bias,
        attention_gain,
        attention_shift,
        up_weight,
        up_bias,
        down_weight,
        down_bias,
        feed_gain,
        feed_shift,
        cotangent,
    ) = arguments
    share, model = tokens.shape
    lane = 2 * share
    chunks = lane // CHUNK
    local = query_weight.shape[2]
    width = 2 * local
    head_count = width // HEAD_DIM
    units = up_weight.shape[2]
    place = lax.axis_index("narrow")
    chip, core = place // 2, place % 2
    first_chip, first_core = chip == 0, core == 0

    def by_core(own, other, axis):
        return jnp.where(
            first_core,
            jnp.concatenate([own, other], axis),
            jnp.concatenate([other, own], axis),
        )

    def by_chip(own, other):
        return jnp.where(
            first_chip, jnp.concatenate([own, other], 0), jnp.concatenate([other, own], 0)
        )

    def own_rows(rows):
        return jnp.where(first_chip, rows[:share], rows[share:])

    def other_rows(rows):
        return jnp.where(first_chip, rows[share:], rows[:share])

    lane_tokens = by_chip(tokens, over_chip(tokens))
    lane_buckets = by_chip(buckets, over_chip(buckets))
    lane_cotangent = by_chip(cotangent, over_chip(cotangent))

    smem = pl.BlockSpec(memory_space=pltpu.SMEM)
    core_number = core.astype(jnp.int32).reshape(1)
    shards = []
    turned_weights = [
        jnp.swapaxes(weight, 1, 2) for weight in (query_weight, key_weight, value_weight)
    ]
    for weight in turned_weights + [output_weight]:
        shards += [(weight, ON_CHIP), (over_core(weight), ON_CHIP)]

    small = jnp.concatenate([query_bias, value_bias, up_bias], 1)
    vectors = [
        output_bias,
        attention_gain,
        attention_shift,
        down_bias,
        feed_gain,
        feed_shift,
        small,
        over_core(small),
    ]
    qw, kvw, ow, vec, q_bias, kv_bias, unit_bias = call(
        weights_kernel,
        None,
        [(core_number, smem)] + shards + [(vector, ON_CHIP) for vector in vectors],
        [
            (shape, dtype, ON_CHIP, None)
            for shape, dtype in (
                ((LAYERS, width, model), BF16),
                ((LAYERS, 2 * width, model), BF16),
                ((LAYERS, width, model), BF16),
                ((LAYERS, 8, model), F32),
                ((LAYERS, 1, width), F32),
                ((LAYERS, 1, 2 * width), F32),
                ((LAYERS, 1, 2 * units), F32),
            )
        ],
    )
    up_other = over_core(up_weight)
    down_other = over_core(down_weight)

    ends = jnp.cumsum(lengths[0], dtype=jnp.int32)
    offsets = lax.iota(jnp.int32, share)
    spots = jnp.concatenate(
        [
            offsets + (block * 2 + which) * share
            for which in (core, 1 - core)
            for block in range(2)
        ]
    )
    labels = jnp.sum((spots[:, None] >= ends[None, :]).astype(jnp.int32), 1, dtype=jnp.int32)
    tiles = 2 * chunks
    tile_labels = labels.reshape(tiles, CHUNK)
    present = jnp.any(
        tile_labels[:, :, None] == lax.iota(jnp.int32, lengths.shape[1])[None, None, :], axis=1
    )
    bits = jnp.sum(
        jnp.where(present, jnp.left_shift(1, lax.iota(jnp.int32, lengths.shape[1]))[None, :], 0),
        axis=1,
        dtype=jnp.int32,
    )
    bits = jnp.concatenate([bits, bits[:chunks]])
    k_labels = tile_labels[:, :, None]
    q_labels = tile_labels[:chunks, None, :]

    block = (CHUNK, model)

    def layer_spec(layer, shape):
        return pl.BlockSpec((1,) + shape, lambda *ids: (layer,) + (0,) * len(shape))

    selector = (lane_buckets[:, None] == lax.iota(jnp.int32, type_table.shape[0])[None, :]).astype(
        BF16
    )
    stream = lane_tokens.astype(F32) + dot(selector, type_table)
    low_first = stream.astype(BF16)
    state = [stream[CHUNK * i : CHUNK * (i + 1)] for i in range(chunks)]
    kept = []
    for layer in range(LAYERS):
        keep = {}
        if layer == 0:
            kv = (dot(low_first, kvw[0], 1, 1) + kv_bias[0]).astype(BF16)
            queries = ((dot(low_first, qw[0], 1, 1) + q_bias[0]) * HEAD_DIM**-0.5).astype(BF16)
            low_in, kv, queries = (
                [value[CHUNK * i : CHUNK * (i + 1)] for i in range(chunks)]
                for value in (low_first, kv, queries)
            )
            kv_other = [over_core(part) for part in kv]
        else:
            low_in, queries, kv, kv_other = [], [], [], []
            units_now, inverses = [], []
            for i in range(chunks):
                outs = call(
                    functools.partial(project_kernel, layer, i),
                    None,
                    [
                        (value, ON_CHIP)
                        for value in (
                            state[i],
                            feed_share[i],
                            feed_recv[i],
                            vec,
                            qw,
                            kvw,
                            q_bias,
                            kv_bias,
                        )
                    ],
                    [
                        (block, F32, ON_CHIP, None),
                        ((CHUNK, 1), F32, ON_CHIP, None),
                        (block, BF16, ON_CHIP, None),
                        ((CHUNK, width), BF16, ON_CHIP, None),
                        ((CHUNK, 2 * width), BF16, ON_CHIP, None),
                    ],
                    cost=2,
                )
                units_now.append(outs[0])
                inverses.append(outs[1])
                low_in.append(outs[2])
                queries.append(outs[3])
                kv.append(outs[4])
                kv_other.append(over_core(outs[4]))
            state = units_now
            kept[layer - 1]["second_unit"] = units_now
            kept[layer - 1]["second_inverse"] = inverses
        kv_all, turned = call(
            gather_kernel,
            None,
            [(part, ON_CHIP) for part in kv + kv_other],
            [
                ((tiles, CHUNK, 2 * width), BF16, ON_CHIP, None),
                ((tiles, 2 * width, CHUNK), BF16, ON_CHIP, None),
            ],
            cost=2,
        )
        context, exact, logsum, shares = [], [], [], []
        for i in range(chunks):
            outs = call(
                functools.partial(attend_kernel, head_count, layer, i),
                None,
                [(bits, smem)]
                + [
                    (value, ON_CHIP)
                    for value in (queries[i], kv_all, turned, q_labels, k_labels, ow)
                ],
                [
                    ((CHUNK, width), BF16, ON_CHIP, None),
                    ((CHUNK, width), F32, ON_CHIP, None),
                    ((8, CHUNK), F32, ON_CHIP, None),
                    (block, BF16, ON_CHIP, None),
                ],
                scratch=[
                    pltpu.VMEM((head_count, CHUNK, 128), BF16),
                    pltpu.VMEM((width, CHUNK), F32),
                    pltpu.VMEM((head_count, 8, CHUNK), F32),
                    pltpu.VMEM((head_count, 8, CHUNK), F32),
                    pltpu.VMEM((head_count, tiles, CHUNK, CHUNK), F32),
                ],
                cost=6,
                limit=20,
            )
            for target, value in zip((context, exact, logsum, shares), outs):
                target.append(value)
        received = [over_chip(part) for part in shares]
        low_middle, act, slope, first_unit, first_inverse, feed_share = [], [], [], [], [], []
        for i in range(chunks):
            outs = call(
                functools.partial(feed_kernel, layer, i),
                None,
                [
                    (value, ON_CHIP)
                    for value in (
                        state[i],
                        shares[i],
                        received[i],
                        vec,
                        up_weight,
                        up_other,
                        unit_bias,
                        down_weight,
                        down_other,
                    )
                ],
                [
                    (block, F32, ON_CHIP, None),
                    ((CHUNK, 1), F32, ON_CHIP, None),
                    (block, BF16, ON_CHIP, None),
                    ((CHUNK, 2 * units), BF16, ON_CHIP, None),
                    ((CHUNK, 2 * units), BF16, ON_CHIP, None),
                    (block, BF16, ON_CHIP, None),
                ],
                cost=8,
            )
            for target, value in zip(
                (first_unit, first_inverse, low_middle, act, slope, feed_share), outs
            ):
                target.append(value)
        feed_recv = [over_chip(part) for part in feed_share]
        state = first_unit
        keep.update(
            low_in=low_in,
            queries=queries,
            kv_all=kv_all,
            turned=turned,
            context=context,
            exact=exact,
            logsum=logsum,
            first_unit=first_unit,
            first_inverse=first_inverse,
            low_middle=low_middle,
            act=act,
            slope=slope,
        )
        kept.append(keep)

    sums = Wide(wide)
    pair_order, other_order = ("y", "near", "far"), ("near", "y", "far")

    def halves(full, axis):
        left, right = jnp.split(full, 2, axis)
        return jnp.where(first_core, left, right), jnp.where(first_core, right, left)

    def unpacked(kernel, layer, places, sources, shapes, buffers, scratch=()):
        return call(
            kernel,
            (1,),
            ([] if places is None else [(jnp.stack(places), smem)])
            + [(source, whole(source.shape)) for source in sources],
            [
                ((LAYERS,) + shape, F32, layer_spec(layer, shape), buffer)
                for shape, buffer in zip(shapes, buffers)
            ],
            scratch,
        )

    turned_out = [None] * 4
    shared = [None] * LAYERS
    split_vectors = [None] * LAYERS
    encoded = []
    for layer in reversed(range(LAYERS)):
        keep = kept[layer]
        top_layer = layer == LAYERS - 1
        second, low_second, up_grad, unit_sums, second_sums, parts = [], [], [], [], [], []
        for i in range(chunks):
            if top_layer:
                upstream = lane_cotangent
                unit = keep["first_unit"][i]
                inverse = keep["first_inverse"][i]
                added = (feed_share[i], feed_recv[i])
            else:
                upstream = first_total[i]
                unit = keep["second_unit"][i]
                inverse = keep["second_inverse"][i]
                added = (joint_share[i], joint_recv[i])
            outs = call(
                functools.partial(feed_back_kernel, layer, i, top_layer),
                None,
                [
                    (value, ON_CHIP)
                    for value in (
                        upstream,
                        unit,
                        inverse,
                        added[0],
                        added[1],
                        vec,
                        keep["slope"][i],
                        up_weight,
                        up_other,
                        down_weight,
                        down_other,
                    )
                ],
                [
                    (block if top_layer else (8, 128), BF16, ON_CHIP, None),
                    (block, F32, ON_CHIP, None),
                    (block, BF16, ON_CHIP, None),
                    ((CHUNK, 2 * units), BF16, ON_CHIP, None),
                    ((1, 2 * units), F32, ON_CHIP, None),
                    ((8, model), F32, ON_CHIP, None),
                    (block, BF16, ON_CHIP, None),
                ],
                cost=8,
                after=[upper.advance(*second_sums[1:2])] if i != 1 and not top_layer else [],
            )
            if top_layer:
                encoded.append(outs[0])
            for target, value in zip(
                (second, low_second, up_grad, unit_sums, second_sums, parts), outs[1:]
            ):
                target.append(value)
        received = [over_chip(part) for part in parts]

        def weight_grad(lefts, rights, shape, left_start=0, right_start=0, received=()):
            return call(
                functools.partial(weight_grad_kernel, chunks, left_start, right_start),
                None,
                [(value, ON_CHIP) for value in [*lefts, *rights, *received]],
                [(shape, BF16, ON_CHIP, None)],
                cost=2,
            )[0]

        square = (model, units)
        down_other_grad = over_core(
            weight_grad(keep["act"], low_second, square[::-1], left_start=units)
        )
        up_other_grad = over_core(
            weight_grad(keep["low_middle"], up_grad, square, right_start=units)
        )
        down_grad = weight_grad(
            keep["act"], low_second, square[::-1], received=[down_other_grad]
        )
        up_weight_grad = weight_grad(
            keep["low_middle"], up_grad, square, received=[up_other_grad]
        )
        first_total, low_total, context_grad, first_sums = [], [], [], []
        for i in range(chunks):
            outs = call(
                functools.partial(context_back_kernel, layer, i),
                None,
                [
                    (value, ON_CHIP)
                    for value in (
                        second[i],
                        parts[i],
                        received[i],
                        keep["first_unit"][i],
                        keep["first_inverse"][i],
                        vec,
                        ow,
                    )
                ],
                [
                    (block, F32, ON_CHIP, None),
                    (block, BF16, ON_CHIP, None),
                    ((CHUNK, width), BF16, ON_CHIP, None),
                    ((8, model), F32, ON_CHIP, None),
                ],
                after=[upper.advance(second_sums[2])] if i == 1 and not top_layer else [],
            )
            for target, value in zip((first_total, low_total, context_grad, first_sums), outs):
                target.append(value)
        own, other = call(
            functools.partial(out_grad_kernel, chunks),
            None,
            [(core_number, smem)]
            + [(value, ON_CHIP) for value in keep["context"] + low_total],
            [((local, model), F32, ON_CHIP, None), ((local, model), BF16, ON_CHIP, None)],
            scratch=[pltpu.VMEM((width, model), F32)],
        )
        out_grad = (own + over_core(other).astype(F32)).astype(BF16)
        pending = [out_grad, up_weight_grad, down_grad]
        if top_layer:
            feed_sums = lax.psum((up_weight_grad, down_grad), "wide")
        else:
            strands = [
                sums.chain(up_weight_grad, pair_order),
                sums.chain(down_grad, other_order),
            ]
            pending = [out_grad, upper.advance(first_sums[2])] + [
                strand.advance() for strand in strands
            ]
        half_shape = (chunks, CHUNK, 256)
        q_grads, kv_owns, kv_recvs = [], [], []
        for pair in range(head_count // 2):
            q_grad, kv_grad, kv_grad_other = call(
                functools.partial(attend_back_kernel, pair, head_count, chunks),
                None,
                [(bits, smem)]
                + [
                    (value, ON_CHIP)
                    for value in [keep["kv_all"], keep["turned"], q_labels, k_labels]
                    + keep["queries"]
                    + context_grad
                    + keep["exact"]
                    + keep["logsum"]
                ],
                [
                    ((lane, 128), BF16, ON_CHIP, None),
                    (half_shape, F32, ON_CHIP, None),
                    (half_shape, BF16, ON_CHIP, None),
                ],
                scratch=[
                    pltpu.VMEM((2, CHUNK, 128), BF16),
                    pltpu.VMEM((2, CHUNK, 128), BF16),
                    pltpu.VMEM((8, CHUNK), F32),
                    pltpu.VMEM((128, CHUNK), F32),
                    pltpu.VMEM((tiles, CHUNK, 256), F32),
                ],
                cost=10,
                limit=16,
                after=pending + q_grads[-1:],
            )
            pending = []
            if not top_layer:
                if pair < 2:
                    pending = [upper.advance(q_grad)]
                pending += [strand.advance(q_grad) for strand in strands]
            q_grads.append(q_grad)
            kv_owns.append(kv_grad)
            kv_recvs.append(over_core(kv_grad_other))
        joint_own, joint_other, bias_sums, joint_share = [], [], [], []
        for i in range(chunks):
            outs = call(
                functools.partial(joint_back_kernel, layer, i),
                None,
                [(core_number, smem)]
                + [(value, ON_CHIP) for value in q_grads + kv_owns + kv_recvs + [qw, kvw]],
                [
                    ((CHUNK, 3 * local), BF16, ON_CHIP, None),
                    ((CHUNK, 3 * local), BF16, ON_CHIP, None),
                    ((8, width), F32, ON_CHIP, None),
                    (block, BF16, ON_CHIP, None),
                ],
                cost=2,
            )
            for target, value in zip((joint_own, joint_other, bias_sums, joint_share), outs):
                target.append(value)
        if layer > 0:
            joint_recv = [over_chip(part) for part in joint_share]
        joint_recv_grad = over_core(weight_grad(joint_other, keep["low_in"], (3 * local, model)))
        joint_grad = weight_grad(
            joint_own, keep["low_in"], (3 * local, model), received=[joint_recv_grad]
        )
        flat = [(local, model)] * 4
        if layer > 0:
            upper = sums.chain(jnp.concatenate([joint_grad, out_grad], 0), other_order)
        else:
            (up_out,) = unpacked(
                widen_kernel, 1, None, [gate(feed_sums[0], joint_share[-1])], [square], [None]
            )
            (down_out,) = unpacked(
                widen_kernel, 1, None, [gate(feed_sums[1], joint_share[-1])], [square[::-1]], [None]
            )
            turned_out = unpacked(
                unpack_rows_kernel, 1, [sums.place(other_order)], [upper.finish()], flat, turned_out
            )
            first_chain = sums.chain(joint_grad[: 2 * local], pair_order)
            second_chain = sums.chain(
                jnp.concatenate([joint_grad[2 * local :], out_grad], 0), other_order
            )
            turned_out = unpacked(
                unpack_rows_kernel,
                layer,
                [sums.place(pair_order), sums.place(other_order)],
                [first_chain.finish(), second_chain.finish()],
                flat,
                turned_out,
            )
            (up_out,) = unpacked(
                unpack_rows_kernel,
                layer,
                [sums.place(pair_order)],
                [strands[0].finish()],
                [square],
                [up_out],
            )
            (down_out,) = unpacked(
                unpack_rows_kernel,
                layer,
                [sums.place(other_order)],
                [strands[1].finish()],
                [square[::-1]],
                [down_out],
            )
        second_sum, first_sum = sum(second_sums), sum(first_sums)
        shared[layer] = jnp.concatenate([second_sum[:3], first_sum[:3]], 0)
        unit_sum, bias_sum = sum(unit_sums), sum(bias_sums)
        q_own, q_other = halves(bias_sum[0], 0)
        v_own, v_other = halves(bias_sum[1], 0)
        split_vectors[layer] = (
            jnp.concatenate([q_own, v_own, unit_sum[0, :units]]),
            jnp.concatenate([q_other, v_other, unit_sum[0, units:]]),
        )

    joint_rows = jnp.concatenate(joint_share, 0)
    first_rows = own_rows(jnp.concatenate(first_total, 0))
    joint_theirs = over_chip(other_rows(joint_rows)).astype(F32)
    tokens_grad = first_rows + (own_rows(joint_rows).astype(F32) + joint_theirs)
    own_selector = (buckets[:, None] == lax.iota(jnp.int32, type_table.shape[0])[None, :]).astype(
        BF16
    )
    high = first_rows.astype(BF16)
    rest = (first_rows - high.astype(F32)).astype(BF16)
    table = (
        dot(own_selector, high, 0, 0) + dot(own_selector, rest, 0, 0)
    ) + dot(selector, joint_rows, 0, 0)

    common = jnp.concatenate(shared, 0)
    mine = jnp.stack([value[0] for value in split_vectors])
    theirs = jnp.stack([value[1] for value in split_vectors])
    vectors = jnp.concatenate([common.reshape(-1), mine.reshape(-1)])
    sent = jnp.concatenate([common.reshape(-1), theirs.reshape(-1)])
    vectors = (vectors + over_core(sent)).reshape(-1, model)

    table_own, table_other = halves(table, 0)
    table_half = table_own + over_core(table_other.astype(BF16)).astype(F32)
    low_half = table_half.astype(BF16)
    table_half = low_half.astype(F32) + over_chip(low_half).astype(F32)
    packed = sums.exchanged(jnp.concatenate([table_half, vectors], 0))
    table_half = packed[: table_half.shape[0]]
    vectors = packed[table_half.shape[0] :].reshape(-1)
    low_half = table_half.astype(BF16)
    table_grad = by_core(low_half, over_core(low_half), 0).astype(F32)
    common = vectors[: common.size].reshape(LAYERS, 6, model)
    mine = vectors[common.size :].reshape(LAYERS, -1)

    return (
        own_rows(jnp.concatenate(encoded, 0)),
        tokens_grad,
        table_grad,
        jnp.swapaxes(turned_out[0], 1, 2),
        mine[:, :local],
        jnp.swapaxes(turned_out[1], 1, 2),
        jnp.swapaxes(turned_out[2], 1, 2),
        mine[:, local : 2 * local],
        turned_out[3],
        common[:, 5],
        common[:, 3],
        common[:, 4],
        up_out,
        mine[:, 2 * local :],
        down_out,
        common[:, 2],
        common[:, 0],
        common[:, 1],
    )


def solution(mesh):
    rows = P(("wide", "narrow"), None)
    third = P(None, None, "narrow")
    second = P(None, "narrow")
    middle = P(None, "narrow", None)
    in_specs = (
        rows,
        P(("wide", "narrow")),
        P("wide", None),
        P(),
        third,
        second,
        third,
        third,
        second,
        middle,
        P(),
        P(),
        P(),
        third,
        second,
        middle,
        P(),
        P(),
        P(),
        rows,
    )
    out_specs = (
        rows,
        rows,
        P(),
        third,
        second,
        third,
        third,
        second,
        middle,
        P(),
        P(),
        P(),
        third,
        second,
        middle,
        P(),
        P(),
        P(),
    )
    return jax.shard_map(
        functools.partial(on_device, mesh.shape["wide"]),
        mesh=mesh,
        in_specs=in_specs,
        out_specs=out_specs,
        check_vma=False,
    )
```

```python
import functools

import jax
import jax.numpy as jnp
from jax import lax
from jax.experimental import pallas as pl
from jax.experimental.pallas import tpu as pltpu
from jax.sharding import PartitionSpec as P

HEAD_DIM = 64
LAYERS = 2
CHUNK = 256
EPS = 1e-12
ROOT_HALF = 0.7071067811865476
DENSITY = 0.3989422804014327
NEG = -1e30
F32 = jnp.float32
BF16 = jnp.bfloat16
MIB = 1 << 20
CORE_SWAP = [(0, 1), (1, 0), (2, 3), (3, 2)]
CHIP_SWAP = [(0, 2), (2, 0), (1, 3), (3, 1)]


def over_core(value):
    return lax.ppermute(value, "narrow", CORE_SWAP)


def over_chip(value):
    return lax.ppermute(value, "narrow", CHIP_SWAP)


def dot(left, right, left_axis=1, right_axis=0):
    return lax.dot_general(
        left, right, (((left_axis,), (right_axis,)), ((), ())), preferred_element_type=F32
    )


def norm_parts(summed):
    row_mean = jnp.mean(summed, -1, keepdims=True)
    centred = summed - row_mean
    spread = jnp.mean(centred * centred, -1, keepdims=True)
    inverse = lax.rsqrt(spread + EPS)
    return centred * inverse, inverse


def norm_back(upstream, unit_rows, inverse, gain_row):
    scaled = upstream * gain_row
    return inverse * (
        scaled
        - jnp.mean(scaled, -1, keepdims=True)
        - unit_rows * jnp.mean(scaled * unit_rows, -1, keepdims=True)
    )


def gelu_parts(preact):
    size = jnp.abs(preact) * ROOT_HALF
    bell = jnp.exp(-(size * size))
    step = 1.0 / (1.0 + 0.3275911 * size)
    series = step * (
        0.254829592
        + step * (-0.284496736 + step * (1.421413741 + step * (-1.453152027 + step * 1.061405429)))
    )
    tail = 0.5 * series * bell
    cdf = jnp.where(preact >= 0.0, 1.0 - tail, tail)
    return preact * cdf, cdf + preact * DENSITY * bell


ON_CHIP = pl.BlockSpec(memory_space=pltpu.VMEM)


def whole(shape):
    zeros = (0,) * len(shape)
    return pl.BlockSpec(shape, lambda *ids: zeros)


def call(kernel, grid, inputs, outputs, scratch=(), cost=0, limit=16, after=()):
    arrays = [array for array, spec in inputs]
    specs = [spec for array, spec in inputs]
    aliases = {}
    for place, (shape, dtype, spec, buffer) in enumerate(outputs):
        if buffer is not None:
            aliases[len(arrays)] = place
            arrays.append(buffer)
            specs.append(pl.BlockSpec(memory_space=pl.ANY))
    for array in after:
        arrays.append(array)
        specs.append(pl.BlockSpec(memory_space=pl.ANY))
    given, extra = len(inputs), len(aliases) + len(after)

    def body(*refs):
        kernel(*refs[:given], *refs[given + extra :])

    return pl.pallas_call(
        body,
        **({} if grid is None else {"grid": grid}),
        in_specs=specs,
        out_specs=[spec for shape, dtype, spec, buffer in outputs],
        out_shape=[
            jax.ShapeDtypeStruct(shape, dtype) for shape, dtype, spec, buffer in outputs
        ],
        scratch_shapes=list(scratch),
        input_output_aliases=aliases,
        compiler_params=pltpu.CompilerParams(vmem_limit_bytes=limit * MIB),
        cost_estimate=pl.CostEstimate(flops=cost * 4000000000, bytes_accessed=1, transcendentals=0),
    )(*arrays)


def gather_kernel(*refs):
    sources, (rows_ref, turned_ref) = refs[:-2], refs[-2:]
    for place, source in enumerate(sources):
        tile = source[...]
        rows_ref[place] = tile
        turned_ref[place] = tile.astype(F32).T.astype(BF16)


def split_pairs(pair_block, target, head_count):
    lanes = lax.broadcasted_iota(jnp.int32, (CHUNK, 2 * HEAD_DIM), 1)
    low_half = lanes < HEAD_DIM
    for head in range(head_count):
        pair = pair_block[:, (head // 2) * 128 : (head // 2) * 128 + 128]
        keep = low_half if head % 2 == 0 else jnp.logical_not(low_half)
        target[head] = jnp.where(keep, pair, jnp.zeros_like(pair))


def attend_kernel(
    head_count,
    layer,
    place,
    bits_ref,
    q_ref,
    kv_ref,
    turned_ref,
    q_label_ref,
    k_label_ref,
    out_weight_ref,
    context_ref,
    exact_ref,
    logsum_ref,
    share_ref,
    masked_q,
    total,
    top,
    mass,
    score_tiles,
):
    width = head_count * HEAD_DIM
    split_pairs(q_ref[...], masked_q, head_count)
    top[...] = jnp.full_like(top, NEG)
    mass[...] = jnp.zeros_like(mass)
    total[...] = jnp.zeros_like(total)
    tiles = kv_ref.shape[0]
    q_bits = bits_ref[tiles + place]

    def score_tile(tile, carry):
        @pl.when((bits_ref[tile] & q_bits) != 0)
        def _():
            hide = jnp.where(k_label_ref[tile] == q_label_ref[place], 0.0, NEG)
            for head in range(head_count):
                pair = (head // 2) * 128
                scores = dot(kv_ref[tile, :, pair : pair + 128], masked_q[head], 1, 1) + hide
                score_tiles[head, tile] = scores
                highest = jnp.max(scores.reshape(-1, 8, CHUNK), 0)
                top[head] = jnp.maximum(top[head], highest)

        return carry

    lax.fori_loop(0, tiles, score_tile, 0)
    for head in range(head_count):
        top[head] = jnp.broadcast_to(jnp.max(top[head], 0, keepdims=True), (8, CHUNK))

    def weigh_tile(tile, carry):
        @pl.when((bits_ref[tile] & q_bits) != 0)
        def _():
            for head in range(head_count):
                weights = jnp.exp(score_tiles[head, tile] - top[head, 0:1, :])
                mass[head] += jnp.sum(weights.reshape(-1, 8, CHUNK), 0)
                rows = slice(head * HEAD_DIM, (head + 1) * HEAD_DIM)
                total[rows, :] += dot(
                    turned_ref[tile, width + head * HEAD_DIM : width + (head + 1) * HEAD_DIM, :],
                    weights.astype(BF16),
                )

        return carry

    lax.fori_loop(0, tiles, weigh_tile, 0)
    logsum_ref[...] = jnp.zeros_like(logsum_ref)
    for head in range(head_count):
        rows = slice(head * HEAD_DIM, (head + 1) * HEAD_DIM)
        amount = jnp.sum(mass[head], 0, keepdims=True)
        total[rows, :] = total[rows, :] / amount
        logsum_ref[head : head + 1, :] = top[head, 0:1, :] + jnp.log(amount)
    exact = total[...].T
    exact_ref[...] = exact
    context = exact.astype(BF16)
    context_ref[...] = context
    share_ref[...] = dot(context, out_weight_ref[layer]).astype(BF16)


def attend_back_kernel(pair, head_count, chunks, *refs):
    bits_ref, kv_ref, turned_ref, q_label_ref, k_label_ref = refs[:5]
    q_refs, grad_refs, exact_refs, logsum_refs = (
        refs[5 + chunks * k : 5 + chunks * (k + 1)] for k in range(4)
    )
    q_grad_ref, own_ref, other_ref, masked_q, masked_grad, centre, q_total, kv_total = refs[
        5 + 4 * chunks :
    ]
    tiles = kv_ref.shape[0]
    lanes = slice(pair * 128, pair * 128 + 128)
    v_lanes = slice(head_count * HEAD_DIM + pair * 128, head_count * HEAD_DIM + pair * 128 + 128)
    kv_total[...] = jnp.zeros_like(kv_total)
    for place in range(chunks):
        split_pairs(q_refs[place][:, lanes], masked_q, 2)
        split_pairs(grad_refs[place][:, lanes], masked_grad, 2)
        crossed = (grad_refs[place][:, lanes].astype(F32) * exact_refs[place][:, lanes]).T
        for head in range(2):
            rows = slice(head * HEAD_DIM, (head + 1) * HEAD_DIM)
            centre[head : head + 1, :] = jnp.sum(crossed[rows, :], 0, keepdims=True)
        q_total[...] = jnp.zeros_like(q_total)
        q_bits = bits_ref[tiles + place]
        logsum_ref = logsum_refs[place]

        def one_tile(tile, carry):
            @pl.when((bits_ref[tile] & q_bits) != 0)
            def _():
                hide = jnp.where(k_label_ref[tile] == q_label_ref[place], 0.0, NEG)
                key_part = None
                value_part = None
                for head in range(2):
                    number = 2 * pair + head
                    scores = dot(kv_ref[tile, :, lanes], masked_q[head], 1, 1) + hide
                    weights = jnp.exp(scores - logsum_ref[number : number + 1, :])
                    weight_grad = dot(kv_ref[tile, :, v_lanes], masked_grad[head], 1, 1)
                    score_grad = (weights * (weight_grad - centre[head : head + 1, :])).astype(BF16)
                    value_now = dot(weights.astype(BF16), masked_grad[head])
                    key_now = dot(score_grad, masked_q[head])
                    value_part = value_now if value_part is None else value_part + value_now
                    key_part = key_now if key_part is None else key_part + key_now
                    rows = slice(head * HEAD_DIM, (head + 1) * HEAD_DIM)
                    turned = slice(number * HEAD_DIM, (number + 1) * HEAD_DIM)
                    q_total[rows, :] += dot(turned_ref[tile, turned, :], score_grad)
                kv_total[tile, :, :128] += key_part
                kv_total[tile, :, 128:] += value_part

            return carry

        lax.fori_loop(0, tiles, one_tile, 0)
        q_grad_ref[place * CHUNK : (place + 1) * CHUNK, :] = q_total[...].T.astype(
            BF16
        ) * jnp.asarray(HEAD_DIM**-0.5, BF16)
    own_ref[...] = kv_total[: tiles // 2]
    other_ref[...] = kv_total[tiles // 2 :].astype(BF16)


def weight_grad_kernel(chunks, left_start, right_start, *refs):
    lefts, rights, recv_refs = refs[:chunks], refs[chunks : 2 * chunks], refs[2 * chunks : -1]
    out_ref = refs[-1]
    rows, columns = out_ref.shape
    step = CHUNK if rows % CHUNK == 0 else rows
    for start in range(0, rows, step):
        left_lanes = slice(left_start + start, left_start + start + step)
        right_lanes = slice(right_start, right_start + columns)
        total = None
        for left, right in zip(lefts, rights):
            part = dot(left[:, left_lanes], right[:, right_lanes], 0, 0)
            total = part if total is None else total + part
        for recv_ref in recv_refs:
            total = total + recv_ref[start : start + step, :].astype(F32)
        out_ref[start : start + step, :] = total.astype(out_ref.dtype)


def out_grad_kernel(chunks, core_ref, *refs):
    lefts, rights, (own_ref, other_ref, full) = refs[:chunks], refs[chunks:-3], refs[-3:]
    total = None
    for left, right in zip(lefts, rights):
        part = dot(left[...], right[...], 0, 0)
        total = part if total is None else total + part
    full[...] = total
    local = own_ref.shape[0]
    own_ref[...] = full[pl.ds(pl.multiple_of(core_ref[0] * local, local), local), :]
    other_ref[...] = full[pl.ds(pl.multiple_of((1 - core_ref[0]) * local, local), local), :].astype(
        BF16
    )


def feed_kernel(
    layer,
    place,
    unit_ref,
    share_ref,
    recv_ref,
    vec_ref,
    up_own_ref,
    up_other_ref,
    bias_ref,
    down_own_ref,
    down_other_ref,
    new_unit_ref,
    inverse_ref,
    low_ref,
    act_ref,
    slope_ref,
    part_ref,
):
    stream = unit_ref[...] * vec_ref[layer, 6:7, :] + vec_ref[layer, 7:8, :]
    attention = share_ref[...].astype(F32) + recv_ref[...].astype(F32)
    unit, inverse = norm_parts(stream + attention + vec_ref[layer, 0:1, :])
    new_unit_ref[...] = unit
    inverse_ref[...] = inverse
    low_ref[...] = (unit * vec_ref[layer, 1:2, :] + vec_ref[layer, 2:3, :]).astype(BF16)
    units = up_own_ref.shape[2]
    total = None
    for half, (up_ref, down_ref) in enumerate(
        ((up_own_ref, down_own_ref), (up_other_ref, down_other_ref))
    ):
        lanes = slice(half * units, (half + 1) * units)
        act, slope = gelu_parts(dot(low_ref[...], up_ref[layer]) + bias_ref[layer, :, lanes])
        low_act = act.astype(BF16)
        act_ref[:, lanes] = low_act
        slope_ref[:, lanes] = slope.astype(BF16)
        part = dot(low_act, down_ref[layer])
        total = part if total is None else total + part
    part_ref[...] = total.astype(BF16)


def project_kernel(
    layer,
    place,
    unit_ref,
    share_ref,
    recv_ref,
    vec_ref,
    q_weight_ref,
    kv_weight_ref,
    q_bias_ref,
    kv_bias_ref,
    new_unit_ref,
    inverse_ref,
    low_ref,
    q_ref,
    kv_ref,
):
    old = layer - 1
    middle = unit_ref[...] * vec_ref[old, 1:2, :] + vec_ref[old, 2:3, :]
    feed = share_ref[...].astype(F32) + recv_ref[...].astype(F32)
    unit, inverse = norm_parts(middle + feed + vec_ref[old, 3:4, :])
    new_unit_ref[...] = unit
    inverse_ref[...] = inverse
    low = (unit * vec_ref[old, 4:5, :] + vec_ref[old, 5:6, :]).astype(BF16)
    low_ref[...] = low
    kv_ref[...] = (dot(low, kv_weight_ref[layer], 1, 1) + kv_bias_ref[layer]).astype(BF16)
    q_ref[...] = (
        (dot(low, q_weight_ref[layer], 1, 1) + q_bias_ref[layer]) * HEAD_DIM**-0.5
    ).astype(BF16)


def feed_back_kernel(
    layer,
    place,
    top_layer,
    up_ref,
    unit_ref,
    inverse_ref,
    share_ref,
    recv_ref,
    vec_ref,
    slope_ref,
    up_own_ref,
    up_other_ref,
    down_own_ref,
    down_other_ref,
    *rest,
):
    before = rest[:-7]
    encoded_ref, total_ref, low_ref, grad_ref, bias_ref, sums_ref, part_ref = rest[-7:]
    keep_span = slice(place * CHUNK, (place + 1) * CHUNK)
    added = share_ref[...].astype(F32) + recv_ref[...].astype(F32)
    if top_layer:
        middle = unit_ref[...] * vec_ref[layer, 1:2, :] + vec_ref[layer, 2:3, :]
        unit, inverse = norm_parts(middle + added + vec_ref[layer, 3:4, :])
        encoded_ref[...] = (unit * vec_ref[layer, 4:5, :] + vec_ref[layer, 5:6, :]).astype(BF16)
        upstream = up_ref[keep_span, :].astype(F32)
    else:
        unit = unit_ref[...]
        inverse = inverse_ref[...]
        upstream = up_ref[...] + added
        encoded_ref[...] = jnp.zeros_like(encoded_ref)
    second = norm_back(upstream, unit, inverse, vec_ref[layer, 4:5, :])
    sums_ref[...] = before[0][...] if before else jnp.zeros_like(sums_ref)
    sums_ref[0:1, :] += jnp.sum(upstream * unit, 0, keepdims=True)
    sums_ref[1:2, :] += jnp.sum(upstream, 0, keepdims=True)
    sums_ref[2:3, :] += jnp.sum(second, 0, keepdims=True)
    total_ref[...] = second
    low_ref[...] = second.astype(BF16)
    units = up_own_ref.shape[2]
    total = None
    for half, (up_weight_ref, down_ref) in enumerate(
        ((up_own_ref, down_own_ref), (up_other_ref, down_other_ref))
    ):
        lanes = slice(half * units, (half + 1) * units)
        grad = (
            dot(low_ref[...], down_ref[layer], 1, 1) * slope_ref[:, lanes].astype(F32)
        ).astype(BF16)
        grad_ref[:, lanes] = grad
        bias = jnp.sum(grad.astype(F32), 0, keepdims=True)
        bias_ref[:, lanes] = bias + before[1][:, lanes] if before else bias
        part = dot(grad, up_weight_ref[layer], 1, 1)
        total = part if total is None else total + part
    part_ref[...] = total.astype(BF16)


def context_back_kernel(
    layer,
    place,
    second_ref,
    share_ref,
    recv_ref,
    unit_ref,
    inverse_ref,
    vec_ref,
    out_weight_ref,
    *rest,
):
    before = rest[:-4]
    total_ref, low_ref, grad_ref, sums_ref = rest[-4:]
    added = share_ref[...].astype(F32) + recv_ref[...].astype(F32)
    upstream = second_ref[...] + added
    unit = unit_ref[...]
    first = norm_back(upstream, unit, inverse_ref[...], vec_ref[layer, 1:2, :])
    sums_ref[...] = before[0][...] if before else jnp.zeros_like(sums_ref)
    sums_ref[0:1, :] += jnp.sum(upstream * unit, 0, keepdims=True)
    sums_ref[1:2, :] += jnp.sum(upstream, 0, keepdims=True)
    sums_ref[2:3, :] += jnp.sum(first, 0, keepdims=True)
    total_ref[...] = first
    low = first.astype(BF16)
    low_ref[...] = low
    grad_ref[...] = dot(low, out_weight_ref[layer], 1, 1).astype(BF16)


def joint_back_kernel(
    layer,
    place,
    core_ref,
    *refs,
):
    pairs = (len(refs) - 6) // 3
    q_refs, own_refs, recv_refs = (refs[k * pairs : (k + 1) * pairs] for k in range(3))
    q_weight_ref, kv_weight_ref, mine_ref, theirs_ref, bias_ref, part_ref = refs[3 * pairs :]
    span = slice(place * CHUNK, (place + 1) * CHUNK)
    width = 128 * pairs
    local = width // 2
    q_grad = jnp.concatenate([ref[span, :] for ref in q_refs], 1)
    both = [
        (own[place] + recv[place].astype(F32)).astype(BF16)
        for own, recv in zip(own_refs, recv_refs)
    ]
    kv_grad = jnp.concatenate(
        [part[:, :128] for part in both] + [part[:, 128:] for part in both], 1
    )
    first = core_ref[0] == 0
    for member, value in enumerate((q_grad, kv_grad[:, :width], kv_grad[:, width:])):
        left, right = value[:, :local].astype(F32), value[:, local:].astype(F32)
        lanes = slice(member * local, (member + 1) * local)
        mine_ref[:, lanes] = jnp.where(first, left, right).astype(BF16)
        theirs_ref[:, lanes] = jnp.where(first, right, left).astype(BF16)
    bias_ref[...] = jnp.zeros_like(bias_ref)
    bias_ref[0:1, :] = jnp.sum(q_grad.astype(F32), 0, keepdims=True)
    bias_ref[1:2, :] = jnp.sum(kv_grad[:, width:].astype(F32), 0, keepdims=True)
    part_ref[...] = (
        dot(q_grad, q_weight_ref[layer]) + dot(kv_grad, kv_weight_ref[layer])
    ).astype(BF16)


def weights_kernel(core_ref, *refs):
    sources, vectors, small_ref, other_ref = refs[:8], refs[8:14], refs[14], refs[15]
    q_ref, kv_ref, out_ref, vec_ref, q_bias_ref, kv_bias_ref, unit_bias_ref = refs[16:]
    local = sources[0].shape[1]
    width = 2 * local
    own_row = pl.multiple_of(core_ref[0] * local, local)
    other_row = pl.multiple_of((1 - core_ref[0]) * local, local)
    for layer in range(LAYERS):
        for member, (target, start) in enumerate(
            ((q_ref, 0), (kv_ref, 0), (kv_ref, width), (out_ref, 0))
        ):
            target[layer, pl.ds(start + own_row, local), :] = sources[2 * member][layer]
            target[layer, pl.ds(start + other_row, local), :] = sources[2 * member + 1][layer]

    first = core_ref[0] == 0
    for layer in range(LAYERS):
        row = slice(layer, layer + 1)
        for member, vector in enumerate(vectors):
            vec_ref[layer, member : member + 1, :] = vector[...].astype(F32)[row]
        if layer == 0:
            vec_ref[layer, 6:7, :] = jnp.ones_like(vec_ref[layer, 6:7, :])
            vec_ref[layer, 7:8, :] = jnp.zeros_like(vec_ref[layer, 7:8, :])
        else:
            vec_ref[layer, 6:8, :] = vec_ref[layer - 1, 4:6, :]
        own = small_ref[...].astype(F32)[row]
        other = other_ref[...].astype(F32)[row]
        kv_bias_ref[layer] = jnp.zeros_like(kv_bias_ref[layer])
        for target, start, lanes in (
            (q_bias_ref, 0, slice(0, local)),
            (kv_bias_ref, width, slice(local, width)),
        ):
            left, right = own[:, lanes], other[:, lanes]
            target[layer, :, start : start + local] = jnp.where(first, left, right)
            target[layer, :, start + local : start + width] = jnp.where(first, right, left)
        units = own.shape[1] - width
        unit_bias_ref[layer, :, :units] = own[:, width:]
        unit_bias_ref[layer, :, units:] = other[:, width:]


def halve_kernel(bit, numbers_ref, *refs):
    parts, (sent_ref, kept_ref) = refs[:-2], refs[-2:]
    half = sent_ref.shape[0]
    for target, number in ((sent_ref, 1 - numbers_ref[bit]), (kept_ref, numbers_ref[bit])):
        rows = pl.ds(pl.multiple_of(number * half, half), half)
        target[...] = sum(part[rows, :].astype(F32) for part in parts).astype(target.dtype)


def add_kernel(kept_ref, recv_ref, piece_ref):
    piece_ref[0] = (kept_ref[...] + recv_ref[...].astype(F32)).astype(BF16)


def join_kernel(pieces_ref, recv_ref, joined_ref):
    count = pieces_ref.shape[0]
    joined_ref[:count] = pieces_ref[...]
    joined_ref[count:] = recv_ref[...]


def arrange(place, pieces_ref, recv_ref, full):
    count, rows = pieces_ref.shape[0], pieces_ref.shape[1]
    for number in range(2 * count):
        source = pieces_ref[number] if number < count else recv_ref[number - count]
        start = pl.multiple_of((number ^ place) * rows, rows)
        full[pl.ds(start, rows), :] = source.astype(F32)


def unpack_kernel(place, numbers_ref, pieces_ref, recv_ref, *refs):
    targets, full = refs[:-1], refs[-1]
    arrange(numbers_ref[place], pieces_ref, recv_ref, full)
    start = 0
    for target in targets:
        rows = target.shape[-2]
        value = full[start : start + rows, :]
        if len(target.shape) == 3:
            target[0] = value
        else:
            target[...] = value.astype(target.dtype)
        start += rows


def vectors_unpack_kernel(place, numbers_ref, pieces_ref, recv_ref, *refs):
    q_ref, table_ref, targets, full = refs[0], refs[1], refs[2:-1], refs[-1]
    arrange(numbers_ref[place], pieces_ref, recv_ref, full)
    local = q_ref.shape[1]
    half = table_ref.shape[0]
    q_ref[0] = full[:local, :]
    table_ref[...] = full[local : local + half, :].astype(BF16)
    for layer in range(LAYERS):
        start = local + half + 8 * layer
        row = slice(layer, layer + 1)
        for member in range(7):
            targets[member][row, :] = full[start + member : start + member + 1, :]
        last = full[start + 7 : start + 8, :]
        for member in range(2):
            targets[7 + member][row, :] = last[:, member * local : (member + 1) * local]


def table_kernel(chunks, share, numbers_ref, bucket_ref, *refs):
    joints, firsts = refs[:chunks], refs[chunks : 2 * chunks]
    vectors = refs[2 * chunks : -3]
    mine_ref, sent_ref, full = refs[-3:]
    buckets, half = full.shape[0], full.shape[0] // 2
    chip, core = numbers_ref[1], numbers_ref[0]
    numbers = lax.broadcasted_iota(jnp.int32, (buckets, CHUNK), 0)
    places = lax.broadcasted_iota(jnp.int32, (buckets, CHUNK), 1)
    total = None
    for place in range(chunks):
        hit = numbers == bucket_ref[place]
        rows = places + place * CHUNK
        mine = jnp.logical_and(rows >= chip * share, rows < (chip + 1) * share)
        every = jnp.where(hit, 1.0, 0.0).astype(BF16)
        own = jnp.where(jnp.logical_and(hit, mine), 1.0, 0.0).astype(BF16)
        first = firsts[place][...]
        high = first.astype(BF16)
        rest = (first - high.astype(F32)).astype(BF16)
        part = dot(every, joints[place][...]) + (dot(own, high) + dot(own, rest))
        total = part if total is None else total + part
    full[...] = total
    mine_ref[:half, :] = full[pl.ds(pl.multiple_of(core * half, half), half), :]
    sent_ref[:half, :] = full[pl.ds(pl.multiple_of((1 - core) * half, half), half), :].astype(BF16)
    for layer in range(LAYERS):
        rows = slice(half + 8 * layer, half + 8 * layer + 8)
        mine_ref[rows, :] = vectors[2 * layer][...]
        sent_ref[rows, :] = vectors[2 * layer + 1][...].astype(BF16)


def vectors_kernel(numbers_ref, second_ref, first_ref, unit_ref, *refs):
    mine_ref, sent_ref = refs[-2:]
    second, first, unit = second_ref[...], first_ref[...], unit_ref[...]
    bias = sum(ref[...] for ref in refs[:-2])
    units, local = unit.shape[1] // 2, bias.shape[1] // 2
    low = numbers_ref[0] == 0
    for target, lanes, flip in (
        (mine_ref, slice(0, units), False),
        (sent_ref, slice(units, 2 * units), True),
    ):
        target[0:3, :] = second[0:3, :]
        target[3:6, :] = first[0:3, :]
        target[6:7, :] = unit[:, lanes]
        target[7:8, :] = jnp.zeros_like(target[7:8, :])
        for member in range(2):
            left, right = bias[member : member + 1, :local], bias[member : member + 1, local:]
            if flip:
                left, right = right, left
            target[7:8, member * local : (member + 1) * local] = jnp.where(low, left, right)


def table_add_kernel(mine_ref, recv_ref, both_ref, sent_ref):
    total = mine_ref[...] + recv_ref[...].astype(F32)
    both_ref[...] = total
    sent_ref[...] = total[: sent_ref.shape[0], :].astype(BF16)


def pack_kernel(q_ref, both_ref, sent_ref, recv_ref, packed_ref):
    local, half, rows = q_ref.shape[0], sent_ref.shape[0], both_ref.shape[0]
    packed_ref[...] = jnp.zeros_like(packed_ref)
    packed_ref[:local, :] = q_ref[...]
    table = sent_ref[...].astype(F32) + recv_ref[...].astype(F32)
    packed_ref[local : local + half, :] = table.astype(BF16)
    packed_ref[local + half : local + rows, :] = both_ref[half:, :].astype(BF16)


def pile_kernel(*refs):
    sources, target = refs[:-1], refs[-1]
    start = 0
    for source in sources:
        rows = source.shape[0]
        target[start : start + rows, :] = source[...].astype(target.dtype)
        start += rows
    if start < target.shape[0]:
        target[start:, :] = jnp.zeros_like(target[start:, :])


def pick_rows(chip, chunk_refs, share, target):
    for number in range(2):

        @pl.when(chip == number)
        def _():
            start, end = number * share, (number + 1) * share
            for place, ref in enumerate(chunk_refs):
                low, high = max(start, place * CHUNK), min(end, (place + 1) * CHUNK)
                if low < high:
                    target[low - start : high - start, :] = ref[
                        low - place * CHUNK : high - place * CHUNK, :
                    ]


def tokens_send_kernel(numbers_ref, *refs):
    pick_rows(1 - numbers_ref[1], refs[:-1], refs[-1].shape[0], refs[-1])


def tokens_kernel(chunks, numbers_ref, *refs):
    joints, firsts = refs[:chunks], refs[chunks : 2 * chunks]
    recv_ref, target, own = refs[2 * chunks :]
    share = target.shape[0]
    pick_rows(numbers_ref[1], joints, share, own)
    pick_rows(numbers_ref[1], firsts, share, target)
    target[...] += own[...].astype(F32) + recv_ref[...].astype(F32)


class Wide:
    BITS = {"y": (2, 1), "near": (3, 2), "far": (4, 4)}
    PLACES = {("y", "near", "far"): 5, ("near", "y", "far"): 6}

    def __init__(self, size, chip, core):
        self.small, self.size = size == 8, size
        index = lax.axis_index("wide")
        bits = {name: (index >> k) & 1 for k, name in enumerate(("y", "near", "far"))}
        places = [
            sum(bits[name] << (2 - k) for k, name in enumerate(order)) if self.small else 0
            for order in self.PLACES
        ]
        self.numbers = jnp.stack(
            [
                jnp.asarray(value, jnp.int32)
                for value in (core, chip, bits["y"], bits["near"], bits["far"], *places, 0)
            ]
        )

    def pairs(self, name):
        reach = self.BITS[name][1]
        return [(number, number ^ reach) for number in range(self.size)]


def gate(value, *later):
    return lax.optimization_barrier((value,) + later)[0] if later else value


SMEM = pl.BlockSpec(memory_space=pltpu.SMEM)


class Chain:
    def __init__(self, wide, value, order):
        self.wide, self.order, self.step = wide, order, 0
        self.parts, self.rows = [value], value.shape[0]

    def advance(self, *after):
        if not self.wide.small:
            if self.step == 0:
                value = self.parts[0]
                self.parts = lax.psum(value, "wide").reshape(2, 4, -1, value.shape[1])
            self.step = 6
            self.sent = self.parts[0]
            return self.parts[0]
        self.step += 1
        parts = [(part, ON_CHIP) for part in self.parts]
        columns = self.parts[0].shape[-1]
        if self.step <= 3:
            name = self.order[self.step - 1]
            half = (self.parts[0].shape[0] // 2, columns)
            sent, kept = call(
                functools.partial(halve_kernel, Wide.BITS[name][0]),
                None,
                [(self.wide.numbers, SMEM)] + parts,
                [(half, BF16, ON_CHIP, None), (half, F32, ON_CHIP, None)],
                after=after,
            )
            self.parts = [kept, lax.ppermute(sent, "wide", self.wide.pairs(name))]
            self.sent = sent
            return sent
        kernel = add_kernel if self.step == 4 else join_kernel
        shape = self.parts[0].shape
        shape = (1,) + shape if self.step == 4 else (2 * shape[0],) + shape[1:]
        (sent,) = call(kernel, None, parts, [(shape, BF16, ON_CHIP, None)], after=after)
        name = self.order[6 - self.step]
        self.parts = [sent, lax.ppermute(sent, "wide", self.wide.pairs(name))]
        return sent

    def finish(self):
        while self.step < 6:
            self.advance()
        return [self.parts[0], self.parts[1]]


def on_device(wide, *arguments):
    (
        tokens,
        buckets,
        lengths,
        type_table,
        query_weight,
        query_bias,
        key_weight,
        value_weight,
        value_bias,
        output_weight,
        output_bias,
        attention_gain,
        attention_shift,
        up_weight,
        up_bias,
        down_weight,
        down_bias,
        feed_gain,
        feed_shift,
        cotangent,
    ) = arguments
    share, model = tokens.shape
    lane = 2 * share
    chunks = lane // CHUNK
    local = query_weight.shape[2]
    width = 2 * local
    head_count = width // HEAD_DIM
    units = up_weight.shape[2]
    place = lax.axis_index("narrow")
    chip, core = place // 2, place % 2
    first_chip, first_core = chip == 0, core == 0

    def by_core(own, other, axis):
        return jnp.where(
            first_core,
            jnp.concatenate([own, other], axis),
            jnp.concatenate([other, own], axis),
        )

    def by_chip(own, other):
        return jnp.where(
            first_chip, jnp.concatenate([own, other], 0), jnp.concatenate([other, own], 0)
        )

    def own_rows(rows):
        return jnp.where(first_chip, rows[:share], rows[share:])

    def other_rows(rows):
        return jnp.where(first_chip, rows[share:], rows[:share])

    lane_tokens = by_chip(tokens, over_chip(tokens))
    lane_buckets = by_chip(buckets, over_chip(buckets))
    lane_cotangent = by_chip(cotangent, over_chip(cotangent))

    smem = pl.BlockSpec(memory_space=pltpu.SMEM)
    sums = Wide(wide, chip, core)
    core_number = sums.numbers
    shards = []
    turned_weights = [
        jnp.swapaxes(weight, 1, 2) for weight in (query_weight, key_weight, value_weight)
    ]
    for weight in turned_weights + [output_weight]:
        shards += [(weight, ON_CHIP), (over_core(weight), ON_CHIP)]

    small = jnp.concatenate([query_bias, value_bias, up_bias], 1)
    vectors = [
        output_bias,
        attention_gain,
        attention_shift,
        down_bias,
        feed_gain,
        feed_shift,
        small,
        over_core(small),
    ]
    qw, kvw, ow, vec, q_bias, kv_bias, unit_bias = call(
        weights_kernel,
        None,
        [(core_number, smem)] + shards + [(vector, ON_CHIP) for vector in vectors],
        [
            (shape, dtype, ON_CHIP, None)
            for shape, dtype in (
                ((LAYERS, width, model), BF16),
                ((LAYERS, 2 * width, model), BF16),
                ((LAYERS, width, model), BF16),
                ((LAYERS, 8, model), F32),
                ((LAYERS, 1, width), F32),
                ((LAYERS, 1, 2 * width), F32),
                ((LAYERS, 1, 2 * units), F32),
            )
        ],
    )
    up_other = over_core(up_weight)
    down_other = over_core(down_weight)

    ends = jnp.cumsum(lengths[0], dtype=jnp.int32)
    offsets = lax.iota(jnp.int32, share)
    spots = jnp.concatenate(
        [
            offsets + (block * 2 + which) * share
            for which in (core, 1 - core)
            for block in range(2)
        ]
    )
    labels = jnp.sum((spots[:, None] >= ends[None, :]).astype(jnp.int32), 1, dtype=jnp.int32)
    tiles = 2 * chunks
    tile_labels = labels.reshape(tiles, CHUNK)
    present = jnp.any(
        tile_labels[:, :, None] == lax.iota(jnp.int32, lengths.shape[1])[None, None, :], axis=1
    )
    bits = jnp.sum(
        jnp.where(present, jnp.left_shift(1, lax.iota(jnp.int32, lengths.shape[1]))[None, :], 0),
        axis=1,
        dtype=jnp.int32,
    )
    bits = jnp.concatenate([bits, bits[:chunks]])
    k_labels = tile_labels[:, :, None]
    q_labels = tile_labels[:chunks, None, :]

    block = (CHUNK, model)

    def layer_spec(layer, shape):
        return pl.BlockSpec((1,) + shape, lambda *ids: (layer,) + (0,) * len(shape))

    selector = (lane_buckets[:, None] == lax.iota(jnp.int32, type_table.shape[0])[None, :]).astype(
        BF16
    )
    stream = lane_tokens.astype(F32) + dot(selector, type_table)
    low_first = stream.astype(BF16)
    state = [stream[CHUNK * i : CHUNK * (i + 1)] for i in range(chunks)]
    kept = []
    for layer in range(LAYERS):
        keep = {}
        if layer == 0:
            kv = (dot(low_first, kvw[0], 1, 1) + kv_bias[0]).astype(BF16)
            queries = ((dot(low_first, qw[0], 1, 1) + q_bias[0]) * HEAD_DIM**-0.5).astype(BF16)
            low_in, kv, queries = (
                [value[CHUNK * i : CHUNK * (i + 1)] for i in range(chunks)]
                for value in (low_first, kv, queries)
            )
            kv_other = [over_core(part) for part in kv]
        else:
            low_in, queries, kv, kv_other = [], [], [], []
            units_now, inverses = [], []
            for i in range(chunks):
                outs = call(
                    functools.partial(project_kernel, layer, i),
                    None,
                    [
                        (value, ON_CHIP)
                        for value in (
                            state[i],
                            feed_share[i],
                            feed_recv[i],
                            vec,
                            qw,
                            kvw,
                            q_bias,
                            kv_bias,
                        )
                    ],
                    [
                        (block, F32, ON_CHIP, None),
                        ((CHUNK, 1), F32, ON_CHIP, None),
                        (block, BF16, ON_CHIP, None),
                        ((CHUNK, width), BF16, ON_CHIP, None),
                        ((CHUNK, 2 * width), BF16, ON_CHIP, None),
                    ],
                    cost=2,
                )
                units_now.append(outs[0])
                inverses.append(outs[1])
                low_in.append(outs[2])
                queries.append(outs[3])
                kv.append(outs[4])
                kv_other.append(over_core(outs[4]))
            state = units_now
            kept[layer - 1]["second_unit"] = units_now
            kept[layer - 1]["second_inverse"] = inverses
        kv_all, turned = call(
            gather_kernel,
            None,
            [(part, ON_CHIP) for part in kv + kv_other],
            [
                ((tiles, CHUNK, 2 * width), BF16, ON_CHIP, None),
                ((tiles, 2 * width, CHUNK), BF16, ON_CHIP, None),
            ],
            cost=2,
        )
        context, exact, logsum, shares = [], [], [], []
        for i in range(chunks):
            outs = call(
                functools.partial(attend_kernel, head_count, layer, i),
                None,
                [(bits, smem)]
                + [
                    (value, ON_CHIP)
                    for value in (queries[i], kv_all, turned, q_labels, k_labels, ow)
                ],
                [
                    ((CHUNK, width), BF16, ON_CHIP, None),
                    ((CHUNK, width), F32, ON_CHIP, None),
                    ((8, CHUNK), F32, ON_CHIP, None),
                    (block, BF16, ON_CHIP, None),
                ],
                scratch=[
                    pltpu.VMEM((head_count, CHUNK, 128), BF16),
                    pltpu.VMEM((width, CHUNK), F32),
                    pltpu.VMEM((head_count, 8, CHUNK), F32),
                    pltpu.VMEM((head_count, 8, CHUNK), F32),
                    pltpu.VMEM((head_count, tiles, CHUNK, CHUNK), F32),
                ],
                cost=6,
                limit=20,
            )
            for target, value in zip((context, exact, logsum, shares), outs):
                target.append(value)
        received = [over_chip(part) for part in shares]
        low_middle, act, slope, first_unit, first_inverse, feed_share = [], [], [], [], [], []
        for i in range(chunks):
            outs = call(
                functools.partial(feed_kernel, layer, i),
                None,
                [
                    (value, ON_CHIP)
                    for value in (
                        state[i],
                        shares[i],
                        received[i],
                        vec,
                        up_weight,
                        up_other,
                        unit_bias,
                        down_weight,
                        down_other,
                    )
                ],
                [
                    (block, F32, ON_CHIP, None),
                    ((CHUNK, 1), F32, ON_CHIP, None),
                    (block, BF16, ON_CHIP, None),
                    ((CHUNK, 2 * units), BF16, ON_CHIP, None),
                    ((CHUNK, 2 * units), BF16, ON_CHIP, None),
                    (block, BF16, ON_CHIP, None),
                ],
                cost=8,
            )
            for target, value in zip(
                (first_unit, first_inverse, low_middle, act, slope, feed_share), outs
            ):
                target.append(value)
        feed_recv = [over_chip(part) for part in feed_share]
        state = first_unit
        keep.update(
            low_in=low_in,
            queries=queries,
            kv_all=kv_all,
            turned=turned,
            context=context,
            exact=exact,
            logsum=logsum,
            first_unit=first_unit,
            first_inverse=first_inverse,
            low_middle=low_middle,
            act=act,
            slope=slope,
        )
        kept.append(keep)

    pair_order, other_order = ("y", "near", "far"), ("near", "y", "far")

    def unpacked(kernel, layer, sources, shapes, buffers, scratch=(), after=()):
        return call(
            kernel,
            (1,),
            [(source, smem if source is sums.numbers else whole(source.shape)) for source in sources],
            [
                ((LAYERS,) + shape, F32, layer_spec(layer, shape), buffer)
                for shape, buffer in zip(shapes, buffers)
            ],
            scratch,
            after=after,
        )

    def unpacked_rows(layer, chain, shapes, buffers, after=()):
        return unpacked(
            functools.partial(unpack_kernel, Wide.PLACES[chain.order]),
            layer,
            [sums.numbers] + chain.finish(),
            shapes,
            buffers,
            [pltpu.VMEM((chain.rows, model), F32)],
            after,
        )

    def piled(rows, *values):
        return call(
            pile_kernel,
            None,
            [(value, ON_CHIP) for value in values],
            [((rows, model), BF16, ON_CHIP, None)],
        )[0]

    vector_sums = [None] * LAYERS
    encoded = []
    for layer in reversed(range(LAYERS)):
        keep = kept[layer]
        top_layer = layer == LAYERS - 1
        second, low_second, up_grad, unit_sums, second_sums, parts = [], [], [], [], [], []
        for i in range(chunks):
            if top_layer:
                upstream = lane_cotangent
                unit = keep["first_unit"][i]
                inverse = keep["first_inverse"][i]
                added = (feed_share[i], feed_recv[i])
            else:
                upstream = first_total[i]
                unit = keep["second_unit"][i]
                inverse = keep["second_inverse"][i]
                added = (joint_share[i], joint_recv[i])
            outs = call(
                functools.partial(feed_back_kernel, layer, i, top_layer),
                None,
                [
                    (value, ON_CHIP)
                    for value in (
                        upstream,
                        unit,
                        inverse,
                        added[0],
                        added[1],
                        vec,
                        keep["slope"][i],
                        up_weight,
                        up_other,
                        down_weight,
                        down_other,
                        *second_sums[-1:],
                        *unit_sums[-1:],
                    )
                ],
                [
                    (block if top_layer else (8, 128), BF16, ON_CHIP, None),
                    (block, F32, ON_CHIP, None),
                    (block, BF16, ON_CHIP, None),
                    ((CHUNK, 2 * units), BF16, ON_CHIP, None),
                    ((1, 2 * units), F32, ON_CHIP, None),
                    ((8, model), F32, ON_CHIP, None),
                    (block, BF16, ON_CHIP, None),
                ],
                cost=0,
                after=(
                    []
                    if top_layer or i == 1
                    else [upper.advance(), feed_chain.advance(joint_share[2]), vector_sums[1][0]]
                    if i == 0
                    else []
                ),
            )
            if top_layer:
                encoded.append(outs[0])
            for target, value in zip(
                (second, low_second, up_grad, unit_sums, second_sums, parts), outs[1:]
            ):
                target.append(value)
        received = [over_chip(part) for part in parts]

        def weight_grad(lefts, rights, shape, left_start=0, right_start=0, received=()):
            return call(
                functools.partial(weight_grad_kernel, chunks, left_start, right_start),
                None,
                [(value, ON_CHIP) for value in [*lefts, *rights, *received]],
                [(shape, BF16, ON_CHIP, None)],
                cost=0,
            )[0]

        square = (model, units)
        down_other_grad = over_core(
            weight_grad(keep["act"], low_second, square[::-1], left_start=units)
        )
        up_other_grad = over_core(
            weight_grad(keep["low_middle"], up_grad, square, right_start=units)
        )
        down_grad = weight_grad(
            keep["act"], low_second, square[::-1], received=[down_other_grad]
        )
        up_weight_grad = weight_grad(
            keep["low_middle"], up_grad, square, received=[up_other_grad]
        )
        first_total, low_total, context_grad, first_sums = [], [], [], []
        for i in range(chunks):
            outs = call(
                functools.partial(context_back_kernel, layer, i),
                None,
                [
                    (value, ON_CHIP)
                    for value in (
                        second[i],
                        parts[i],
                        received[i],
                        keep["first_unit"][i],
                        keep["first_inverse"][i],
                        vec,
                        ow,
                        *first_sums[-1:],
                    )
                ],
                [
                    (block, F32, ON_CHIP, None),
                    (block, BF16, ON_CHIP, None),
                    ((CHUNK, width), BF16, ON_CHIP, None),
                    ((8, model), F32, ON_CHIP, None),
                ],
                after=(
                    []
                    if top_layer or i != 1
                    else [upper.advance(second_sums[2]), feed_chain.advance(second_sums[2])]
                ),
            )
            for target, value in zip((first_total, low_total, context_grad, first_sums), outs):
                target.append(value)
        own, other = call(
            functools.partial(out_grad_kernel, chunks),
            None,
            [(core_number, smem)]
            + [(value, ON_CHIP) for value in keep["context"] + low_total],
            [((local, model), F32, ON_CHIP, None), ((local, model), BF16, ON_CHIP, None)],
            scratch=[pltpu.VMEM((width, model), F32)],
        )
        out_grad = (own + over_core(other).astype(F32)).astype(BF16)
        pending = [out_grad, up_weight_grad, down_grad]
        if top_layer:
            feed_chain = Chain(sums, piled(2 * units, up_weight_grad, down_grad), pair_order)
            pending = [out_grad, feed_chain.advance()]
        else:
            strands = [
                Chain(sums, up_weight_grad, pair_order),
                Chain(sums, down_grad, other_order),
            ]
            pending = [
                out_grad,
                upper.advance(first_sums[2]),
                feed_chain.advance(first_sums[2]),
                *[strand.advance() for strand in strands],
            ]
        half_shape = (chunks, CHUNK, 256)
        q_grads, kv_owns, kv_recvs = [], [], []
        for pair in range(head_count // 2):
            q_grad, kv_grad, kv_grad_other = call(
                functools.partial(attend_back_kernel, pair, head_count, chunks),
                None,
                [(bits, smem)]
                + [
                    (value, ON_CHIP)
                    for value in [keep["kv_all"], keep["turned"], q_labels, k_labels]
                    + keep["queries"]
                    + context_grad
                    + keep["exact"]
                    + keep["logsum"]
                ],
                [
                    ((lane, 128), BF16, ON_CHIP, None),
                    (half_shape, F32, ON_CHIP, None),
                    (half_shape, BF16, ON_CHIP, None),
                ],
                scratch=[
                    pltpu.VMEM((2, CHUNK, 128), BF16),
                    pltpu.VMEM((2, CHUNK, 128), BF16),
                    pltpu.VMEM((8, CHUNK), F32),
                    pltpu.VMEM((128, CHUNK), F32),
                    pltpu.VMEM((tiles, CHUNK, 256), F32),
                ],
                cost=0,
                limit=16,
                after=pending + q_grads[-1:],
            )
            pending = []
            if not top_layer:
                pending = [upper.advance(q_grad)]
                if pair == 0:
                    pending.append(feed_chain.advance(q_grad))
                if pair == 2:
                    up_out, down_out = unpacked_rows(
                        1, feed_chain, [square, square[::-1]], [None] * 2, after=[q_grad]
                    )
                    pending.append(up_out)
                if pair > 0:
                    pending += [strand.advance(q_grad) for strand in strands]
            elif pair == 2:
                pending = [feed_chain.advance(q_grad)]
            q_grads.append(q_grad)
            kv_owns.append(kv_grad)
            kv_recvs.append(over_core(gate(kv_grad_other, *pending)))
        joint_own, joint_other, bias_sums, joint_share = [], [], [], []
        for i in range(chunks):
            outs = call(
                functools.partial(joint_back_kernel, layer, i),
                None,
                [(core_number, smem)]
                + [(value, ON_CHIP) for value in q_grads + kv_owns + kv_recvs + [qw, kvw]],
                [
                    ((CHUNK, 3 * local), BF16, ON_CHIP, None),
                    ((CHUNK, 3 * local), BF16, ON_CHIP, None),
                    ((8, width), F32, ON_CHIP, None),
                    (block, BF16, ON_CHIP, None),
                ],
                cost=0,
            )
            for target, value in zip((joint_own, joint_other, bias_sums, joint_share), outs):
                target.append(value)
        vector_sums[layer] = call(
            vectors_kernel,
            None,
            [(sums.numbers, smem)]
            + [(value, ON_CHIP) for value in second_sums[-1:] + first_sums[-1:] + unit_sums[-1:] + bias_sums],
            [((8, model), F32, ON_CHIP, None), ((8, model), F32, ON_CHIP, None)],
        )
        if layer > 0:
            joint_recv = [over_chip(part) for part in joint_share]
        joint_other_grad = weight_grad(joint_other, keep["low_in"], (3 * local, model))
        if layer == 0:
            buckets_total = type_table.shape[0]
            half_table = buckets_total // 2
            table_mine, table_sent = call(
                functools.partial(table_kernel, chunks, share),
                None,
                [
                    (value, smem if value is sums.numbers else ON_CHIP)
                    for value in [sums.numbers, lane_buckets.reshape(chunks, 1, CHUNK)]
                    + joint_share
                    + first_total
                    + [*vector_sums[0], *vector_sums[1]]
                ],
                [
                    ((half_table + 16, model), F32, ON_CHIP, None),
                    ((half_table + 16, model), BF16, ON_CHIP, None),
                ],
                scratch=[pltpu.VMEM((buckets_total, model), F32)],
                cost=0,
                after=[joint_other_grad],
            )
            table_recv = over_core(table_sent)
        joint_recv_grad = over_core(joint_other_grad)
        if layer == 0:
            table_both, table_low = call(
                table_add_kernel,
                None,
                [(table_mine, ON_CHIP), (table_recv, ON_CHIP)],
                [
                    ((half_table + 16, model), F32, ON_CHIP, None),
                    ((half_table, model), BF16, ON_CHIP, None),
                ],
            )
        joint_grad = weight_grad(
            joint_own, keep["low_in"], (3 * local, model), received=[joint_recv_grad]
        )
        flat = [(local, model)] * 4
        if layer > 0:
            upper = Chain(sums, piled(4 * local, joint_grad, out_grad), other_order)

    second_chain = Chain(
        sums, piled(10 * half_table // 2, joint_grad[local:], out_grad), other_order
    )
    second_sent = second_chain.advance()
    table_other = over_chip(table_low)
    (tokens_sent,) = call(
        tokens_send_kernel,
        None,
        [(sums.numbers, smem)] + [(part, ON_CHIP) for part in joint_share],
        [((share, model), BF16, ON_CHIP, None)],
        after=[table_low],
    )
    tokens_recv = over_chip(tokens_sent)
    (packed,) = call(
        pack_kernel,
        None,
        [(value, ON_CHIP) for value in (joint_grad[:local], table_both, table_low, table_other)],
        [((3 * half_table, model), BF16, ON_CHIP, None)],
    )
    first_chain = Chain(sums, packed, pair_order)
    token = first_chain.advance()
    for step in range(5):
        for strand in strands:
            if strand.step < 6:
                token = strand.advance(token)
        token = second_chain.advance(token)
        if upper.step < 6:
            token = upper.advance(token)
        token = first_chain.advance(token)
        if step == 0:
            turned_out = unpacked_rows(1, upper, flat, [None] * 4, after=[token])
            token = strands[0].advance(turned_out[0])
        if step == 3:
            (tokens_grad,) = call(
                functools.partial(tokens_kernel, chunks),
                (1,),
                [(sums.numbers, smem)]
                + [
                    (value, whole(value.shape))
                    for value in joint_share + first_total + [tokens_recv]
                ],
                [((share, model), F32, whole((share, model)), None)],
                scratch=[pltpu.VMEM((share, model), BF16)],
                after=[token],
            )
        if step == 4:
            (up_out,) = unpacked_rows(0, strands[0], [square], [up_out], after=[token])
            (down_out,) = unpacked_rows(0, strands[1], [square[::-1]], [down_out])
    k_out, v_out, o_out = unpacked_rows(0, second_chain, flat[:3], turned_out[1:])
    shapes = [(LAYERS, model)] * 7 + [(LAYERS, local)] * 2
    q_out, table_half, *vector_out = call(
        functools.partial(vectors_unpack_kernel, Wide.PLACES[pair_order]),
        (1,),
        [(sums.numbers, smem)] + [(value, whole(value.shape)) for value in first_chain.finish()],
        [
            ((LAYERS, local, model), F32, layer_spec(0, (local, model)), turned_out[0]),
            ((half_table, model), BF16, whole((half_table, model)), None),
        ]
        + [(shape, F32, whole(shape), None) for shape in shapes],
        scratch=[pltpu.VMEM((first_chain.rows, model), F32)],
    )
    table_grad = by_core(table_half, over_core(table_half), 0).astype(F32)

    return (
        own_rows(jnp.concatenate(encoded, 0)),
        tokens_grad,
        table_grad,
        jnp.swapaxes(q_out, 1, 2),
        vector_out[7],
        jnp.swapaxes(k_out, 1, 2),
        jnp.swapaxes(v_out, 1, 2),
        vector_out[8],
        o_out,
        vector_out[5],
        vector_out[3],
        vector_out[4],
        up_out,
        vector_out[6],
        down_out,
        vector_out[2],
        vector_out[0],
        vector_out[1],
    )


def solution(mesh):
    rows = P(("wide", "narrow"), None)
    third = P(None, None, "narrow")
    second = P(None, "narrow")
    middle = P(None, "narrow", None)
    in_specs = (
        rows,
        P(("wide", "narrow")),
        P("wide", None),
        P(),
        third,
        second,
        third,
        third,
        second,
        middle,
        P(),
        P(),
        P(),
        third,
        second,
        middle,
        P(),
        P(),
        P(),
        rows,
    )
    out_specs = (
        rows,
        rows,
        P(),
        third,
        second,
        third,
        third,
        second,
        middle,
        P(),
        P(),
        P(),
        third,
        second,
        middle,
        P(),
        P(),
        P(),
    )
    return jax.shard_map(
        functools.partial(on_device, mesh.shape["wide"]),
        mesh=mesh,
        in_specs=in_specs,
        out_specs=out_specs,
        check_vma=False,
    )
```

```python
import functools

import jax
import jax.numpy as jnp
from jax import lax
from jax.experimental import pallas as pl
from jax.experimental.pallas import tpu as pltpu
from jax.sharding import PartitionSpec as P

HEAD_DIM = 64
LAYERS = 2
CHUNK = 256
EPS = 1e-12
ROOT_HALF = 0.7071067811865476
DENSITY = 0.3989422804014327
NEG = -1e30
F32 = jnp.float32
BF16 = jnp.bfloat16
MIB = 1 << 20
CORE_SWAP = [(0, 1), (1, 0), (2, 3), (3, 2)]
CHIP_SWAP = [(0, 2), (2, 0), (1, 3), (3, 1)]


def over_core(value):
    return lax.ppermute(value, "narrow", CORE_SWAP)


def over_chip(value):
    return lax.ppermute(value, "narrow", CHIP_SWAP)


def dot(left, right, left_axis=1, right_axis=0):
    return lax.dot_general(
        left, right, (((left_axis,), (right_axis,)), ((), ())), preferred_element_type=F32
    )


def norm_parts(summed):
    row_mean = jnp.mean(summed, -1, keepdims=True)
    centred = summed - row_mean
    spread = jnp.mean(centred * centred, -1, keepdims=True)
    inverse = lax.rsqrt(spread + EPS)
    return centred * inverse, inverse


def norm_back(upstream, unit_rows, inverse, gain_row):
    scaled = upstream * gain_row
    return inverse * (
        scaled
        - jnp.mean(scaled, -1, keepdims=True)
        - unit_rows * jnp.mean(scaled * unit_rows, -1, keepdims=True)
    )


def gelu_parts(preact):
    size = jnp.abs(preact) * ROOT_HALF
    bell = jnp.exp(-(size * size))
    step = 1.0 / (1.0 + 0.3275911 * size)
    series = step * (
        0.254829592
        + step * (-0.284496736 + step * (1.421413741 + step * (-1.453152027 + step * 1.061405429)))
    )
    tail = 0.5 * series * bell
    cdf = jnp.where(preact >= 0.0, 1.0 - tail, tail)
    return preact * cdf, cdf + preact * DENSITY * bell


ON_CHIP = pl.BlockSpec(memory_space=pltpu.VMEM)


def whole(shape):
    zeros = (0,) * len(shape)
    return pl.BlockSpec(shape, lambda *ids: zeros)


def call(kernel, grid, inputs, outputs, scratch=(), cost=0, limit=16, after=()):
    arrays = [array for array, spec in inputs]
    specs = [spec for array, spec in inputs]
    aliases = {}
    for place, (shape, dtype, spec, buffer) in enumerate(outputs):
        if buffer is not None:
            aliases[len(arrays)] = place
            arrays.append(buffer)
            specs.append(pl.BlockSpec(memory_space=pl.ANY))
    for array in after:
        arrays.append(array)
        specs.append(pl.BlockSpec(memory_space=pl.ANY))
    given, extra = len(inputs), len(aliases) + len(after)

    def body(*refs):
        kernel(*refs[:given], *refs[given + extra :])

    return pl.pallas_call(
        body,
        **({} if grid is None else {"grid": grid}),
        in_specs=specs,
        out_specs=[spec for shape, dtype, spec, buffer in outputs],
        out_shape=[
            jax.ShapeDtypeStruct(shape, dtype) for shape, dtype, spec, buffer in outputs
        ],
        scratch_shapes=list(scratch),
        input_output_aliases=aliases,
        compiler_params=pltpu.CompilerParams(vmem_limit_bytes=limit * MIB),
        cost_estimate=pl.CostEstimate(flops=cost * 4000000000, bytes_accessed=1, transcendentals=0),
    )(*arrays)


def gather_kernel(*refs):
    sources, (rows_ref, turned_ref) = refs[:-2], refs[-2:]
    for place, source in enumerate(sources):
        tile = source[...]
        rows_ref[place] = tile
        turned_ref[place] = tile.astype(F32).T.astype(BF16)


def split_pairs(pair_block, target, head_count):
    lanes = lax.broadcasted_iota(jnp.int32, (CHUNK, 2 * HEAD_DIM), 1)
    low_half = lanes < HEAD_DIM
    for head in range(head_count):
        pair = pair_block[:, (head // 2) * 128 : (head // 2) * 128 + 128]
        keep = low_half if head % 2 == 0 else jnp.logical_not(low_half)
        target[head * CHUNK : (head + 1) * CHUNK, :] = jnp.where(keep, pair, jnp.zeros_like(pair))


def attend_kernel(
    head_count,
    layer,
    place,
    bits_ref,
    q_ref,
    kv_ref,
    turned_ref,
    q_label_ref,
    k_label_ref,
    out_weight_ref,
    context_ref,
    exact_ref,
    logsum_ref,
    share_ref,
    masked_q,
    total,
    top,
    mass,
    score_tiles,
):
    width = head_count * HEAD_DIM
    split_pairs(q_ref[...], masked_q, head_count)
    top[...] = jnp.full_like(top, NEG)
    mass[...] = jnp.zeros_like(mass)
    total[...] = jnp.zeros_like(total)
    tiles = kv_ref.shape[0]
    q_bits = bits_ref[tiles + place]

    def score_tile(tile, carry):
        @pl.when((bits_ref[tile] & q_bits) != 0)
        def _():
            hide = jnp.where(k_label_ref[tile] == q_label_ref[place], 0.0, NEG)
            hide = jnp.concatenate([hide, hide], 1)
            for pair in range(head_count // 2):
                lanes = slice(pair * 128, pair * 128 + 128)
                rows = slice(2 * pair * CHUNK, 2 * (pair + 1) * CHUNK)
                scores = dot(kv_ref[tile, :, lanes], masked_q[rows, :], 1, 1) + hide
                score_tiles[pair, tile] = scores
                highest = jnp.max(scores.reshape(-1, 8, 2 * CHUNK), 0)
                top[pair] = jnp.maximum(top[pair], highest)

        return carry

    lax.fori_loop(0, tiles, score_tile, 0)
    for pair in range(head_count // 2):
        top[pair] = jnp.broadcast_to(jnp.max(top[pair], 0, keepdims=True), (8, 2 * CHUNK))

    def weigh_tile(tile, carry):
        @pl.when((bits_ref[tile] & q_bits) != 0)
        def _():
            for pair in range(head_count // 2):
                weights = jnp.exp(score_tiles[pair, tile] - top[pair, 0:1, :])
                mass[pair] += jnp.sum(weights.reshape(-1, 8, 2 * CHUNK), 0)
                low = weights.astype(BF16)
                for side in range(2):
                    start = (2 * pair + side) * HEAD_DIM
                    total[start : start + HEAD_DIM, :] += dot(
                        turned_ref[tile, width + start : width + start + HEAD_DIM, :],
                        low[:, side * CHUNK : (side + 1) * CHUNK],
                    )

        return carry

    lax.fori_loop(0, tiles, weigh_tile, 0)
    logsum_ref[...] = jnp.zeros_like(logsum_ref)
    for head in range(head_count):
        rows = slice(head * HEAD_DIM, (head + 1) * HEAD_DIM)
        lanes = slice((head % 2) * CHUNK, (head % 2 + 1) * CHUNK)
        amount = jnp.sum(mass[head // 2][:, lanes], 0, keepdims=True)
        total[rows, :] = total[rows, :] / amount
        logsum_ref[head : head + 1, :] = top[head // 2, 0:1, lanes] + jnp.log(amount)
    exact = total[...].T
    exact_ref[...] = exact
    context = exact.astype(BF16)
    context_ref[...] = context
    share_ref[...] = dot(context, out_weight_ref[layer]).astype(BF16)


def attend_back_kernel(pair, head_count, chunks, *refs):
    bits_ref, kv_ref, turned_ref, q_label_ref, k_label_ref = refs[:5]
    q_refs, grad_refs, exact_refs, logsum_refs = (
        refs[5 + chunks * k : 5 + chunks * (k + 1)] for k in range(4)
    )
    q_grad_ref, own_ref, other_ref, masked_q, masked_grad, centre, q_total, kv_total = refs[
        5 + 4 * chunks :
    ]
    tiles = kv_ref.shape[0]
    lanes = slice(pair * 128, pair * 128 + 128)
    v_lanes = slice(head_count * HEAD_DIM + pair * 128, head_count * HEAD_DIM + pair * 128 + 128)
    kv_total[...] = jnp.zeros_like(kv_total)
    for place in range(chunks):
        split_pairs(q_refs[place][:, lanes], masked_q, 2)
        split_pairs(grad_refs[place][:, lanes], masked_grad, 2)
        crossed = (grad_refs[place][:, lanes].astype(F32) * exact_refs[place][:, lanes]).T
        for head in range(2):
            rows = slice(head * HEAD_DIM, (head + 1) * HEAD_DIM)
            side = slice(head * CHUNK, (head + 1) * CHUNK)
            number = 2 * pair + head
            centre[0:1, side] = jnp.sum(crossed[rows, :], 0, keepdims=True)
            centre[2:3, side] = logsum_refs[place][number : number + 1, :]
        q_total[...] = jnp.zeros_like(q_total)
        q_bits = bits_ref[tiles + place]

        def one_tile(tile, carry):
            @pl.when((bits_ref[tile] & q_bits) != 0)
            def _():
                hide = jnp.where(k_label_ref[tile] == q_label_ref[place], 0.0, NEG)
                hide = jnp.concatenate([hide, hide], 1)
                scores = dot(kv_ref[tile, :, lanes], masked_q[...], 1, 1) + hide
                weight_grad = dot(kv_ref[tile, :, v_lanes], masked_grad[...], 1, 1)
                weights = jnp.exp(scores - centre[2:3, :])
                score_grad = (weights * (weight_grad - centre[0:1, :])).astype(BF16)
                kv_total[tile, :, 128:] += dot(weights.astype(BF16), masked_grad[...])
                kv_total[tile, :, :128] += dot(score_grad, masked_q[...])
                for side in range(2):
                    rows = slice(side * HEAD_DIM, (side + 1) * HEAD_DIM)
                    turned = slice((2 * pair + side) * HEAD_DIM, (2 * pair + side + 1) * HEAD_DIM)
                    q_total[rows, :] += dot(
                        turned_ref[tile, turned, :],
                        score_grad[:, side * CHUNK : (side + 1) * CHUNK],
                    )

            return carry

        lax.fori_loop(0, tiles, one_tile, 0)
        q_grad_ref[place * CHUNK : (place + 1) * CHUNK, :] = q_total[...].T.astype(
            BF16
        ) * jnp.asarray(HEAD_DIM**-0.5, BF16)
    own_ref[...] = kv_total[: tiles // 2]
    other_ref[...] = kv_total[tiles // 2 :].astype(BF16)


def weight_grad_kernel(chunks, left_start, right_start, *refs):
    lefts, rights, recv_refs = refs[:chunks], refs[chunks : 2 * chunks], refs[2 * chunks : -1]
    out_ref = refs[-1]
    rows, columns = out_ref.shape
    step = CHUNK if rows % CHUNK == 0 else rows
    for start in range(0, rows, step):
        left_lanes = slice(left_start + start, left_start + start + step)
        right_lanes = slice(right_start, right_start + columns)
        total = None
        for left, right in zip(lefts, rights):
            part = dot(left[:, left_lanes], right[:, right_lanes], 0, 0)
            total = part if total is None else total + part
        for recv_ref in recv_refs:
            total = total + recv_ref[start : start + step, :].astype(F32)
        out_ref[start : start + step, :] = total.astype(out_ref.dtype)


def out_grad_kernel(chunks, core_ref, *refs):
    lefts, rights, (own_ref, other_ref, full) = refs[:chunks], refs[chunks:-3], refs[-3:]
    total = None
    for left, right in zip(lefts, rights):
        part = dot(left[...], right[...], 0, 0)
        total = part if total is None else total + part
    full[...] = total
    local = own_ref.shape[0]
    own_ref[...] = full[pl.ds(pl.multiple_of(core_ref[0] * local, local), local), :]
    other_ref[...] = full[pl.ds(pl.multiple_of((1 - core_ref[0]) * local, local), local), :].astype(
        BF16
    )


def feed_kernel(
    layer,
    place,
    unit_ref,
    share_ref,
    recv_ref,
    vec_ref,
    up_own_ref,
    up_other_ref,
    bias_ref,
    down_own_ref,
    down_other_ref,
    new_unit_ref,
    inverse_ref,
    low_ref,
    act_ref,
    slope_ref,
    part_ref,
):
    stream = unit_ref[...] * vec_ref[layer, 6:7, :] + vec_ref[layer, 7:8, :]
    attention = share_ref[...].astype(F32) + recv_ref[...].astype(F32)
    unit, inverse = norm_parts(stream + attention + vec_ref[layer, 0:1, :])
    new_unit_ref[...] = unit
    inverse_ref[...] = inverse
    low_ref[...] = (unit * vec_ref[layer, 1:2, :] + vec_ref[layer, 2:3, :]).astype(BF16)
    units = up_own_ref.shape[2]
    total = None
    for half, (up_ref, down_ref) in enumerate(
        ((up_own_ref, down_own_ref), (up_other_ref, down_other_ref))
    ):
        lanes = slice(half * units, (half + 1) * units)
        act, slope = gelu_parts(dot(low_ref[...], up_ref[layer]) + bias_ref[layer, :, lanes])
        low_act = act.astype(BF16)
        act_ref[:, lanes] = low_act
        slope_ref[:, lanes] = slope.astype(BF16)
        part = dot(low_act, down_ref[layer])
        total = part if total is None else total + part
    part_ref[...] = total.astype(BF16)


def project_kernel(
    layer,
    place,
    unit_ref,
    share_ref,
    recv_ref,
    vec_ref,
    q_weight_ref,
    kv_weight_ref,
    q_bias_ref,
    kv_bias_ref,
    new_unit_ref,
    inverse_ref,
    low_ref,
    q_ref,
    kv_ref,
):
    old = layer - 1
    middle = unit_ref[...] * vec_ref[old, 1:2, :] + vec_ref[old, 2:3, :]
    feed = share_ref[...].astype(F32) + recv_ref[...].astype(F32)
    unit, inverse = norm_parts(middle + feed + vec_ref[old, 3:4, :])
    new_unit_ref[...] = unit
    inverse_ref[...] = inverse
    low = (unit * vec_ref[old, 4:5, :] + vec_ref[old, 5:6, :]).astype(BF16)
    low_ref[...] = low
    kv_ref[...] = (dot(low, kv_weight_ref[layer], 1, 1) + kv_bias_ref[layer]).astype(BF16)
    q_ref[...] = (
        (dot(low, q_weight_ref[layer], 1, 1) + q_bias_ref[layer]) * HEAD_DIM**-0.5
    ).astype(BF16)


def feed_back_kernel(
    layer,
    place,
    top_layer,
    up_ref,
    unit_ref,
    inverse_ref,
    share_ref,
    recv_ref,
    vec_ref,
    slope_ref,
    up_own_ref,
    up_other_ref,
    down_own_ref,
    down_other_ref,
    *rest,
):
    before = rest[:-7]
    encoded_ref, total_ref, low_ref, grad_ref, bias_ref, sums_ref, part_ref = rest[-7:]
    keep_span = slice(place * CHUNK, (place + 1) * CHUNK)
    added = share_ref[...].astype(F32) + recv_ref[...].astype(F32)
    if top_layer:
        middle = unit_ref[...] * vec_ref[layer, 1:2, :] + vec_ref[layer, 2:3, :]
        unit, inverse = norm_parts(middle + added + vec_ref[layer, 3:4, :])
        encoded_ref[...] = (unit * vec_ref[layer, 4:5, :] + vec_ref[layer, 5:6, :]).astype(BF16)
        upstream = up_ref[keep_span, :].astype(F32)
    else:
        unit = unit_ref[...]
        inverse = inverse_ref[...]
        upstream = up_ref[...] + added
        encoded_ref[...] = jnp.zeros_like(encoded_ref)
    second = norm_back(upstream, unit, inverse, vec_ref[layer, 4:5, :])
    sums_ref[...] = before[0][...] if before else jnp.zeros_like(sums_ref)
    sums_ref[0:1, :] += jnp.sum(upstream * unit, 0, keepdims=True)
    sums_ref[1:2, :] += jnp.sum(upstream, 0, keepdims=True)
    sums_ref[2:3, :] += jnp.sum(second, 0, keepdims=True)
    total_ref[...] = second
    low_ref[...] = second.astype(BF16)
    units = up_own_ref.shape[2]
    total = None
    for half, (up_weight_ref, down_ref) in enumerate(
        ((up_own_ref, down_own_ref), (up_other_ref, down_other_ref))
    ):
        lanes = slice(half * units, (half + 1) * units)
        grad = (
            dot(low_ref[...], down_ref[layer], 1, 1) * slope_ref[:, lanes].astype(F32)
        ).astype(BF16)
        grad_ref[:, lanes] = grad
        bias = jnp.sum(grad.astype(F32), 0, keepdims=True)
        bias_ref[:, lanes] = bias + before[1][:, lanes] if before else bias
        part = dot(grad, up_weight_ref[layer], 1, 1)
        total = part if total is None else total + part
    part_ref[...] = total.astype(BF16)


def context_back_kernel(
    layer,
    place,
    second_ref,
    share_ref,
    recv_ref,
    unit_ref,
    inverse_ref,
    vec_ref,
    out_weight_ref,
    *rest,
):
    before = rest[:-4]
    total_ref, low_ref, grad_ref, sums_ref = rest[-4:]
    added = share_ref[...].astype(F32) + recv_ref[...].astype(F32)
    upstream = second_ref[...] + added
    unit = unit_ref[...]
    first = norm_back(upstream, unit, inverse_ref[...], vec_ref[layer, 1:2, :])
    sums_ref[...] = before[0][...] if before else jnp.zeros_like(sums_ref)
    sums_ref[0:1, :] += jnp.sum(upstream * unit, 0, keepdims=True)
    sums_ref[1:2, :] += jnp.sum(upstream, 0, keepdims=True)
    sums_ref[2:3, :] += jnp.sum(first, 0, keepdims=True)
    total_ref[...] = first
    low = first.astype(BF16)
    low_ref[...] = low
    grad_ref[...] = dot(low, out_weight_ref[layer], 1, 1).astype(BF16)


def joint_back_kernel(
    layer,
    place,
    core_ref,
    *refs,
):
    pairs = (len(refs) - 6) // 3
    q_refs, own_refs, recv_refs = (refs[k * pairs : (k + 1) * pairs] for k in range(3))
    q_weight_ref, kv_weight_ref, mine_ref, theirs_ref, bias_ref, part_ref = refs[3 * pairs :]
    span = slice(place * CHUNK, (place + 1) * CHUNK)
    width = 128 * pairs
    local = width // 2
    q_grad = jnp.concatenate([ref[span, :] for ref in q_refs], 1)
    both = [
        (own[place] + recv[place].astype(F32)).astype(BF16)
        for own, recv in zip(own_refs, recv_refs)
    ]
    kv_grad = jnp.concatenate(
        [part[:, :128] for part in both] + [part[:, 128:] for part in both], 1
    )
    first = core_ref[0] == 0
    for member, value in enumerate((q_grad, kv_grad[:, :width], kv_grad[:, width:])):
        left, right = value[:, :local].astype(F32), value[:, local:].astype(F32)
        lanes = slice(member * local, (member + 1) * local)
        mine_ref[:, lanes] = jnp.where(first, left, right).astype(BF16)
        theirs_ref[:, lanes] = jnp.where(first, right, left).astype(BF16)
    bias_ref[...] = jnp.zeros_like(bias_ref)
    bias_ref[0:1, :] = jnp.sum(q_grad.astype(F32), 0, keepdims=True)
    bias_ref[1:2, :] = jnp.sum(kv_grad[:, width:].astype(F32), 0, keepdims=True)
    part_ref[...] = (
        dot(q_grad, q_weight_ref[layer]) + dot(kv_grad, kv_weight_ref[layer])
    ).astype(BF16)


def weights_kernel(core_ref, *refs):
    sources, vectors, small_ref, other_ref = refs[:8], refs[8:14], refs[14], refs[15]
    q_ref, kv_ref, out_ref, vec_ref, q_bias_ref, kv_bias_ref, unit_bias_ref = refs[16:]
    local = sources[0].shape[1]
    width = 2 * local
    own_row = pl.multiple_of(core_ref[0] * local, local)
    other_row = pl.multiple_of((1 - core_ref[0]) * local, local)
    for layer in range(LAYERS):
        for member, (target, start) in enumerate(
            ((q_ref, 0), (kv_ref, 0), (kv_ref, width), (out_ref, 0))
        ):
            target[layer, pl.ds(start + own_row, local), :] = sources[2 * member][layer]
            target[layer, pl.ds(start + other_row, local), :] = sources[2 * member + 1][layer]

    first = core_ref[0] == 0
    for layer in range(LAYERS):
        row = slice(layer, layer + 1)
        for member, vector in enumerate(vectors):
            vec_ref[layer, member : member + 1, :] = vector[...].astype(F32)[row]
        if layer == 0:
            vec_ref[layer, 6:7, :] = jnp.ones_like(vec_ref[layer, 6:7, :])
            vec_ref[layer, 7:8, :] = jnp.zeros_like(vec_ref[layer, 7:8, :])
        else:
            vec_ref[layer, 6:8, :] = vec_ref[layer - 1, 4:6, :]
        own = small_ref[...].astype(F32)[row]
        other = other_ref[...].astype(F32)[row]
        kv_bias_ref[layer] = jnp.zeros_like(kv_bias_ref[layer])
        for target, start, lanes in (
            (q_bias_ref, 0, slice(0, local)),
            (kv_bias_ref, width, slice(local, width)),
        ):
            left, right = own[:, lanes], other[:, lanes]
            target[layer, :, start : start + local] = jnp.where(first, left, right)
            target[layer, :, start + local : start + width] = jnp.where(first, right, left)
        units = own.shape[1] - width
        unit_bias_ref[layer, :, :units] = own[:, width:]
        unit_bias_ref[layer, :, units:] = other[:, width:]


def halve_kernel(bit, numbers_ref, *refs):
    parts, (sent_ref, kept_ref) = refs[:-2], refs[-2:]
    half = sent_ref.shape[0]
    for target, number in ((sent_ref, 1 - numbers_ref[bit]), (kept_ref, numbers_ref[bit])):
        rows = pl.ds(pl.multiple_of(number * half, half), half)
        target[...] = sum(part[rows, :].astype(F32) for part in parts).astype(target.dtype)


def add_kernel(kept_ref, recv_ref, piece_ref):
    piece_ref[0] = (kept_ref[...] + recv_ref[...].astype(F32)).astype(BF16)


def join_kernel(pieces_ref, recv_ref, joined_ref):
    count = pieces_ref.shape[0]
    joined_ref[:count] = pieces_ref[...]
    joined_ref[count:] = recv_ref[...]


def arrange(place, pieces_ref, recv_ref, full):
    count, rows = pieces_ref.shape[0], pieces_ref.shape[1]
    for number in range(2 * count):
        source = pieces_ref[number] if number < count else recv_ref[number - count]
        start = pl.multiple_of((number ^ place) * rows, rows)
        full[pl.ds(start, rows), :] = source.astype(F32)


def unpack_kernel(place, numbers_ref, pieces_ref, recv_ref, *refs):
    targets, full = refs[:-1], refs[-1]
    arrange(numbers_ref[place], pieces_ref, recv_ref, full)
    start = 0
    for target in targets:
        rows = target.shape[-2]
        value = full[start : start + rows, :]
        if len(target.shape) == 3:
            target[0] = value
        else:
            target[...] = value.astype(target.dtype)
        start += rows


def vectors_unpack_kernel(place, numbers_ref, pieces_ref, recv_ref, *refs):
    q_ref, table_ref, targets, full = refs[0], refs[1], refs[2:-1], refs[-1]
    arrange(numbers_ref[place], pieces_ref, recv_ref, full)
    local = q_ref.shape[1]
    half = table_ref.shape[0]
    q_ref[0] = full[:local, :]
    table_ref[...] = full[local : local + half, :].astype(BF16)
    for layer in range(LAYERS):
        start = local + half + 8 * layer
        row = slice(layer, layer + 1)
        for member in range(7):
            targets[member][row, :] = full[start + member : start + member + 1, :]
        last = full[start + 7 : start + 8, :]
        for member in range(2):
            targets[7 + member][row, :] = last[:, member * local : (member + 1) * local]


def table_kernel(chunks, share, numbers_ref, bucket_ref, *refs):
    joints, firsts = refs[:chunks], refs[chunks : 2 * chunks]
    vectors = refs[2 * chunks : -3]
    mine_ref, sent_ref, full = refs[-3:]
    buckets, half = full.shape[0], full.shape[0] // 2
    chip, core = numbers_ref[1], numbers_ref[0]
    numbers = lax.broadcasted_iota(jnp.int32, (buckets, CHUNK), 0)
    places = lax.broadcasted_iota(jnp.int32, (buckets, CHUNK), 1)
    total = None
    for place in range(chunks):
        hit = numbers == bucket_ref[place]
        rows = places + place * CHUNK
        mine = jnp.logical_and(rows >= chip * share, rows < (chip + 1) * share)
        every = jnp.where(hit, 1.0, 0.0).astype(BF16)
        own = jnp.where(jnp.logical_and(hit, mine), 1.0, 0.0).astype(BF16)
        first = firsts[place][...]
        high = first.astype(BF16)
        rest = (first - high.astype(F32)).astype(BF16)
        part = dot(every, joints[place][...]) + (dot(own, high) + dot(own, rest))
        total = part if total is None else total + part
    full[...] = total
    mine_ref[:half, :] = full[pl.ds(pl.multiple_of(core * half, half), half), :]
    sent_ref[:half, :] = full[pl.ds(pl.multiple_of((1 - core) * half, half), half), :].astype(BF16)
    for layer in range(LAYERS):
        rows = slice(half + 8 * layer, half + 8 * layer + 8)
        mine_ref[rows, :] = vectors[2 * layer][...]
        sent_ref[rows, :] = vectors[2 * layer + 1][...].astype(BF16)


def vectors_kernel(numbers_ref, second_ref, first_ref, unit_ref, *refs):
    mine_ref, sent_ref = refs[-2:]
    second, first, unit = second_ref[...], first_ref[...], unit_ref[...]
    bias = sum(ref[...] for ref in refs[:-2])
    units, local = unit.shape[1] // 2, bias.shape[1] // 2
    low = numbers_ref[0] == 0
    for target, lanes, flip in (
        (mine_ref, slice(0, units), False),
        (sent_ref, slice(units, 2 * units), True),
    ):
        target[0:3, :] = second[0:3, :]
        target[3:6, :] = first[0:3, :]
        target[6:7, :] = unit[:, lanes]
        target[7:8, :] = jnp.zeros_like(target[7:8, :])
        for member in range(2):
            left, right = bias[member : member + 1, :local], bias[member : member + 1, local:]
            if flip:
                left, right = right, left
            target[7:8, member * local : (member + 1) * local] = jnp.where(low, left, right)


def table_add_kernel(mine_ref, recv_ref, both_ref, sent_ref):
    total = mine_ref[...] + recv_ref[...].astype(F32)
    both_ref[...] = total
    sent_ref[...] = total[: sent_ref.shape[0], :].astype(BF16)


def pack_kernel(q_ref, both_ref, sent_ref, recv_ref, packed_ref):
    local, half, rows = q_ref.shape[0], sent_ref.shape[0], both_ref.shape[0]
    packed_ref[...] = jnp.zeros_like(packed_ref)
    packed_ref[:local, :] = q_ref[...]
    table = sent_ref[...].astype(F32) + recv_ref[...].astype(F32)
    packed_ref[local : local + half, :] = table.astype(BF16)
    packed_ref[local + half : local + rows, :] = both_ref[half:, :].astype(BF16)


def pile_kernel(*refs):
    sources, target = refs[:-1], refs[-1]
    start = 0
    for source in sources:
        rows = source.shape[0]
        target[start : start + rows, :] = source[...].astype(target.dtype)
        start += rows
    if start < target.shape[0]:
        target[start:, :] = jnp.zeros_like(target[start:, :])


def pick_rows(chip, chunk_refs, share, target):
    for number in range(2):

        @pl.when(chip == number)
        def _():
            start, end = number * share, (number + 1) * share
            for place, ref in enumerate(chunk_refs):
                low, high = max(start, place * CHUNK), min(end, (place + 1) * CHUNK)
                if low < high:
                    target[low - start : high - start, :] = ref[
                        low - place * CHUNK : high - place * CHUNK, :
                    ]


def own_rows_kernel(numbers_ref, *refs):
    pick_rows(numbers_ref[1], refs[:-1], refs[-1].shape[0], refs[-1])


def tokens_send_kernel(numbers_ref, *refs):
    pick_rows(1 - numbers_ref[1], refs[:-1], refs[-1].shape[0], refs[-1])


def tokens_kernel(chunks, numbers_ref, *refs):
    joints, firsts = refs[:chunks], refs[chunks : 2 * chunks]
    recv_ref, target, own = refs[2 * chunks :]
    share = target.shape[0]
    pick_rows(numbers_ref[1], joints, share, own)
    pick_rows(numbers_ref[1], firsts, share, target)
    target[...] += own[...].astype(F32) + recv_ref[...].astype(F32)


class Wide:
    BITS = {"y": (2, 1), "near": (3, 2), "far": (4, 4)}
    PLACES = {("y", "near", "far"): 5, ("near", "y", "far"): 6}

    def __init__(self, size, chip, core):
        self.small, self.size = size == 8, size
        index = lax.axis_index("wide")
        bits = {name: (index >> k) & 1 for k, name in enumerate(("y", "near", "far"))}
        places = [
            sum(bits[name] << (2 - k) for k, name in enumerate(order)) if self.small else 0
            for order in self.PLACES
        ]
        self.numbers = jnp.stack(
            [
                jnp.asarray(value, jnp.int32)
                for value in (core, chip, bits["y"], bits["near"], bits["far"], *places, 0)
            ]
        )

    def pairs(self, name):
        reach = self.BITS[name][1]
        return [(number, number ^ reach) for number in range(self.size)]


def gate(value, *later):
    return lax.optimization_barrier((value,) + later)[0] if later else value


SMEM = pl.BlockSpec(memory_space=pltpu.SMEM)


class Chain:
    def __init__(self, wide, value, order):
        self.wide, self.order, self.step = wide, order, 0
        self.parts, self.rows = [value], value.shape[0]

    def advance(self, *after):
        if not self.wide.small:
            if self.step == 0:
                value = self.parts[0]
                self.parts = lax.psum(value, "wide").reshape(2, 4, -1, value.shape[1])
            self.step = 6
            self.sent = self.parts[0]
            return self.parts[0]
        self.step += 1
        parts = [(part, ON_CHIP) for part in self.parts]
        columns = self.parts[0].shape[-1]
        if self.step <= 3:
            name = self.order[self.step - 1]
            half = (self.parts[0].shape[0] // 2, columns)
            sent, kept = call(
                functools.partial(halve_kernel, Wide.BITS[name][0]),
                None,
                [(self.wide.numbers, SMEM)] + parts,
                [(half, BF16, ON_CHIP, None), (half, F32, ON_CHIP, None)],
                after=after,
            )
            self.parts = [kept, lax.ppermute(sent, "wide", self.wide.pairs(name))]
            self.sent = sent
            return sent
        kernel = add_kernel if self.step == 4 else join_kernel
        shape = self.parts[0].shape
        shape = (1,) + shape if self.step == 4 else (2 * shape[0],) + shape[1:]
        (sent,) = call(kernel, None, parts, [(shape, BF16, ON_CHIP, None)], after=after)
        name = self.order[6 - self.step]
        self.parts = [sent, lax.ppermute(sent, "wide", self.wide.pairs(name))]
        return sent

    def finish(self):
        while self.step < 6:
            self.advance()
        return [self.parts[0], self.parts[1]]


def on_device(wide, *arguments):
    (
        tokens,
        buckets,
        lengths,
        type_table,
        query_weight,
        query_bias,
        key_weight,
        value_weight,
        value_bias,
        output_weight,
        output_bias,
        attention_gain,
        attention_shift,
        up_weight,
        up_bias,
        down_weight,
        down_bias,
        feed_gain,
        feed_shift,
        cotangent,
    ) = arguments
    share, model = tokens.shape
    lane = 2 * share
    chunks = lane // CHUNK
    local = query_weight.shape[2]
    width = 2 * local
    head_count = width // HEAD_DIM
    units = up_weight.shape[2]
    place = lax.axis_index("narrow")
    chip, core = place // 2, place % 2
    first_chip, first_core = chip == 0, core == 0

    def by_core(own, other, axis):
        return jnp.where(
            first_core,
            jnp.concatenate([own, other], axis),
            jnp.concatenate([other, own], axis),
        )

    def by_chip(own, other):
        return jnp.where(
            first_chip, jnp.concatenate([own, other], 0), jnp.concatenate([other, own], 0)
        )

    def own_rows(rows):
        return jnp.where(first_chip, rows[:share], rows[share:])

    def other_rows(rows):
        return jnp.where(first_chip, rows[share:], rows[:share])

    lane_tokens = by_chip(tokens, over_chip(tokens))
    lane_buckets = by_chip(buckets, over_chip(buckets))
    lane_cotangent = by_chip(cotangent, over_chip(cotangent))

    smem = pl.BlockSpec(memory_space=pltpu.SMEM)
    sums = Wide(wide, chip, core)
    core_number = sums.numbers
    shards = []
    turned_weights = [
        jnp.swapaxes(weight, 1, 2) for weight in (query_weight, key_weight, value_weight)
    ]
    for weight in turned_weights + [output_weight]:
        shards += [(weight, ON_CHIP), (over_core(weight), ON_CHIP)]

    small = jnp.concatenate([query_bias, value_bias, up_bias], 1)
    vectors = [
        output_bias,
        attention_gain,
        attention_shift,
        down_bias,
        feed_gain,
        feed_shift,
        small,
        over_core(small),
    ]
    qw, kvw, ow, vec, q_bias, kv_bias, unit_bias = call(
        weights_kernel,
        None,
        [(core_number, smem)] + shards + [(vector, ON_CHIP) for vector in vectors],
        [
            (shape, dtype, ON_CHIP, None)
            for shape, dtype in (
                ((LAYERS, width, model), BF16),
                ((LAYERS, 2 * width, model), BF16),
                ((LAYERS, width, model), BF16),
                ((LAYERS, 8, model), F32),
                ((LAYERS, 1, width), F32),
                ((LAYERS, 1, 2 * width), F32),
                ((LAYERS, 1, 2 * units), F32),
            )
        ],
    )
    up_other = over_core(up_weight)
    down_other = over_core(down_weight)

    ends = jnp.cumsum(lengths[0], dtype=jnp.int32)
    offsets = lax.iota(jnp.int32, share)
    spots = jnp.concatenate(
        [
            offsets + (block * 2 + which) * share
            for which in (core, 1 - core)
            for block in range(2)
        ]
    )
    labels = jnp.sum((spots[:, None] >= ends[None, :]).astype(jnp.int32), 1, dtype=jnp.int32)
    tiles = 2 * chunks
    tile_labels = labels.reshape(tiles, CHUNK)
    present = jnp.any(
        tile_labels[:, :, None] == lax.iota(jnp.int32, lengths.shape[1])[None, None, :], axis=1
    )
    bits = jnp.sum(
        jnp.where(present, jnp.left_shift(1, lax.iota(jnp.int32, lengths.shape[1]))[None, :], 0),
        axis=1,
        dtype=jnp.int32,
    )
    bits = jnp.concatenate([bits, bits[:chunks]])
    k_labels = tile_labels[:, :, None]
    q_labels = tile_labels[:chunks, None, :]

    block = (CHUNK, model)

    def layer_spec(layer, shape):
        return pl.BlockSpec((1,) + shape, lambda *ids: (layer,) + (0,) * len(shape))

    selector = (lane_buckets[:, None] == lax.iota(jnp.int32, type_table.shape[0])[None, :]).astype(
        BF16
    )
    stream = lane_tokens.astype(F32) + dot(selector, type_table)
    low_first = stream.astype(BF16)
    state = [stream[CHUNK * i : CHUNK * (i + 1)] for i in range(chunks)]
    kept = []
    for layer in range(LAYERS):
        keep = {}
        if layer == 0:
            kv = (dot(low_first, kvw[0], 1, 1) + kv_bias[0]).astype(BF16)
            queries = ((dot(low_first, qw[0], 1, 1) + q_bias[0]) * HEAD_DIM**-0.5).astype(BF16)
            low_in, kv, queries = (
                [value[CHUNK * i : CHUNK * (i + 1)] for i in range(chunks)]
                for value in (low_first, kv, queries)
            )
            kv_other = [over_core(part) for part in kv]
        else:
            low_in, queries, kv, kv_other = [], [], [], []
            units_now, inverses = [], []
            for i in range(chunks):
                outs = call(
                    functools.partial(project_kernel, layer, i),
                    None,
                    [
                        (value, ON_CHIP)
                        for value in (
                            state[i],
                            feed_share[i],
                            feed_recv[i],
                            vec,
                            qw,
                            kvw,
                            q_bias,
                            kv_bias,
                        )
                    ],
                    [
                        (block, F32, ON_CHIP, None),
                        ((CHUNK, 1), F32, ON_CHIP, None),
                        (block, BF16, ON_CHIP, None),
                        ((CHUNK, width), BF16, ON_CHIP, None),
                        ((CHUNK, 2 * width), BF16, ON_CHIP, None),
                    ],
                    cost=2,
                )
                units_now.append(outs[0])
                inverses.append(outs[1])
                low_in.append(outs[2])
                queries.append(outs[3])
                kv.append(outs[4])
                kv_other.append(over_core(outs[4]))
            state = units_now
            kept[layer - 1]["second_unit"] = units_now
            kept[layer - 1]["second_inverse"] = inverses
        kv_all, turned = call(
            gather_kernel,
            None,
            [(part, ON_CHIP) for part in kv + kv_other],
            [
                ((tiles, CHUNK, 2 * width), BF16, ON_CHIP, None),
                ((tiles, 2 * width, CHUNK), BF16, ON_CHIP, None),
            ],
            cost=2,
        )
        context, exact, logsum, shares = [], [], [], []
        for i in range(chunks):
            outs = call(
                functools.partial(attend_kernel, head_count, layer, i),
                None,
                [(bits, smem)]
                + [
                    (value, ON_CHIP)
                    for value in (queries[i], kv_all, turned, q_labels, k_labels, ow)
                ],
                [
                    ((CHUNK, width), BF16, ON_CHIP, None),
                    ((CHUNK, width), F32, ON_CHIP, None),
                    ((8, CHUNK), F32, ON_CHIP, None),
                    (block, BF16, ON_CHIP, None),
                ],
                scratch=[
                    pltpu.VMEM((head_count * CHUNK, 128), BF16),
                    pltpu.VMEM((width, CHUNK), F32),
                    pltpu.VMEM((head_count // 2, 8, 2 * CHUNK), F32),
                    pltpu.VMEM((head_count // 2, 8, 2 * CHUNK), F32),
                    pltpu.VMEM((head_count // 2, tiles, CHUNK, 2 * CHUNK), F32),
                ],
                cost=6,
                limit=20,
            )
            for target, value in zip((context, exact, logsum, shares), outs):
                target.append(value)
        received = [over_chip(part) for part in shares]
        low_middle, act, slope, first_unit, first_inverse, feed_share = [], [], [], [], [], []
        for i in range(chunks):
            outs = call(
                functools.partial(feed_kernel, layer, i),
                None,
                [
                    (value, ON_CHIP)
                    for value in (
                        state[i],
                        shares[i],
                        received[i],
                        vec,
                        up_weight,
                        up_other,
                        unit_bias,
                        down_weight,
                        down_other,
                    )
                ],
                [
                    (block, F32, ON_CHIP, None),
                    ((CHUNK, 1), F32, ON_CHIP, None),
                    (block, BF16, ON_CHIP, None),
                    ((CHUNK, 2 * units), BF16, ON_CHIP, None),
                    ((CHUNK, 2 * units), BF16, ON_CHIP, None),
                    (block, BF16, ON_CHIP, None),
                ],
                cost=8,
            )
            for target, value in zip(
                (first_unit, first_inverse, low_middle, act, slope, feed_share), outs
            ):
                target.append(value)
        feed_recv = [over_chip(part) for part in feed_share]
        state = first_unit
        keep.update(
            low_in=low_in,
            queries=queries,
            kv_all=kv_all,
            turned=turned,
            context=context,
            exact=exact,
            logsum=logsum,
            first_unit=first_unit,
            first_inverse=first_inverse,
            low_middle=low_middle,
            act=act,
            slope=slope,
        )
        kept.append(keep)

    pair_order, other_order = ("y", "near", "far"), ("near", "y", "far")

    def unpacked(kernel, layer, sources, shapes, buffers, scratch=(), after=()):
        return call(
            kernel,
            (1,),
            [(source, smem if source is sums.numbers else whole(source.shape)) for source in sources],
            [
                ((LAYERS,) + shape, F32, layer_spec(layer, shape), buffer)
                for shape, buffer in zip(shapes, buffers)
            ],
            scratch,
            after=after,
        )

    def unpacked_rows(layer, chain, shapes, buffers, after=()):
        return unpacked(
            functools.partial(unpack_kernel, Wide.PLACES[chain.order]),
            layer,
            [sums.numbers] + chain.finish(),
            shapes,
            buffers,
            [pltpu.VMEM((chain.rows, model), F32)],
            after,
        )

    def piled(rows, *values):
        return call(
            pile_kernel,
            None,
            [(value, ON_CHIP) for value in values],
            [((rows, model), BF16, ON_CHIP, None)],
        )[0]

    vector_sums = [None] * LAYERS
    encoded = []
    for layer in reversed(range(LAYERS)):
        keep = kept[layer]
        top_layer = layer == LAYERS - 1
        second, low_second, up_grad, unit_sums, second_sums, parts = [], [], [], [], [], []
        for i in range(chunks):
            if top_layer:
                upstream = lane_cotangent
                unit = keep["first_unit"][i]
                inverse = keep["first_inverse"][i]
                added = (feed_share[i], feed_recv[i])
            else:
                upstream = first_total[i]
                unit = keep["second_unit"][i]
                inverse = keep["second_inverse"][i]
                added = (joint_share[i], joint_recv[i])
            outs = call(
                functools.partial(feed_back_kernel, layer, i, top_layer),
                None,
                [
                    (value, ON_CHIP)
                    for value in (
                        upstream,
                        unit,
                        inverse,
                        added[0],
                        added[1],
                        vec,
                        keep["slope"][i],
                        up_weight,
                        up_other,
                        down_weight,
                        down_other,
                        *second_sums[-1:],
                        *unit_sums[-1:],
                    )
                ],
                [
                    (block if top_layer else (8, 128), BF16, ON_CHIP, None),
                    (block, F32, ON_CHIP, None),
                    (block, BF16, ON_CHIP, None),
                    ((CHUNK, 2 * units), BF16, ON_CHIP, None),
                    ((1, 2 * units), F32, ON_CHIP, None),
                    ((8, model), F32, ON_CHIP, None),
                    (block, BF16, ON_CHIP, None),
                ],
                cost=0,
                after=(
                    []
                    if top_layer or i == 1
                    else [upper.advance(), feed_chain.advance(joint_share[2]), vector_sums[1][0]]
                    if i == 0
                    else []
                ),
            )
            if top_layer:
                encoded.append(outs[0])
            for target, value in zip(
                (second, low_second, up_grad, unit_sums, second_sums, parts), outs[1:]
            ):
                target.append(value)
        received = [over_chip(part) for part in parts]

        def weight_grad(lefts, rights, shape, left_start=0, right_start=0, received=()):
            return call(
                functools.partial(weight_grad_kernel, chunks, left_start, right_start),
                None,
                [(value, ON_CHIP) for value in [*lefts, *rights, *received]],
                [(shape, BF16, ON_CHIP, None)],
                cost=0,
            )[0]

        square = (model, units)
        down_other_grad = over_core(
            weight_grad(keep["act"], low_second, square[::-1], left_start=units)
        )
        up_other_grad = over_core(
            weight_grad(keep["low_middle"], up_grad, square, right_start=units)
        )
        down_grad = weight_grad(
            keep["act"], low_second, square[::-1], received=[down_other_grad]
        )
        up_weight_grad = weight_grad(
            keep["low_middle"], up_grad, square, received=[up_other_grad]
        )
        first_total, low_total, context_grad, first_sums = [], [], [], []
        if top_layer:
            (own_encoded,) = call(
                own_rows_kernel,
                (1,),
                [(sums.numbers, smem)] + [(part, whole(block)) for part in encoded],
                [((share, model), BF16, whole((share, model)), None)],
            )
        for i in range(chunks):
            outs = call(
                functools.partial(context_back_kernel, layer, i),
                None,
                [
                    (value, ON_CHIP)
                    for value in (
                        second[i],
                        parts[i],
                        received[i],
                        keep["first_unit"][i],
                        keep["first_inverse"][i],
                        vec,
                        ow,
                        *first_sums[-1:],
                    )
                ],
                [
                    (block, F32, ON_CHIP, None),
                    (block, BF16, ON_CHIP, None),
                    ((CHUNK, width), BF16, ON_CHIP, None),
                    ((8, model), F32, ON_CHIP, None),
                ],
                after=(
                    [own_encoded] * (top_layer and i == 0)
                    if top_layer or i != 1
                    else [upper.advance(second_sums[2]), feed_chain.advance(second_sums[2])]
                ),
            )
            for target, value in zip((first_total, low_total, context_grad, first_sums), outs):
                target.append(value)
        own, other = call(
            functools.partial(out_grad_kernel, chunks),
            None,
            [(core_number, smem)]
            + [(value, ON_CHIP) for value in keep["context"] + low_total],
            [((local, model), F32, ON_CHIP, None), ((local, model), BF16, ON_CHIP, None)],
            scratch=[pltpu.VMEM((width, model), F32)],
        )
        out_grad = (own + over_core(other).astype(F32)).astype(BF16)
        pending = [out_grad, up_weight_grad, down_grad]
        if top_layer:
            feed_chain = Chain(sums, piled(2 * units, up_weight_grad, down_grad), pair_order)
            pending = [out_grad, feed_chain.advance()]
        else:
            strands = [
                Chain(sums, up_weight_grad, pair_order),
                Chain(sums, down_grad, other_order),
            ]
            pending = [
                out_grad,
                upper.advance(first_sums[2]),
                feed_chain.advance(first_sums[2]),
                *[strand.advance() for strand in strands],
            ]
        half_shape = (chunks, CHUNK, 256)
        q_grads, kv_owns, kv_recvs = [], [], []
        for pair in range(head_count // 2):
            q_grad, kv_grad, kv_grad_other = call(
                functools.partial(attend_back_kernel, pair, head_count, chunks),
                None,
                [(bits, smem)]
                + [
                    (value, ON_CHIP)
                    for value in [keep["kv_all"], keep["turned"], q_labels, k_labels]
                    + keep["queries"]
                    + context_grad
                    + keep["exact"]
                    + keep["logsum"]
                ],
                [
                    ((lane, 128), BF16, ON_CHIP, None),
                    (half_shape, F32, ON_CHIP, None),
                    (half_shape, BF16, ON_CHIP, None),
                ],
                scratch=[
                    pltpu.VMEM((2 * CHUNK, 128), BF16),
                    pltpu.VMEM((2 * CHUNK, 128), BF16),
                    pltpu.VMEM((8, 2 * CHUNK), F32),
                    pltpu.VMEM((128, CHUNK), F32),
                    pltpu.VMEM((tiles, CHUNK, 256), F32),
                ],
                cost=0,
                limit=16,
                after=pending + q_grads[-1:],
            )
            pending = []
            if not top_layer:
                pending = [upper.advance(q_grad)]
                if pair == 0:
                    pending.append(feed_chain.advance(q_grad))
                if pair == 2:
                    up_out, down_out = unpacked_rows(
                        1, feed_chain, [square, square[::-1]], [None] * 2, after=[q_grad]
                    )
                    pending.append(up_out)
                if pair > 0:
                    pending += [strand.advance(q_grad) for strand in strands]
            elif pair == 2:
                pending = [feed_chain.advance(q_grad)]
            q_grads.append(q_grad)
            kv_owns.append(kv_grad)
            kv_recvs.append(over_core(gate(kv_grad_other, *pending)))
        joint_own, joint_other, bias_sums, joint_share = [], [], [], []
        for i in range(chunks):
            outs = call(
                functools.partial(joint_back_kernel, layer, i),
                None,
                [(core_number, smem)]
                + [(value, ON_CHIP) for value in q_grads + kv_owns + kv_recvs + [qw, kvw]],
                [
                    ((CHUNK, 3 * local), BF16, ON_CHIP, None),
                    ((CHUNK, 3 * local), BF16, ON_CHIP, None),
                    ((8, width), F32, ON_CHIP, None),
                    (block, BF16, ON_CHIP, None),
                ],
                cost=0,
            )
            for target, value in zip((joint_own, joint_other, bias_sums, joint_share), outs):
                target.append(value)
        vector_sums[layer] = call(
            vectors_kernel,
            None,
            [(sums.numbers, smem)]
            + [(value, ON_CHIP) for value in second_sums[-1:] + first_sums[-1:] + unit_sums[-1:] + bias_sums],
            [((8, model), F32, ON_CHIP, None), ((8, model), F32, ON_CHIP, None)],
        )
        if layer > 0:
            joint_recv = [over_chip(part) for part in joint_share]
        joint_other_grad = weight_grad(joint_other, keep["low_in"], (3 * local, model))
        if layer == 0:
            buckets_total = type_table.shape[0]
            half_table = buckets_total // 2
            table_mine, table_sent = call(
                functools.partial(table_kernel, chunks, share),
                None,
                [
                    (value, smem if value is sums.numbers else ON_CHIP)
                    for value in [sums.numbers, lane_buckets.reshape(chunks, 1, CHUNK)]
                    + joint_share
                    + first_total
                    + [*vector_sums[0], *vector_sums[1]]
                ],
                [
                    ((half_table + 16, model), F32, ON_CHIP, None),
                    ((half_table + 16, model), BF16, ON_CHIP, None),
                ],
                scratch=[pltpu.VMEM((buckets_total, model), F32)],
                cost=0,
                after=[joint_other_grad],
            )
            table_recv = over_core(table_sent)
        joint_recv_grad = over_core(joint_other_grad)
        if layer == 0:
            table_both, table_low = call(
                table_add_kernel,
                None,
                [(table_mine, ON_CHIP), (table_recv, ON_CHIP)],
                [
                    ((half_table + 16, model), F32, ON_CHIP, None),
                    ((half_table, model), BF16, ON_CHIP, None),
                ],
            )
        joint_grad = weight_grad(
            joint_own, keep["low_in"], (3 * local, model), received=[joint_recv_grad]
        )
        flat = [(local, model)] * 4
        if layer > 0:
            upper = Chain(sums, piled(4 * local, joint_grad, out_grad), other_order)

    second_chain = Chain(
        sums, piled(10 * half_table // 2, joint_grad[local:], out_grad), other_order
    )
    second_sent = second_chain.advance()
    table_other = over_chip(table_low)
    (tokens_sent,) = call(
        tokens_send_kernel,
        None,
        [(sums.numbers, smem)] + [(part, ON_CHIP) for part in joint_share],
        [((share, model), BF16, ON_CHIP, None)],
        after=[table_low],
    )
    tokens_recv = over_chip(tokens_sent)
    (packed,) = call(
        pack_kernel,
        None,
        [(value, ON_CHIP) for value in (joint_grad[:local], table_both, table_low, table_other)],
        [((3 * half_table, model), BF16, ON_CHIP, None)],
    )
    first_chain = Chain(sums, packed, pair_order)
    token = first_chain.advance()
    for step in range(5):
        for strand in strands:
            if strand.step < 6:
                token = strand.advance(token)
        token = second_chain.advance(token)
        if upper.step < 6:
            token = upper.advance(token)
        token = first_chain.advance(token)
        if step == 0:
            turned_out = unpacked_rows(1, upper, flat, [None] * 4, after=[token])
            token = strands[0].advance(turned_out[0])
        if step == 3:
            (tokens_grad,) = call(
                functools.partial(tokens_kernel, chunks),
                (1,),
                [(sums.numbers, smem)]
                + [
                    (value, whole(value.shape))
                    for value in joint_share + first_total + [tokens_recv]
                ],
                [((share, model), F32, whole((share, model)), None)],
                scratch=[pltpu.VMEM((share, model), BF16)],
                after=[token],
            )
        if step == 4:
            (up_out,) = unpacked_rows(0, strands[0], [square], [up_out], after=[token])
            (down_out,) = unpacked_rows(0, strands[1], [square[::-1]], [down_out])
    k_out, v_out, o_out = unpacked_rows(0, second_chain, flat[:3], turned_out[1:])
    shapes = [(LAYERS, model)] * 7 + [(LAYERS, local)] * 2
    q_out, table_half, *vector_out = call(
        functools.partial(vectors_unpack_kernel, Wide.PLACES[pair_order]),
        (1,),
        [(sums.numbers, smem)] + [(value, whole(value.shape)) for value in first_chain.finish()],
        [
            ((LAYERS, local, model), F32, layer_spec(0, (local, model)), turned_out[0]),
            ((half_table, model), BF16, whole((half_table, model)), None),
        ]
        + [(shape, F32, whole(shape), None) for shape in shapes],
        scratch=[pltpu.VMEM((first_chain.rows, model), F32)],
    )
    table_grad = by_core(table_half, over_core(table_half), 0).astype(F32)

    return (
        own_encoded,
        tokens_grad,
        table_grad,
        jnp.swapaxes(q_out, 1, 2),
        vector_out[7],
        jnp.swapaxes(k_out, 1, 2),
        jnp.swapaxes(v_out, 1, 2),
        vector_out[8],
        o_out,
        vector_out[5],
        vector_out[3],
        vector_out[4],
        up_out,
        vector_out[6],
        down_out,
        vector_out[2],
        vector_out[0],
        vector_out[1],
    )


def solution(mesh):
    rows = P(("wide", "narrow"), None)
    third = P(None, None, "narrow")
    second = P(None, "narrow")
    middle = P(None, "narrow", None)
    in_specs = (
        rows,
        P(("wide", "narrow")),
        P("wide", None),
        P(),
        third,
        second,
        third,
        third,
        second,
        middle,
        P(),
        P(),
        P(),
        third,
        second,
        middle,
        P(),
        P(),
        P(),
        rows,
    )
    out_specs = (
        rows,
        rows,
        P(),
        third,
        second,
        third,
        third,
        second,
        middle,
        P(),
        P(),
        P(),
        third,
        second,
        middle,
        P(),
        P(),
        P(),
    )
    return jax.shard_map(
        functools.partial(on_device, mesh.shape["wide"]),
        mesh=mesh,
        in_specs=in_specs,
        out_specs=out_specs,
        check_vma=False,
    )
```

```python
import functools

import jax
import jax.numpy as jnp
from jax import lax
from jax.experimental import pallas as pl
from jax.experimental.pallas import tpu as pltpu
from jax.sharding import PartitionSpec as P

HEAD_DIM = 64
LAYERS = 2
CHUNK = 256
EPS = 1e-12
ROOT_HALF = 0.7071067811865476
DENSITY = 0.3989422804014327
NEG = -1e30
F32 = jnp.float32
BF16 = jnp.bfloat16
MIB = 1 << 20
CORE_SWAP = [(0, 1), (1, 0), (2, 3), (3, 2)]
CHIP_SWAP = [(0, 2), (2, 0), (1, 3), (3, 1)]


def over_core(value):
    return lax.ppermute(value, "narrow", CORE_SWAP)


def over_chip(value):
    return lax.ppermute(value, "narrow", CHIP_SWAP)


def dot(left, right, left_axis=1, right_axis=0):
    return lax.dot_general(
        left, right, (((left_axis,), (right_axis,)), ((), ())), preferred_element_type=F32
    )


def norm_parts(summed):
    row_mean = jnp.mean(summed, -1, keepdims=True)
    centred = summed - row_mean
    spread = jnp.mean(centred * centred, -1, keepdims=True)
    inverse = lax.rsqrt(spread + EPS)
    return centred * inverse, inverse


def norm_back(upstream, unit_rows, inverse, gain_row):
    scaled = upstream * gain_row
    return inverse * (
        scaled
        - jnp.mean(scaled, -1, keepdims=True)
        - unit_rows * jnp.mean(scaled * unit_rows, -1, keepdims=True)
    )


def gelu_parts(preact):
    size = jnp.abs(preact) * ROOT_HALF
    bell = jnp.exp(-(size * size))
    step = 1.0 / (1.0 + 0.3275911 * size)
    series = step * (
        0.254829592
        + step * (-0.284496736 + step * (1.421413741 + step * (-1.453152027 + step * 1.061405429)))
    )
    tail = 0.5 * series * bell
    cdf = jnp.where(preact >= 0.0, 1.0 - tail, tail)
    return preact * cdf, cdf + preact * DENSITY * bell


ON_CHIP = pl.BlockSpec(memory_space=pltpu.VMEM)


def whole(shape):
    zeros = (0,) * len(shape)
    return pl.BlockSpec(shape, lambda *ids: zeros)


def call(kernel, grid, inputs, outputs, scratch=(), cost=0, limit=16, after=()):
    arrays = [array for array, spec in inputs]
    specs = [spec for array, spec in inputs]
    aliases = {}
    for place, (shape, dtype, spec, buffer) in enumerate(outputs):
        if buffer is not None:
            aliases[len(arrays)] = place
            arrays.append(buffer)
            specs.append(pl.BlockSpec(memory_space=pl.ANY))
    for array in after:
        arrays.append(array)
        specs.append(pl.BlockSpec(memory_space=pl.ANY))
    given, extra = len(inputs), len(aliases) + len(after)

    def body(*refs):
        kernel(*refs[:given], *refs[given + extra :])

    return pl.pallas_call(
        body,
        **({} if grid is None else {"grid": grid}),
        in_specs=specs,
        out_specs=[spec for shape, dtype, spec, buffer in outputs],
        out_shape=[
            jax.ShapeDtypeStruct(shape, dtype) for shape, dtype, spec, buffer in outputs
        ],
        scratch_shapes=list(scratch),
        input_output_aliases=aliases,
        compiler_params=pltpu.CompilerParams(vmem_limit_bytes=limit * MIB),
        cost_estimate=pl.CostEstimate(flops=cost * 4000000000, bytes_accessed=1, transcendentals=0),
    )(*arrays)


def gather_kernel(*refs):
    sources, (rows_ref, turned_ref) = refs[:-2], refs[-2:]
    for place, source in enumerate(sources):
        tile = source[...]
        rows_ref[place] = tile
        turned_ref[place] = tile.astype(F32).T.astype(BF16)


def split_pairs(pair_block, target, head_count):
    lanes = lax.broadcasted_iota(jnp.int32, (CHUNK, 2 * HEAD_DIM), 1)
    low_half = lanes < HEAD_DIM
    for head in range(head_count):
        pair = pair_block[:, (head // 2) * 128 : (head // 2) * 128 + 128]
        keep = low_half if head % 2 == 0 else jnp.logical_not(low_half)
        target[head * CHUNK : (head + 1) * CHUNK, :] = jnp.where(keep, pair, jnp.zeros_like(pair))


def attend_kernel(
    head_count,
    layer,
    place,
    bits_ref,
    q_ref,
    kv_ref,
    turned_ref,
    q_label_ref,
    k_label_ref,
    out_weight_ref,
    context_ref,
    exact_ref,
    logsum_ref,
    share_ref,
    masked_q,
    total,
    top,
    mass,
    score_tiles,
):
    width = head_count * HEAD_DIM
    split_pairs(q_ref[...], masked_q, head_count)
    top[...] = jnp.full_like(top, NEG)
    mass[...] = jnp.zeros_like(mass)
    total[...] = jnp.zeros_like(total)
    tiles = kv_ref.shape[0]
    q_bits = bits_ref[tiles + place]

    def score_tile(tile, carry):
        @pl.when((bits_ref[tile] & q_bits) != 0)
        def _():
            hide = jnp.where(k_label_ref[tile] == q_label_ref[place], 0.0, NEG)
            hide = jnp.concatenate([hide, hide], 1)
            for pair in range(head_count // 2):
                lanes = slice(pair * 128, pair * 128 + 128)
                rows = slice(2 * pair * CHUNK, 2 * (pair + 1) * CHUNK)
                scores = dot(kv_ref[tile, :, lanes], masked_q[rows, :], 1, 1) + hide
                score_tiles[pair, tile] = scores
                highest = jnp.max(scores.reshape(-1, 8, 2 * CHUNK), 0)
                top[pair] = jnp.maximum(top[pair], highest)

        return carry

    lax.fori_loop(0, tiles, score_tile, 0)
    for pair in range(head_count // 2):
        top[pair] = jnp.broadcast_to(jnp.max(top[pair], 0, keepdims=True), (8, 2 * CHUNK))

    def weigh_tile(tile, carry):
        @pl.when((bits_ref[tile] & q_bits) != 0)
        def _():
            for pair in range(head_count // 2):
                weights = jnp.exp(score_tiles[pair, tile] - top[pair, 0:1, :])
                mass[pair] += jnp.sum(weights.reshape(-1, 8, 2 * CHUNK), 0)
                low = weights.astype(BF16)
                for side in range(2):
                    start = (2 * pair + side) * HEAD_DIM
                    total[start : start + HEAD_DIM, :] += dot(
                        turned_ref[tile, width + start : width + start + HEAD_DIM, :],
                        low[:, side * CHUNK : (side + 1) * CHUNK],
                    )

        return carry

    lax.fori_loop(0, tiles, weigh_tile, 0)
    logsum_ref[...] = jnp.zeros_like(logsum_ref)
    for head in range(head_count):
        rows = slice(head * HEAD_DIM, (head + 1) * HEAD_DIM)
        lanes = slice((head % 2) * CHUNK, (head % 2 + 1) * CHUNK)
        amount = jnp.sum(mass[head // 2][:, lanes], 0, keepdims=True)
        total[rows, :] = total[rows, :] / amount
        logsum_ref[head : head + 1, :] = top[head // 2, 0:1, lanes] + jnp.log(amount)
    exact = total[...].T
    exact_ref[...] = exact
    context = exact.astype(BF16)
    context_ref[...] = context
    share_ref[...] = dot(context, out_weight_ref[layer]).astype(BF16)


def attend_back_kernel(pair, head_count, chunks, *refs):
    bits_ref, kv_ref, turned_ref, q_label_ref, k_label_ref = refs[:5]
    q_refs, grad_refs, exact_refs, logsum_refs = (
        refs[5 + chunks * k : 5 + chunks * (k + 1)] for k in range(4)
    )
    q_grad_ref, own_ref, other_ref, masked_q, masked_grad, centre, q_total, kv_total = refs[
        5 + 4 * chunks :
    ]
    tiles = kv_ref.shape[0]
    lanes = slice(pair * 128, pair * 128 + 128)
    v_lanes = slice(head_count * HEAD_DIM + pair * 128, head_count * HEAD_DIM + pair * 128 + 128)
    kv_total[...] = jnp.zeros_like(kv_total)
    for place in range(chunks):
        split_pairs(q_refs[place][:, lanes], masked_q, 2)
        split_pairs(grad_refs[place][:, lanes], masked_grad, 2)
        crossed = (grad_refs[place][:, lanes].astype(F32) * exact_refs[place][:, lanes]).T
        for head in range(2):
            rows = slice(head * HEAD_DIM, (head + 1) * HEAD_DIM)
            side = slice(head * CHUNK, (head + 1) * CHUNK)
            number = 2 * pair + head
            centre[0:1, side] = jnp.sum(crossed[rows, :], 0, keepdims=True)
            centre[2:3, side] = logsum_refs[place][number : number + 1, :]
        q_total[...] = jnp.zeros_like(q_total)
        q_bits = bits_ref[tiles + place]

        def one_tile(tile, carry):
            @pl.when((bits_ref[tile] & q_bits) != 0)
            def _():
                hide = jnp.where(k_label_ref[tile] == q_label_ref[place], 0.0, NEG)
                hide = jnp.concatenate([hide, hide], 1)
                scores = dot(kv_ref[tile, :, lanes], masked_q[...], 1, 1) + hide
                weight_grad = dot(kv_ref[tile, :, v_lanes], masked_grad[...], 1, 1)
                weights = jnp.exp(scores - centre[2:3, :])
                score_grad = (weights * (weight_grad - centre[0:1, :])).astype(BF16)
                kv_total[tile, :, 128:] += dot(weights.astype(BF16), masked_grad[...])
                kv_total[tile, :, :128] += dot(score_grad, masked_q[...])
                for side in range(2):
                    rows = slice(side * HEAD_DIM, (side + 1) * HEAD_DIM)
                    turned = slice((2 * pair + side) * HEAD_DIM, (2 * pair + side + 1) * HEAD_DIM)
                    q_total[rows, :] += dot(
                        turned_ref[tile, turned, :],
                        score_grad[:, side * CHUNK : (side + 1) * CHUNK],
                    )

            return carry

        lax.fori_loop(0, tiles, one_tile, 0)
        q_grad_ref[place * CHUNK : (place + 1) * CHUNK, :] = q_total[...].T.astype(
            BF16
        ) * jnp.asarray(HEAD_DIM**-0.5, BF16)
    own_ref[...] = kv_total[: tiles // 2]
    other_ref[...] = kv_total[tiles // 2 :].astype(BF16)


def weight_grad_kernel(chunks, left_start, right_start, *refs):
    lefts, rights, recv_refs = refs[:chunks], refs[chunks : 2 * chunks], refs[2 * chunks : -1]
    out_ref = refs[-1]
    rows, columns = out_ref.shape
    step = CHUNK if rows % CHUNK == 0 else rows
    for start in range(0, rows, step):
        left_lanes = slice(left_start + start, left_start + start + step)
        right_lanes = slice(right_start, right_start + columns)
        total = None
        for left, right in zip(lefts, rights):
            part = dot(left[:, left_lanes], right[:, right_lanes], 0, 0)
            total = part if total is None else total + part
        for recv_ref in recv_refs:
            total = total + recv_ref[start : start + step, :].astype(F32)
        out_ref[start : start + step, :] = total.astype(out_ref.dtype)


def out_grad_kernel(chunks, core_ref, *refs):
    lefts, rights, (own_ref, other_ref, full) = refs[:chunks], refs[chunks:-3], refs[-3:]
    total = None
    for left, right in zip(lefts, rights):
        part = dot(left[...], right[...], 0, 0)
        total = part if total is None else total + part
    full[...] = total
    local = own_ref.shape[0]
    own_ref[...] = full[pl.ds(pl.multiple_of(core_ref[0] * local, local), local), :]
    other_ref[...] = full[pl.ds(pl.multiple_of((1 - core_ref[0]) * local, local), local), :].astype(
        BF16
    )


def feed_kernel(
    layer,
    place,
    unit_ref,
    share_ref,
    recv_ref,
    vec_ref,
    up_own_ref,
    up_other_ref,
    bias_ref,
    down_own_ref,
    down_other_ref,
    new_unit_ref,
    inverse_ref,
    low_ref,
    act_ref,
    slope_ref,
    part_ref,
):
    stream = unit_ref[...] * vec_ref[layer, 6:7, :] + vec_ref[layer, 7:8, :]
    attention = share_ref[...].astype(F32) + recv_ref[...].astype(F32)
    unit, inverse = norm_parts(stream + attention + vec_ref[layer, 0:1, :])
    new_unit_ref[...] = unit
    inverse_ref[...] = inverse
    low_ref[...] = (unit * vec_ref[layer, 1:2, :] + vec_ref[layer, 2:3, :]).astype(BF16)
    units = up_own_ref.shape[2]
    total = None
    for half, (up_ref, down_ref) in enumerate(
        ((up_own_ref, down_own_ref), (up_other_ref, down_other_ref))
    ):
        lanes = slice(half * units, (half + 1) * units)
        act, slope = gelu_parts(dot(low_ref[...], up_ref[layer]) + bias_ref[layer, :, lanes])
        low_act = act.astype(BF16)
        act_ref[:, lanes] = low_act
        slope_ref[:, lanes] = slope.astype(BF16)
        part = dot(low_act, down_ref[layer])
        total = part if total is None else total + part
    part_ref[...] = total.astype(BF16)


def project_kernel(
    layer,
    place,
    unit_ref,
    share_ref,
    recv_ref,
    vec_ref,
    q_weight_ref,
    kv_weight_ref,
    q_bias_ref,
    kv_bias_ref,
    new_unit_ref,
    inverse_ref,
    low_ref,
    q_ref,
    kv_ref,
):
    old = layer - 1
    middle = unit_ref[...] * vec_ref[old, 1:2, :] + vec_ref[old, 2:3, :]
    feed = share_ref[...].astype(F32) + recv_ref[...].astype(F32)
    unit, inverse = norm_parts(middle + feed + vec_ref[old, 3:4, :])
    new_unit_ref[...] = unit
    inverse_ref[...] = inverse
    low = (unit * vec_ref[old, 4:5, :] + vec_ref[old, 5:6, :]).astype(BF16)
    low_ref[...] = low
    kv_ref[...] = (dot(low, kv_weight_ref[layer], 1, 1) + kv_bias_ref[layer]).astype(BF16)
    q_ref[...] = (
        (dot(low, q_weight_ref[layer], 1, 1) + q_bias_ref[layer]) * HEAD_DIM**-0.5
    ).astype(BF16)


def feed_back_kernel(
    layer,
    place,
    top_layer,
    up_ref,
    unit_ref,
    inverse_ref,
    share_ref,
    recv_ref,
    vec_ref,
    slope_ref,
    up_own_ref,
    up_other_ref,
    down_own_ref,
    down_other_ref,
    *rest,
):
    before = rest[:-7]
    encoded_ref, total_ref, low_ref, grad_ref, bias_ref, sums_ref, part_ref = rest[-7:]
    keep_span = slice(place * CHUNK, (place + 1) * CHUNK)
    added = share_ref[...].astype(F32) + recv_ref[...].astype(F32)
    if top_layer:
        middle = unit_ref[...] * vec_ref[layer, 1:2, :] + vec_ref[layer, 2:3, :]
        unit, inverse = norm_parts(middle + added + vec_ref[layer, 3:4, :])
        encoded_ref[...] = (unit * vec_ref[layer, 4:5, :] + vec_ref[layer, 5:6, :]).astype(BF16)
        upstream = up_ref[keep_span, :].astype(F32)
    else:
        unit = unit_ref[...]
        inverse = inverse_ref[...]
        upstream = up_ref[...] + added
        encoded_ref[...] = jnp.zeros_like(encoded_ref)
    second = norm_back(upstream, unit, inverse, vec_ref[layer, 4:5, :])
    sums_ref[...] = before[0][...] if before else jnp.zeros_like(sums_ref)
    sums_ref[0:1, :] += jnp.sum(upstream * unit, 0, keepdims=True)
    sums_ref[1:2, :] += jnp.sum(upstream, 0, keepdims=True)
    sums_ref[2:3, :] += jnp.sum(second, 0, keepdims=True)
    total_ref[...] = second
    low_ref[...] = second.astype(BF16)
    units = up_own_ref.shape[2]
    total = None
    for half, (up_weight_ref, down_ref) in enumerate(
        ((up_own_ref, down_own_ref), (up_other_ref, down_other_ref))
    ):
        lanes = slice(half * units, (half + 1) * units)
        grad = (
            dot(low_ref[...], down_ref[layer], 1, 1) * slope_ref[:, lanes].astype(F32)
        ).astype(BF16)
        grad_ref[:, lanes] = grad
        bias = jnp.sum(grad.astype(F32), 0, keepdims=True)
        bias_ref[:, lanes] = bias + before[1][:, lanes] if before else bias
        part = dot(grad, up_weight_ref[layer], 1, 1)
        total = part if total is None else total + part
    part_ref[...] = total.astype(BF16)


def context_back_kernel(
    layer,
    place,
    second_ref,
    share_ref,
    recv_ref,
    unit_ref,
    inverse_ref,
    vec_ref,
    out_weight_ref,
    *rest,
):
    before = rest[:-4]
    total_ref, low_ref, grad_ref, sums_ref = rest[-4:]
    added = share_ref[...].astype(F32) + recv_ref[...].astype(F32)
    upstream = second_ref[...] + added
    unit = unit_ref[...]
    first = norm_back(upstream, unit, inverse_ref[...], vec_ref[layer, 1:2, :])
    sums_ref[...] = before[0][...] if before else jnp.zeros_like(sums_ref)
    sums_ref[0:1, :] += jnp.sum(upstream * unit, 0, keepdims=True)
    sums_ref[1:2, :] += jnp.sum(upstream, 0, keepdims=True)
    sums_ref[2:3, :] += jnp.sum(first, 0, keepdims=True)
    total_ref[...] = first
    low = first.astype(BF16)
    low_ref[...] = low
    grad_ref[...] = dot(low, out_weight_ref[layer], 1, 1).astype(BF16)


def joint_back_kernel(
    layer,
    place,
    core_ref,
    *refs,
):
    pairs = (len(refs) - 6) // 3
    q_refs, own_refs, recv_refs = (refs[k * pairs : (k + 1) * pairs] for k in range(3))
    q_weight_ref, kv_weight_ref, mine_ref, theirs_ref, bias_ref, part_ref = refs[3 * pairs :]
    span = slice(place * CHUNK, (place + 1) * CHUNK)
    width = 128 * pairs
    local = width // 2
    q_grad = jnp.concatenate([ref[span, :] for ref in q_refs], 1)
    both = [
        (own[place] + recv[place].astype(F32)).astype(BF16)
        for own, recv in zip(own_refs, recv_refs)
    ]
    kv_grad = jnp.concatenate(
        [part[:, :128] for part in both] + [part[:, 128:] for part in both], 1
    )
    first = core_ref[0] == 0
    for member, value in enumerate((q_grad, kv_grad[:, :width], kv_grad[:, width:])):
        left, right = value[:, :local].astype(F32), value[:, local:].astype(F32)
        lanes = slice(member * local, (member + 1) * local)
        mine_ref[:, lanes] = jnp.where(first, left, right).astype(BF16)
        theirs_ref[:, lanes] = jnp.where(first, right, left).astype(BF16)
    bias_ref[...] = jnp.zeros_like(bias_ref)
    bias_ref[0:1, :] = jnp.sum(q_grad.astype(F32), 0, keepdims=True)
    bias_ref[1:2, :] = jnp.sum(kv_grad[:, width:].astype(F32), 0, keepdims=True)
    part_ref[...] = (
        dot(q_grad, q_weight_ref[layer]) + dot(kv_grad, kv_weight_ref[layer])
    ).astype(BF16)


def weights_kernel(core_ref, *refs):
    sources, vectors, small_ref, other_ref = refs[:8], refs[8:14], refs[14], refs[15]
    q_ref, kv_ref, out_ref, vec_ref, q_bias_ref, kv_bias_ref, unit_bias_ref = refs[16:]
    local = sources[0].shape[1]
    width = 2 * local
    own_row = pl.multiple_of(core_ref[0] * local, local)
    other_row = pl.multiple_of((1 - core_ref[0]) * local, local)
    for layer in range(LAYERS):
        for member, (target, start) in enumerate(
            ((q_ref, 0), (kv_ref, 0), (kv_ref, width), (out_ref, 0))
        ):
            target[layer, pl.ds(start + own_row, local), :] = sources[2 * member][layer]
            target[layer, pl.ds(start + other_row, local), :] = sources[2 * member + 1][layer]

    first = core_ref[0] == 0
    for layer in range(LAYERS):
        row = slice(layer, layer + 1)
        for member, vector in enumerate(vectors):
            vec_ref[layer, member : member + 1, :] = vector[...].astype(F32)[row]
        if layer == 0:
            vec_ref[layer, 6:7, :] = jnp.ones_like(vec_ref[layer, 6:7, :])
            vec_ref[layer, 7:8, :] = jnp.zeros_like(vec_ref[layer, 7:8, :])
        else:
            vec_ref[layer, 6:8, :] = vec_ref[layer - 1, 4:6, :]
        own = small_ref[...].astype(F32)[row]
        other = other_ref[...].astype(F32)[row]
        kv_bias_ref[layer] = jnp.zeros_like(kv_bias_ref[layer])
        for target, start, lanes in (
            (q_bias_ref, 0, slice(0, local)),
            (kv_bias_ref, width, slice(local, width)),
        ):
            left, right = own[:, lanes], other[:, lanes]
            target[layer, :, start : start + local] = jnp.where(first, left, right)
            target[layer, :, start + local : start + width] = jnp.where(first, right, left)
        units = own.shape[1] - width
        unit_bias_ref[layer, :, :units] = own[:, width:]
        unit_bias_ref[layer, :, units:] = other[:, width:]


def halve_kernel(bit, numbers_ref, *refs):
    parts, (sent_ref, kept_ref) = refs[:-2], refs[-2:]
    half = sent_ref.shape[0]
    for target, number in ((sent_ref, 1 - numbers_ref[bit]), (kept_ref, numbers_ref[bit])):
        rows = pl.ds(pl.multiple_of(number * half, half), half)
        target[...] = sum(part[rows, :].astype(F32) for part in parts).astype(target.dtype)


def add_kernel(kept_ref, recv_ref, piece_ref):
    piece_ref[0] = (kept_ref[...] + recv_ref[...].astype(F32)).astype(BF16)


def join_kernel(pieces_ref, recv_ref, joined_ref):
    count = pieces_ref.shape[0]
    joined_ref[:count] = pieces_ref[...]
    joined_ref[count:] = recv_ref[...]


def arrange(place, pieces_ref, recv_ref, full):
    count, rows = pieces_ref.shape[0], pieces_ref.shape[1]
    for number in range(2 * count):
        source = pieces_ref[number] if number < count else recv_ref[number - count]
        start = pl.multiple_of((number ^ place) * rows, rows)
        full[pl.ds(start, rows), :] = source.astype(F32)


def unpack_kernel(place, numbers_ref, pieces_ref, recv_ref, *refs):
    targets, full = refs[:-1], refs[-1]
    arrange(numbers_ref[place], pieces_ref, recv_ref, full)
    start = 0
    for target in targets:
        rows = target.shape[-2]
        value = full[start : start + rows, :]
        if len(target.shape) == 3:
            target[0] = value
        else:
            target[...] = value.astype(target.dtype)
        start += rows


def vectors_unpack_kernel(place, numbers_ref, pieces_ref, recv_ref, *refs):
    q_ref, table_ref, targets, full = refs[0], refs[1], refs[2:-1], refs[-1]
    arrange(numbers_ref[place], pieces_ref, recv_ref, full)
    local = q_ref.shape[1]
    half = table_ref.shape[0]
    q_ref[0] = full[:local, :]
    table_ref[...] = full[local : local + half, :].astype(BF16)
    for layer in range(LAYERS):
        start = local + half + 8 * layer
        row = slice(layer, layer + 1)
        for member in range(7):
            targets[member][row, :] = full[start + member : start + member + 1, :]
        last = full[start + 7 : start + 8, :]
        for member in range(2):
            targets[7 + member][row, :] = last[:, member * local : (member + 1) * local]


def table_kernel(chunks, share, numbers_ref, bucket_ref, *refs):
    joints, firsts = refs[:chunks], refs[chunks : 2 * chunks]
    vectors = refs[2 * chunks : -3]
    mine_ref, sent_ref, full = refs[-3:]
    buckets, half = full.shape[0], full.shape[0] // 2
    chip, core = numbers_ref[1], numbers_ref[0]
    numbers = lax.broadcasted_iota(jnp.int32, (buckets, CHUNK), 0)
    places = lax.broadcasted_iota(jnp.int32, (buckets, CHUNK), 1)
    total = None
    for place in range(chunks):
        hit = numbers == bucket_ref[place]
        rows = places + place * CHUNK
        mine = jnp.logical_and(rows >= chip * share, rows < (chip + 1) * share)
        every = jnp.where(hit, 1.0, 0.0).astype(BF16)
        own = jnp.where(jnp.logical_and(hit, mine), 1.0, 0.0).astype(BF16)
        first = firsts[place][...]
        high = first.astype(BF16)
        rest = (first - high.astype(F32)).astype(BF16)
        part = dot(every, joints[place][...]) + (dot(own, high) + dot(own, rest))
        total = part if total is None else total + part
    full[...] = total
    mine_ref[:half, :] = full[pl.ds(pl.multiple_of(core * half, half), half), :]
    sent_ref[:half, :] = full[pl.ds(pl.multiple_of((1 - core) * half, half), half), :].astype(BF16)
    for layer in range(LAYERS):
        rows = slice(half + 8 * layer, half + 8 * layer + 8)
        mine_ref[rows, :] = vectors[2 * layer][...]
        sent_ref[rows, :] = vectors[2 * layer + 1][...].astype(BF16)


def vectors_kernel(numbers_ref, second_ref, first_ref, unit_ref, *refs):
    mine_ref, sent_ref = refs[-2:]
    second, first, unit = second_ref[...], first_ref[...], unit_ref[...]
    bias = sum(ref[...] for ref in refs[:-2])
    units, local = unit.shape[1] // 2, bias.shape[1] // 2
    low = numbers_ref[0] == 0
    for target, lanes, flip in (
        (mine_ref, slice(0, units), False),
        (sent_ref, slice(units, 2 * units), True),
    ):
        target[0:3, :] = second[0:3, :]
        target[3:6, :] = first[0:3, :]
        target[6:7, :] = unit[:, lanes]
        target[7:8, :] = jnp.zeros_like(target[7:8, :])
        for member in range(2):
            left, right = bias[member : member + 1, :local], bias[member : member + 1, local:]
            if flip:
                left, right = right, left
            target[7:8, member * local : (member + 1) * local] = jnp.where(low, left, right)


def table_add_kernel(mine_ref, recv_ref, both_ref, sent_ref):
    total = mine_ref[...] + recv_ref[...].astype(F32)
    both_ref[...] = total
    sent_ref[...] = total[: sent_ref.shape[0], :].astype(BF16)


def pack_kernel(q_ref, both_ref, sent_ref, recv_ref, packed_ref):
    local, half, rows = q_ref.shape[0], sent_ref.shape[0], both_ref.shape[0]
    packed_ref[...] = jnp.zeros_like(packed_ref)
    packed_ref[:local, :] = q_ref[...]
    table = sent_ref[...].astype(F32) + recv_ref[...].astype(F32)
    packed_ref[local : local + half, :] = table.astype(BF16)
    packed_ref[local + half : local + rows, :] = both_ref[half:, :].astype(BF16)


def pile_kernel(*refs):
    sources, target = refs[:-1], refs[-1]
    start = 0
    for source in sources:
        rows = source.shape[0]
        target[start : start + rows, :] = source[...].astype(target.dtype)
        start += rows
    if start < target.shape[0]:
        target[start:, :] = jnp.zeros_like(target[start:, :])


def pick_rows(chip, chunk_refs, share, target):
    for number in range(2):

        @pl.when(chip == number)
        def _():
            start, end = number * share, (number + 1) * share
            for place, ref in enumerate(chunk_refs):
                low, high = max(start, place * CHUNK), min(end, (place + 1) * CHUNK)
                if low < high:
                    target[low - start : high - start, :] = ref[
                        low - place * CHUNK : high - place * CHUNK, :
                    ]


def own_rows_kernel(numbers_ref, *refs):
    pick_rows(numbers_ref[1], refs[:-1], refs[-1].shape[0], refs[-1])


def tokens_send_kernel(numbers_ref, *refs):
    pick_rows(1 - numbers_ref[1], refs[:-1], refs[-1].shape[0], refs[-1])


def tokens_kernel(chunks, numbers_ref, *refs):
    joints, firsts = refs[:chunks], refs[chunks : 2 * chunks]
    recv_ref, target, own = refs[2 * chunks :]
    share = target.shape[0]
    pick_rows(numbers_ref[1], joints, share, own)
    pick_rows(numbers_ref[1], firsts, share, target)
    target[...] += own[...].astype(F32) + recv_ref[...].astype(F32)


class Wide:
    BITS = {"y": (2, 1), "near": (3, 2), "far": (4, 4)}
    PLACES = {("y", "near", "far"): 5, ("near", "y", "far"): 6}

    def __init__(self, size, chip, core):
        self.small, self.size = size == 8, size
        index = lax.axis_index("wide")
        bits = {name: (index >> k) & 1 for k, name in enumerate(("y", "near", "far"))}
        places = [
            sum(bits[name] << (2 - k) for k, name in enumerate(order)) if self.small else 0
            for order in self.PLACES
        ]
        self.numbers = jnp.stack(
            [
                jnp.asarray(value, jnp.int32)
                for value in (core, chip, bits["y"], bits["near"], bits["far"], *places, 0)
            ]
        )

    def pairs(self, name):
        reach = self.BITS[name][1]
        return [(number, number ^ reach) for number in range(self.size)]


def gate(value, *later):
    return lax.optimization_barrier((value,) + later)[0] if later else value


SMEM = pl.BlockSpec(memory_space=pltpu.SMEM)


class Chain:
    def __init__(self, wide, value, order):
        self.wide, self.order, self.step = wide, order, 0
        self.parts, self.rows = [value], value.shape[0]

    def advance(self, *after):
        if not self.wide.small:
            if self.step == 0:
                value = self.parts[0]
                self.parts = lax.psum(value, "wide").reshape(2, 4, -1, value.shape[1])
            self.step = 6
            self.sent = self.parts[0]
            return self.parts[0]
        self.step += 1
        parts = [(part, ON_CHIP) for part in self.parts]
        columns = self.parts[0].shape[-1]
        if self.step <= 3:
            name = self.order[self.step - 1]
            half = (self.parts[0].shape[0] // 2, columns)
            sent, kept = call(
                functools.partial(halve_kernel, Wide.BITS[name][0]),
                None,
                [(self.wide.numbers, SMEM)] + parts,
                [(half, BF16, ON_CHIP, None), (half, F32, ON_CHIP, None)],
                after=after,
            )
            self.parts = [kept, lax.ppermute(sent, "wide", self.wide.pairs(name))]
            self.sent = sent
            return sent
        kernel = add_kernel if self.step == 4 else join_kernel
        shape = self.parts[0].shape
        shape = (1,) + shape if self.step == 4 else (2 * shape[0],) + shape[1:]
        (sent,) = call(kernel, None, parts, [(shape, BF16, ON_CHIP, None)], after=after)
        name = self.order[6 - self.step]
        self.parts = [sent, lax.ppermute(sent, "wide", self.wide.pairs(name))]
        return sent

    def finish(self):
        while self.step < 6:
            self.advance()
        return [self.parts[0], self.parts[1]]


def on_device(wide, *arguments):
    (
        tokens,
        buckets,
        lengths,
        type_table,
        query_weight,
        query_bias,
        key_weight,
        value_weight,
        value_bias,
        output_weight,
        output_bias,
        attention_gain,
        attention_shift,
        up_weight,
        up_bias,
        down_weight,
        down_bias,
        feed_gain,
        feed_shift,
        cotangent,
    ) = arguments
    share, model = tokens.shape
    lane = 2 * share
    chunks = lane // CHUNK
    local = query_weight.shape[2]
    width = 2 * local
    head_count = width // HEAD_DIM
    units = up_weight.shape[2]
    place = lax.axis_index("narrow")
    chip, core = place // 2, place % 2
    first_chip, first_core = chip == 0, core == 0

    def by_core(own, other, axis):
        return jnp.where(
            first_core,
            jnp.concatenate([own, other], axis),
            jnp.concatenate([other, own], axis),
        )

    def by_chip(own, other):
        return jnp.where(
            first_chip, jnp.concatenate([own, other], 0), jnp.concatenate([other, own], 0)
        )

    def own_rows(rows):
        return jnp.where(first_chip, rows[:share], rows[share:])

    def other_rows(rows):
        return jnp.where(first_chip, rows[share:], rows[:share])

    lane_tokens = by_chip(tokens, over_chip(tokens))
    lane_buckets = by_chip(buckets, over_chip(buckets))
    lane_cotangent = by_chip(cotangent, over_chip(cotangent))

    smem = pl.BlockSpec(memory_space=pltpu.SMEM)
    sums = Wide(wide, chip, core)
    core_number = sums.numbers
    shards = []
    turned_weights = [
        jnp.swapaxes(weight, 1, 2) for weight in (query_weight, key_weight, value_weight)
    ]
    for weight in turned_weights + [output_weight]:
        shards += [(weight, ON_CHIP), (over_core(weight), ON_CHIP)]

    small = jnp.concatenate([query_bias, value_bias, up_bias], 1)
    vectors = [
        output_bias,
        attention_gain,
        attention_shift,
        down_bias,
        feed_gain,
        feed_shift,
        small,
        over_core(small),
    ]
    qw, kvw, ow, vec, q_bias, kv_bias, unit_bias = call(
        weights_kernel,
        None,
        [(core_number, smem)] + shards + [(vector, ON_CHIP) for vector in vectors],
        [
            (shape, dtype, ON_CHIP, None)
            for shape, dtype in (
                ((LAYERS, width, model), BF16),
                ((LAYERS, 2 * width, model), BF16),
                ((LAYERS, width, model), BF16),
                ((LAYERS, 8, model), F32),
                ((LAYERS, 1, width), F32),
                ((LAYERS, 1, 2 * width), F32),
                ((LAYERS, 1, 2 * units), F32),
            )
        ],
    )
    up_other = over_core(up_weight)
    down_other = over_core(down_weight)

    ends = jnp.cumsum(lengths[0], dtype=jnp.int32)
    offsets = lax.iota(jnp.int32, share)
    spots = jnp.concatenate(
        [
            offsets + (block * 2 + which) * share
            for which in (core, 1 - core)
            for block in range(2)
        ]
    )
    labels = jnp.sum((spots[:, None] >= ends[None, :]).astype(jnp.int32), 1, dtype=jnp.int32)
    tiles = 2 * chunks
    tile_labels = labels.reshape(tiles, CHUNK)
    present = jnp.any(
        tile_labels[:, :, None] == lax.iota(jnp.int32, lengths.shape[1])[None, None, :], axis=1
    )
    bits = jnp.sum(
        jnp.where(present, jnp.left_shift(1, lax.iota(jnp.int32, lengths.shape[1]))[None, :], 0),
        axis=1,
        dtype=jnp.int32,
    )
    bits = jnp.concatenate([bits, bits[:chunks]])
    k_labels = tile_labels[:, :, None]
    q_labels = tile_labels[:chunks, None, :]

    block = (CHUNK, model)

    def layer_spec(layer, shape):
        return pl.BlockSpec((1,) + shape, lambda *ids: (layer,) + (0,) * len(shape))

    selector = (lane_buckets[:, None] == lax.iota(jnp.int32, type_table.shape[0])[None, :]).astype(
        BF16
    )
    stream = lane_tokens.astype(F32) + dot(selector, type_table)
    low_first = stream.astype(BF16)
    state = [stream[CHUNK * i : CHUNK * (i + 1)] for i in range(chunks)]
    kept = []
    for layer in range(LAYERS):
        keep = {}
        if layer == 0:
            kv = (dot(low_first, kvw[0], 1, 1) + kv_bias[0]).astype(BF16)
            queries = ((dot(low_first, qw[0], 1, 1) + q_bias[0]) * HEAD_DIM**-0.5).astype(BF16)
            low_in, kv, queries = (
                [value[CHUNK * i : CHUNK * (i + 1)] for i in range(chunks)]
                for value in (low_first, kv, queries)
            )
            kv_other = [over_core(part) for part in kv]
        else:
            low_in, queries, kv, kv_other = [], [], [], []
            units_now, inverses = [], []
            for i in range(chunks):
                outs = call(
                    functools.partial(project_kernel, layer, i),
                    None,
                    [
                        (value, ON_CHIP)
                        for value in (
                            state[i],
                            feed_share[i],
                            feed_recv[i],
                            vec,
                            qw,
                            kvw,
                            q_bias,
                            kv_bias,
                        )
                    ],
                    [
                        (block, F32, ON_CHIP, None),
                        ((CHUNK, 1), F32, ON_CHIP, None),
                        (block, BF16, ON_CHIP, None),
                        ((CHUNK, width), BF16, ON_CHIP, None),
                        ((CHUNK, 2 * width), BF16, ON_CHIP, None),
                    ],
                    cost=2,
                )
                units_now.append(outs[0])
                inverses.append(outs[1])
                low_in.append(outs[2])
                queries.append(outs[3])
                kv.append(outs[4])
                kv_other.append(over_core(outs[4]))
            state = units_now
            kept[layer - 1]["second_unit"] = units_now
            kept[layer - 1]["second_inverse"] = inverses
        kv_all, turned = call(
            gather_kernel,
            None,
            [(part, ON_CHIP) for part in kv + kv_other],
            [
                ((tiles, CHUNK, 2 * width), BF16, ON_CHIP, None),
                ((tiles, 2 * width, CHUNK), BF16, ON_CHIP, None),
            ],
            cost=2,
        )
        context, exact, logsum, shares = [], [], [], []
        for i in range(chunks):
            outs = call(
                functools.partial(attend_kernel, head_count, layer, i),
                None,
                [(bits, smem)]
                + [
                    (value, ON_CHIP)
                    for value in (queries[i], kv_all, turned, q_labels, k_labels, ow)
                ],
                [
                    ((CHUNK, width), BF16, ON_CHIP, None),
                    ((CHUNK, width), F32, ON_CHIP, None),
                    ((8, CHUNK), F32, ON_CHIP, None),
                    (block, BF16, ON_CHIP, None),
                ],
                scratch=[
                    pltpu.VMEM((head_count * CHUNK, 128), BF16),
                    pltpu.VMEM((width, CHUNK), F32),
                    pltpu.VMEM((head_count // 2, 8, 2 * CHUNK), F32),
                    pltpu.VMEM((head_count // 2, 8, 2 * CHUNK), F32),
                    pltpu.VMEM((head_count // 2, tiles, CHUNK, 2 * CHUNK), F32),
                ],
                cost=6,
                limit=20,
            )
            for target, value in zip((context, exact, logsum, shares), outs):
                target.append(value)
        received = [over_chip(part) for part in shares]
        low_middle, act, slope, first_unit, first_inverse, feed_share = [], [], [], [], [], []
        for i in range(chunks):
            outs = call(
                functools.partial(feed_kernel, layer, i),
                None,
                [
                    (value, ON_CHIP)
                    for value in (
                        state[i],
                        shares[i],
                        received[i],
                        vec,
                        up_weight,
                        up_other,
                        unit_bias,
                        down_weight,
                        down_other,
                    )
                ],
                [
                    (block, F32, ON_CHIP, None),
                    ((CHUNK, 1), F32, ON_CHIP, None),
                    (block, BF16, ON_CHIP, None),
                    ((CHUNK, 2 * units), BF16, ON_CHIP, None),
                    ((CHUNK, 2 * units), BF16, ON_CHIP, None),
                    (block, BF16, ON_CHIP, None),
                ],
                cost=8,
            )
            for target, value in zip(
                (first_unit, first_inverse, low_middle, act, slope, feed_share), outs
            ):
                target.append(value)
        feed_recv = [over_chip(part) for part in feed_share]
        state = first_unit
        keep.update(
            low_in=low_in,
            queries=queries,
            kv_all=kv_all,
            turned=turned,
            context=context,
            exact=exact,
            logsum=logsum,
            first_unit=first_unit,
            first_inverse=first_inverse,
            low_middle=low_middle,
            act=act,
            slope=slope,
        )
        kept.append(keep)

    pair_order, other_order = ("y", "near", "far"), ("near", "y", "far")

    def unpacked(kernel, layer, sources, shapes, buffers, scratch=(), after=()):
        return call(
            kernel,
            (1,),
            [(source, smem if source is sums.numbers else whole(source.shape)) for source in sources],
            [
                ((LAYERS,) + shape, F32, layer_spec(layer, shape), buffer)
                for shape, buffer in zip(shapes, buffers)
            ],
            scratch,
            after=after,
        )

    def unpacked_rows(layer, chain, shapes, buffers, after=()):
        return unpacked(
            functools.partial(unpack_kernel, Wide.PLACES[chain.order]),
            layer,
            [sums.numbers] + chain.finish(),
            shapes,
            buffers,
            [pltpu.VMEM((chain.rows, model), F32)],
            after,
        )

    def piled(rows, *values):
        return call(
            pile_kernel,
            None,
            [(value, ON_CHIP) for value in values],
            [((rows, model), BF16, ON_CHIP, None)],
        )[0]

    vector_sums = [None] * LAYERS
    encoded = []
    for layer in reversed(range(LAYERS)):
        keep = kept[layer]
        top_layer = layer == LAYERS - 1
        second, low_second, up_grad, unit_sums, second_sums, parts = [], [], [], [], [], []
        for i in range(chunks):
            if top_layer:
                upstream = lane_cotangent
                unit = keep["first_unit"][i]
                inverse = keep["first_inverse"][i]
                added = (feed_share[i], feed_recv[i])
            else:
                upstream = first_total[i]
                unit = keep["second_unit"][i]
                inverse = keep["second_inverse"][i]
                added = (joint_share[i], joint_recv[i])
            outs = call(
                functools.partial(feed_back_kernel, layer, i, top_layer),
                None,
                [
                    (value, ON_CHIP)
                    for value in (
                        upstream,
                        unit,
                        inverse,
                        added[0],
                        added[1],
                        vec,
                        keep["slope"][i],
                        up_weight,
                        up_other,
                        down_weight,
                        down_other,
                        *second_sums[-1:],
                        *unit_sums[-1:],
                    )
                ],
                [
                    (block if top_layer else (8, 128), BF16, ON_CHIP, None),
                    (block, F32, ON_CHIP, None),
                    (block, BF16, ON_CHIP, None),
                    ((CHUNK, 2 * units), BF16, ON_CHIP, None),
                    ((1, 2 * units), F32, ON_CHIP, None),
                    ((8, model), F32, ON_CHIP, None),
                    (block, BF16, ON_CHIP, None),
                ],
                cost=0,
                after=(
                    []
                    if top_layer or i == 1
                    else [upper.advance(), feed_chain.advance(joint_share[2]), vector_sums[1][0]]
                    if i == 0
                    else []
                ),
            )
            if top_layer:
                encoded.append(outs[0])
            for target, value in zip(
                (second, low_second, up_grad, unit_sums, second_sums, parts), outs[1:]
            ):
                target.append(value)
        received = [over_chip(part) for part in parts]

        def weight_grad(lefts, rights, shape, left_start=0, right_start=0, received=()):
            return call(
                functools.partial(weight_grad_kernel, chunks, left_start, right_start),
                None,
                [(value, ON_CHIP) for value in [*lefts, *rights, *received]],
                [(shape, BF16, ON_CHIP, None)],
                cost=0,
            )[0]

        square = (model, units)
        down_other_grad = over_core(
            weight_grad(keep["act"], low_second, square[::-1], left_start=units)
        )
        up_other_grad = over_core(
            weight_grad(keep["low_middle"], up_grad, square, right_start=units)
        )
        down_grad = weight_grad(
            keep["act"], low_second, square[::-1], received=[down_other_grad]
        )
        up_weight_grad = weight_grad(
            keep["low_middle"], up_grad, square, received=[up_other_grad]
        )
        first_total, low_total, context_grad, first_sums = [], [], [], []
        if top_layer:
            (own_encoded,) = call(
                own_rows_kernel,
                (1,),
                [(sums.numbers, smem)] + [(part, whole(block)) for part in encoded],
                [((share, model), BF16, whole((share, model)), None)],
            )
        for i in range(chunks):
            outs = call(
                functools.partial(context_back_kernel, layer, i),
                None,
                [
                    (value, ON_CHIP)
                    for value in (
                        second[i],
                        parts[i],
                        received[i],
                        keep["first_unit"][i],
                        keep["first_inverse"][i],
                        vec,
                        ow,
                        *first_sums[-1:],
                    )
                ],
                [
                    (block, F32, ON_CHIP, None),
                    (block, BF16, ON_CHIP, None),
                    ((CHUNK, width), BF16, ON_CHIP, None),
                    ((8, model), F32, ON_CHIP, None),
                ],
                after=(
                    [own_encoded] * (top_layer and i == 0)
                    if top_layer or i != 1
                    else [upper.advance(second_sums[2]), feed_chain.advance(second_sums[2])]
                ),
            )
            for target, value in zip((first_total, low_total, context_grad, first_sums), outs):
                target.append(value)
        own, other = call(
            functools.partial(out_grad_kernel, chunks),
            None,
            [(core_number, smem)]
            + [(value, ON_CHIP) for value in keep["context"] + low_total],
            [((local, model), F32, ON_CHIP, None), ((local, model), BF16, ON_CHIP, None)],
            scratch=[pltpu.VMEM((width, model), F32)],
        )
        out_grad = (own + over_core(other).astype(F32)).astype(BF16)
        pending = [out_grad, up_weight_grad, down_grad]
        if top_layer:
            feed_chain = Chain(sums, piled(2 * units, up_weight_grad, down_grad), pair_order)
            pending = [out_grad, feed_chain.advance()]
        else:
            strands = [
                Chain(sums, up_weight_grad, pair_order),
                Chain(sums, down_grad, other_order),
            ]
            pending = [
                out_grad,
                upper.advance(first_sums[2]),
                feed_chain.advance(first_sums[2]),
                *[strand.advance() for strand in strands],
            ]
        half_shape = (chunks, CHUNK, 256)
        q_grads, kv_owns, kv_recvs = [], [], []
        for pair in range(head_count // 2):
            q_grad, kv_grad, kv_grad_other = call(
                functools.partial(attend_back_kernel, pair, head_count, chunks),
                None,
                [(bits, smem)]
                + [
                    (value, ON_CHIP)
                    for value in [keep["kv_all"], keep["turned"], q_labels, k_labels]
                    + keep["queries"]
                    + context_grad
                    + keep["exact"]
                    + keep["logsum"]
                ],
                [
                    ((lane, 128), BF16, ON_CHIP, None),
                    (half_shape, F32, ON_CHIP, None),
                    (half_shape, BF16, ON_CHIP, None),
                ],
                scratch=[
                    pltpu.VMEM((2 * CHUNK, 128), BF16),
                    pltpu.VMEM((2 * CHUNK, 128), BF16),
                    pltpu.VMEM((8, 2 * CHUNK), F32),
                    pltpu.VMEM((128, CHUNK), F32),
                    pltpu.VMEM((tiles, CHUNK, 256), F32),
                ],
                cost=0,
                limit=16,
                after=pending + q_grads[-1:],
            )
            pending = []
            if not top_layer:
                pending = [upper.advance(q_grad)]
                if pair == 0:
                    pending.append(feed_chain.advance(q_grad))
                if pair == 2:
                    up_out, down_out = unpacked_rows(
                        1, feed_chain, [square, square[::-1]], [None] * 2, after=[q_grad]
                    )
                    pending.append(up_out)
                if pair > 0:
                    pending += [strand.advance(q_grad) for strand in strands]
            elif pair == 2:
                pending = [feed_chain.advance(q_grad)]
            q_grads.append(q_grad)
            kv_owns.append(kv_grad)
            kv_recvs.append(over_core(gate(kv_grad_other, *pending)))
        joint_own, joint_other, bias_sums, joint_share = [], [], [], []
        for i in range(chunks):
            outs = call(
                functools.partial(joint_back_kernel, layer, i),
                None,
                [(core_number, smem)]
                + [(value, ON_CHIP) for value in q_grads + kv_owns + kv_recvs + [qw, kvw]],
                [
                    ((CHUNK, 3 * local), BF16, ON_CHIP, None),
                    ((CHUNK, 3 * local), BF16, ON_CHIP, None),
                    ((8, width), F32, ON_CHIP, None),
                    (block, BF16, ON_CHIP, None),
                ],
                cost=0,
            )
            for target, value in zip((joint_own, joint_other, bias_sums, joint_share), outs):
                target.append(value)
        vector_sums[layer] = call(
            vectors_kernel,
            None,
            [(sums.numbers, smem)]
            + [(value, ON_CHIP) for value in second_sums[-1:] + first_sums[-1:] + unit_sums[-1:] + bias_sums],
            [((8, model), F32, ON_CHIP, None), ((8, model), F32, ON_CHIP, None)],
        )
        if layer > 0:
            joint_recv = [over_chip(part) for part in joint_share]
        joint_other_grad = weight_grad(joint_other, keep["low_in"], (3 * local, model))
        if layer == 0:
            buckets_total = type_table.shape[0]
            half_table = buckets_total // 2
            table_mine, table_sent = call(
                functools.partial(table_kernel, chunks, share),
                None,
                [
                    (value, smem if value is sums.numbers else ON_CHIP)
                    for value in [sums.numbers, lane_buckets.reshape(chunks, 1, CHUNK)]
                    + joint_share
                    + first_total
                    + [*vector_sums[0], *vector_sums[1]]
                ],
                [
                    ((half_table + 16, model), F32, ON_CHIP, None),
                    ((half_table + 16, model), BF16, ON_CHIP, None),
                ],
                scratch=[pltpu.VMEM((buckets_total, model), F32)],
                cost=0,
                after=[joint_other_grad],
            )
            table_recv = over_core(table_sent)
        joint_recv_grad = over_core(joint_other_grad)
        if layer == 0:
            table_both, table_low = call(
                table_add_kernel,
                None,
                [(table_mine, ON_CHIP), (table_recv, ON_CHIP)],
                [
                    ((half_table + 16, model), F32, ON_CHIP, None),
                    ((half_table, model), BF16, ON_CHIP, None),
                ],
            )
        joint_grad = weight_grad(
            joint_own, keep["low_in"], (3 * local, model), received=[joint_recv_grad]
        )
        flat = [(local, model)] * 4
        if layer > 0:
            upper = Chain(sums, piled(4 * local, joint_grad, out_grad), other_order)

    second_chain = Chain(
        sums, piled(10 * half_table // 2, joint_grad[local:], out_grad), other_order
    )
    second_sent = second_chain.advance()
    table_other = over_chip(table_low)
    (tokens_sent,) = call(
        tokens_send_kernel,
        None,
        [(sums.numbers, smem)] + [(part, ON_CHIP) for part in joint_share],
        [((share, model), BF16, ON_CHIP, None)],
        after=[table_low],
    )
    tokens_recv = over_chip(tokens_sent)
    (packed,) = call(
        pack_kernel,
        None,
        [(value, ON_CHIP) for value in (joint_grad[:local], table_both, table_low, table_other)],
        [((3 * half_table, model), BF16, ON_CHIP, None)],
    )
    first_chain = Chain(sums, packed, pair_order)
    token = first_chain.advance()
    for step in range(5):
        for strand in strands:
            if strand.step < 6:
                token = strand.advance(token)
        token = second_chain.advance(token)
        if upper.step < 6:
            token = upper.advance(token)
        token = first_chain.advance(token)
        if step == 0:
            turned_out = unpacked_rows(1, upper, flat, [None] * 4, after=[token])
            token = strands[0].advance(turned_out[0])
        if step == 3:
            (tokens_grad,) = call(
                functools.partial(tokens_kernel, chunks),
                (1,),
                [(sums.numbers, smem)]
                + [
                    (value, whole(value.shape))
                    for value in joint_share + first_total + [tokens_recv]
                ],
                [((share, model), F32, whole((share, model)), None)],
                scratch=[pltpu.VMEM((share, model), BF16)],
                after=[token],
            )
            token = tokens_grad
        if step == 4:
            (up_out,) = unpacked_rows(0, strands[0], [square], [up_out], after=[token])
            (down_out,) = unpacked_rows(0, strands[1], [square[::-1]], [down_out])
    k_out, v_out, o_out = unpacked_rows(0, second_chain, flat[:3], turned_out[1:])
    shapes = [(LAYERS, model)] * 7 + [(LAYERS, local)] * 2
    q_out, table_half, *vector_out = call(
        functools.partial(vectors_unpack_kernel, Wide.PLACES[pair_order]),
        (1,),
        [(sums.numbers, smem)] + [(value, whole(value.shape)) for value in first_chain.finish()],
        [
            ((LAYERS, local, model), F32, layer_spec(0, (local, model)), turned_out[0]),
            ((half_table, model), BF16, whole((half_table, model)), None),
        ]
        + [(shape, F32, whole(shape), None) for shape in shapes],
        scratch=[pltpu.VMEM((first_chain.rows, model), F32)],
    )
    table_grad = by_core(table_half, over_core(table_half), 0).astype(F32)

    return (
        own_encoded,
        tokens_grad,
        table_grad,
        jnp.swapaxes(q_out, 1, 2),
        vector_out[7],
        jnp.swapaxes(k_out, 1, 2),
        jnp.swapaxes(v_out, 1, 2),
        vector_out[8],
        o_out,
        vector_out[5],
        vector_out[3],
        vector_out[4],
        up_out,
        vector_out[6],
        down_out,
        vector_out[2],
        vector_out[0],
        vector_out[1],
    )


def solution(mesh):
    rows = P(("wide", "narrow"), None)
    third = P(None, None, "narrow")
    second = P(None, "narrow")
    middle = P(None, "narrow", None)
    in_specs = (
        rows,
        P(("wide", "narrow")),
        P("wide", None),
        P(),
        third,
        second,
        third,
        third,
        second,
        middle,
        P(),
        P(),
        P(),
        third,
        second,
        middle,
        P(),
        P(),
        P(),
        rows,
    )
    out_specs = (
        rows,
        rows,
        P(),
        third,
        second,
        third,
        third,
        second,
        middle,
        P(),
        P(),
        P(),
        third,
        second,
        middle,
        P(),
        P(),
        P(),
    )
    return jax.shard_map(
        functools.partial(on_device, mesh.shape["wide"]),
        mesh=mesh,
        in_specs=in_specs,
        out_specs=out_specs,
        check_vma=False,
    )
```

```python
import functools

import jax
import jax.numpy as jnp
from jax import lax
from jax.experimental import pallas as pl
from jax.experimental.pallas import tpu as pltpu
from jax.sharding import PartitionSpec as P

HEAD_DIM = 64
LAYERS = 2
CHUNK = 256
EPS = 1e-12
ROOT_HALF = 0.7071067811865476
DENSITY = 0.3989422804014327
NEG = -1e30
F32 = jnp.float32
BF16 = jnp.bfloat16
MIB = 1 << 20
CORE_SWAP = [(0, 1), (1, 0), (2, 3), (3, 2)]
CHIP_SWAP = [(0, 2), (2, 0), (1, 3), (3, 1)]


def over_core(value):
    return lax.ppermute(value, "narrow", CORE_SWAP)


def over_chip(value):
    return lax.ppermute(value, "narrow", CHIP_SWAP)


def dot(left, right, left_axis=1, right_axis=0):
    return lax.dot_general(
        left, right, (((left_axis,), (right_axis,)), ((), ())), preferred_element_type=F32
    )


def norm_parts(summed):
    row_mean = jnp.mean(summed, -1, keepdims=True)
    centred = summed - row_mean
    spread = jnp.mean(centred * centred, -1, keepdims=True)
    inverse = lax.rsqrt(spread + EPS)
    return centred * inverse, inverse


def norm_back(upstream, unit_rows, inverse, gain_row):
    scaled = upstream * gain_row
    return inverse * (
        scaled
        - jnp.mean(scaled, -1, keepdims=True)
        - unit_rows * jnp.mean(scaled * unit_rows, -1, keepdims=True)
    )


def gelu_parts(preact):
    size = jnp.abs(preact) * ROOT_HALF
    bell = jnp.exp(-(size * size))
    step = 1.0 / (1.0 + 0.3275911 * size)
    series = step * (
        0.254829592
        + step * (-0.284496736 + step * (1.421413741 + step * (-1.453152027 + step * 1.061405429)))
    )
    tail = 0.5 * series * bell
    cdf = jnp.where(preact >= 0.0, 1.0 - tail, tail)
    return preact * cdf, cdf + preact * DENSITY * bell


ON_CHIP = pl.BlockSpec(memory_space=pltpu.VMEM)


def whole(shape):
    zeros = (0,) * len(shape)
    return pl.BlockSpec(shape, lambda *ids: zeros)


def call(kernel, grid, inputs, outputs, scratch=(), cost=0, limit=16, after=()):
    arrays = [array for array, spec in inputs]
    specs = [spec for array, spec in inputs]
    aliases = {}
    for place, (shape, dtype, spec, buffer) in enumerate(outputs):
        if buffer is not None:
            aliases[len(arrays)] = place
            arrays.append(buffer)
            specs.append(pl.BlockSpec(memory_space=pl.ANY))
    for array in after:
        arrays.append(array)
        specs.append(pl.BlockSpec(memory_space=pl.ANY))
    given, extra = len(inputs), len(aliases) + len(after)

    def body(*refs):
        kernel(*refs[:given], *refs[given + extra :])

    return pl.pallas_call(
        body,
        **({} if grid is None else {"grid": grid}),
        in_specs=specs,
        out_specs=[spec for shape, dtype, spec, buffer in outputs],
        out_shape=[
            jax.ShapeDtypeStruct(shape, dtype) for shape, dtype, spec, buffer in outputs
        ],
        scratch_shapes=list(scratch),
        input_output_aliases=aliases,
        compiler_params=pltpu.CompilerParams(vmem_limit_bytes=limit * MIB),
        cost_estimate=pl.CostEstimate(flops=cost * 4000000000, bytes_accessed=1, transcendentals=0),
    )(*arrays)


def gather_kernel(*refs):
    sources, (rows_ref, turned_ref) = refs[:-2], refs[-2:]
    for place, source in enumerate(sources):
        tile = source[...]
        rows_ref[place] = tile
        turned_ref[place] = tile.astype(F32).T.astype(BF16)


def split_pairs(pair_block, target, head_count):
    lanes = lax.broadcasted_iota(jnp.int32, (CHUNK, 2 * HEAD_DIM), 1)
    low_half = lanes < HEAD_DIM
    for head in range(head_count):
        pair = pair_block[:, (head // 2) * 128 : (head // 2) * 128 + 128]
        keep = low_half if head % 2 == 0 else jnp.logical_not(low_half)
        target[head * CHUNK : (head + 1) * CHUNK, :] = jnp.where(keep, pair, jnp.zeros_like(pair))


def attend_kernel(
    head_count,
    layer,
    place,
    bits_ref,
    q_ref,
    kv_ref,
    turned_ref,
    q_label_ref,
    k_label_ref,
    out_weight_ref,
    context_ref,
    exact_ref,
    logsum_ref,
    share_ref,
    masked_q,
    total,
    top,
    mass,
    score_tiles,
):
    width = head_count * HEAD_DIM
    split_pairs(q_ref[...], masked_q, head_count)
    top[...] = jnp.full_like(top, NEG)
    mass[...] = jnp.zeros_like(mass)
    total[...] = jnp.zeros_like(total)
    tiles = kv_ref.shape[0]
    q_bits = bits_ref[tiles + place]

    def score_tile(tile, carry):
        @pl.when((bits_ref[tile] & q_bits) != 0)
        def _():
            hide = jnp.where(k_label_ref[tile] == q_label_ref[place], 0.0, NEG)
            hide = jnp.concatenate([hide, hide], 1)
            for pair in range(head_count // 2):
                lanes = slice(pair * 128, pair * 128 + 128)
                rows = slice(2 * pair * CHUNK, 2 * (pair + 1) * CHUNK)
                scores = dot(kv_ref[tile, :, lanes], masked_q[rows, :], 1, 1) + hide
                score_tiles[pair, tile] = scores
                highest = jnp.max(scores.reshape(-1, 8, 2 * CHUNK), 0)
                top[pair] = jnp.maximum(top[pair], highest)

        return carry

    lax.fori_loop(0, tiles, score_tile, 0)
    for pair in range(head_count // 2):
        top[pair] = jnp.broadcast_to(jnp.max(top[pair], 0, keepdims=True), (8, 2 * CHUNK))

    def weigh_tile(tile, carry):
        @pl.when((bits_ref[tile] & q_bits) != 0)
        def _():
            for pair in range(head_count // 2):
                weights = jnp.exp(score_tiles[pair, tile] - top[pair, 0:1, :])
                mass[pair] += jnp.sum(weights.reshape(-1, 8, 2 * CHUNK), 0)
                low = weights.astype(BF16)
                for side in range(2):
                    start = (2 * pair + side) * HEAD_DIM
                    total[start : start + HEAD_DIM, :] += dot(
                        turned_ref[tile, width + start : width + start + HEAD_DIM, :],
                        low[:, side * CHUNK : (side + 1) * CHUNK],
                    )

        return carry

    lax.fori_loop(0, tiles, weigh_tile, 0)
    logsum_ref[...] = jnp.zeros_like(logsum_ref)
    for head in range(head_count):
        rows = slice(head * HEAD_DIM, (head + 1) * HEAD_DIM)
        lanes = slice((head % 2) * CHUNK, (head % 2 + 1) * CHUNK)
        amount = jnp.sum(mass[head // 2][:, lanes], 0, keepdims=True)
        total[rows, :] = total[rows, :] / amount
        logsum_ref[head : head + 1, :] = top[head // 2, 0:1, lanes] + jnp.log(amount)
    exact = total[...].T
    exact_ref[...] = exact
    context = exact.astype(BF16)
    context_ref[...] = context
    share_ref[...] = dot(context, out_weight_ref[layer]).astype(BF16)


def attend_back_kernel(pair, head_count, chunks, *refs):
    bits_ref, kv_ref, turned_ref, q_label_ref, k_label_ref = refs[:5]
    q_refs, grad_refs, exact_refs, logsum_refs = (
        refs[5 + chunks * k : 5 + chunks * (k + 1)] for k in range(4)
    )
    q_grad_ref, own_ref, other_ref, masked_q, masked_grad, centre, q_total, kv_total = refs[
        5 + 4 * chunks :
    ]
    tiles = kv_ref.shape[0]
    lanes = slice(pair * 128, pair * 128 + 128)
    v_lanes = slice(head_count * HEAD_DIM + pair * 128, head_count * HEAD_DIM + pair * 128 + 128)
    kv_total[...] = jnp.zeros_like(kv_total)
    for place in range(chunks):
        split_pairs(q_refs[place][:, lanes], masked_q, 2)
        split_pairs(grad_refs[place][:, lanes], masked_grad, 2)
        crossed = (grad_refs[place][:, lanes].astype(F32) * exact_refs[place][:, lanes]).T
        for head in range(2):
            rows = slice(head * HEAD_DIM, (head + 1) * HEAD_DIM)
            side = slice(head * CHUNK, (head + 1) * CHUNK)
            number = 2 * pair + head
            centre[0:1, side] = jnp.sum(crossed[rows, :], 0, keepdims=True)
            centre[2:3, side] = logsum_refs[place][number : number + 1, :]
        q_total[...] = jnp.zeros_like(q_total)
        q_bits = bits_ref[tiles + place]

        def one_tile(tile, carry):
            @pl.when((bits_ref[tile] & q_bits) != 0)
            def _():
                hide = jnp.where(k_label_ref[tile] == q_label_ref[place], 0.0, NEG)
                hide = jnp.concatenate([hide, hide], 1)
                scores = dot(kv_ref[tile, :, lanes], masked_q[...], 1, 1) + hide
                weight_grad = dot(kv_ref[tile, :, v_lanes], masked_grad[...], 1, 1)
                weights = jnp.exp(scores - centre[2:3, :])
                score_grad = (weights * (weight_grad - centre[0:1, :])).astype(BF16)
                kv_total[tile, :, 128:] += dot(weights.astype(BF16), masked_grad[...])
                kv_total[tile, :, :128] += dot(score_grad, masked_q[...])
                for side in range(2):
                    rows = slice(side * HEAD_DIM, (side + 1) * HEAD_DIM)
                    turned = slice((2 * pair + side) * HEAD_DIM, (2 * pair + side + 1) * HEAD_DIM)
                    q_total[rows, :] += dot(
                        turned_ref[tile, turned, :],
                        score_grad[:, side * CHUNK : (side + 1) * CHUNK],
                    )

            return carry

        lax.fori_loop(0, tiles, one_tile, 0)
        q_grad_ref[place * CHUNK : (place + 1) * CHUNK, :] = q_total[...].T.astype(
            BF16
        ) * jnp.asarray(HEAD_DIM**-0.5, BF16)
    own_ref[...] = kv_total[: tiles // 2]
    other_ref[...] = kv_total[tiles // 2 :].astype(BF16)


def weight_grad_kernel(chunks, left_start, right_start, *refs):
    lefts, rights, recv_refs = refs[:chunks], refs[chunks : 2 * chunks], refs[2 * chunks : -1]
    out_ref = refs[-1]
    rows, columns = out_ref.shape
    step = CHUNK if rows % CHUNK == 0 else rows
    for start in range(0, rows, step):
        left_lanes = slice(left_start + start, left_start + start + step)
        right_lanes = slice(right_start, right_start + columns)
        total = None
        for left, right in zip(lefts, rights):
            part = dot(left[:, left_lanes], right[:, right_lanes], 0, 0)
            total = part if total is None else total + part
        for recv_ref in recv_refs:
            total = total + recv_ref[start : start + step, :].astype(F32)
        out_ref[start : start + step, :] = total.astype(out_ref.dtype)


def out_grad_kernel(chunks, core_ref, *refs):
    lefts, rights, (own_ref, other_ref, full) = refs[:chunks], refs[chunks:-3], refs[-3:]
    total = None
    for left, right in zip(lefts, rights):
        part = dot(left[...], right[...], 0, 0)
        total = part if total is None else total + part
    full[...] = total
    local = own_ref.shape[0]
    own_ref[...] = full[pl.ds(pl.multiple_of(core_ref[0] * local, local), local), :]
    other_ref[...] = full[pl.ds(pl.multiple_of((1 - core_ref[0]) * local, local), local), :].astype(
        BF16
    )


def feed_kernel(
    layer,
    place,
    unit_ref,
    share_ref,
    recv_ref,
    vec_ref,
    up_own_ref,
    up_other_ref,
    bias_ref,
    down_own_ref,
    down_other_ref,
    new_unit_ref,
    inverse_ref,
    low_ref,
    act_ref,
    slope_ref,
    part_ref,
):
    stream = unit_ref[...] * vec_ref[layer, 6:7, :] + vec_ref[layer, 7:8, :]
    attention = share_ref[...].astype(F32) + recv_ref[...].astype(F32)
    unit, inverse = norm_parts(stream + attention + vec_ref[layer, 0:1, :])
    new_unit_ref[...] = unit
    inverse_ref[...] = inverse
    low_ref[...] = (unit * vec_ref[layer, 1:2, :] + vec_ref[layer, 2:3, :]).astype(BF16)
    units = up_own_ref.shape[2]
    total = None
    for half, (up_ref, down_ref) in enumerate(
        ((up_own_ref, down_own_ref), (up_other_ref, down_other_ref))
    ):
        lanes = slice(half * units, (half + 1) * units)
        act, slope = gelu_parts(dot(low_ref[...], up_ref[layer]) + bias_ref[layer, :, lanes])
        low_act = act.astype(BF16)
        act_ref[:, lanes] = low_act
        slope_ref[:, lanes] = slope.astype(BF16)
        part = dot(low_act, down_ref[layer])
        total = part if total is None else total + part
    part_ref[...] = total.astype(BF16)


def project_kernel(
    layer,
    place,
    unit_ref,
    share_ref,
    recv_ref,
    vec_ref,
    q_weight_ref,
    kv_weight_ref,
    q_bias_ref,
    kv_bias_ref,
    new_unit_ref,
    inverse_ref,
    low_ref,
    q_ref,
    kv_ref,
):
    old = layer - 1
    middle = unit_ref[...] * vec_ref[old, 1:2, :] + vec_ref[old, 2:3, :]
    feed = share_ref[...].astype(F32) + recv_ref[...].astype(F32)
    unit, inverse = norm_parts(middle + feed + vec_ref[old, 3:4, :])
    new_unit_ref[...] = unit
    inverse_ref[...] = inverse
    low = (unit * vec_ref[old, 4:5, :] + vec_ref[old, 5:6, :]).astype(BF16)
    low_ref[...] = low
    kv_ref[...] = (dot(low, kv_weight_ref[layer], 1, 1) + kv_bias_ref[layer]).astype(BF16)
    q_ref[...] = (
        (dot(low, q_weight_ref[layer], 1, 1) + q_bias_ref[layer]) * HEAD_DIM**-0.5
    ).astype(BF16)


def feed_back_kernel(
    layer,
    place,
    top_layer,
    up_ref,
    unit_ref,
    inverse_ref,
    share_ref,
    recv_ref,
    vec_ref,
    slope_ref,
    up_own_ref,
    up_other_ref,
    down_own_ref,
    down_other_ref,
    *rest,
):
    before = rest[:-7]
    encoded_ref, total_ref, low_ref, grad_ref, bias_ref, sums_ref, part_ref = rest[-7:]
    keep_span = slice(place * CHUNK, (place + 1) * CHUNK)
    added = share_ref[...].astype(F32) + recv_ref[...].astype(F32)
    if top_layer:
        middle = unit_ref[...] * vec_ref[layer, 1:2, :] + vec_ref[layer, 2:3, :]
        unit, inverse = norm_parts(middle + added + vec_ref[layer, 3:4, :])
        encoded_ref[...] = (unit * vec_ref[layer, 4:5, :] + vec_ref[layer, 5:6, :]).astype(BF16)
        upstream = up_ref[keep_span, :].astype(F32)
    else:
        unit = unit_ref[...]
        inverse = inverse_ref[...]
        upstream = up_ref[...] + added
        encoded_ref[...] = jnp.zeros_like(encoded_ref)
    second = norm_back(upstream, unit, inverse, vec_ref[layer, 4:5, :])
    sums_ref[...] = before[0][...] if before else jnp.zeros_like(sums_ref)
    sums_ref[0:1, :] += jnp.sum(upstream * unit, 0, keepdims=True)
    sums_ref[1:2, :] += jnp.sum(upstream, 0, keepdims=True)
    sums_ref[2:3, :] += jnp.sum(second, 0, keepdims=True)
    total_ref[...] = second
    low_ref[...] = second.astype(BF16)
    units = up_own_ref.shape[2]
    total = None
    for half, (up_weight_ref, down_ref) in enumerate(
        ((up_own_ref, down_own_ref), (up_other_ref, down_other_ref))
    ):
        lanes = slice(half * units, (half + 1) * units)
        grad = (
            dot(low_ref[...], down_ref[layer], 1, 1) * slope_ref[:, lanes].astype(F32)
        ).astype(BF16)
        grad_ref[:, lanes] = grad
        bias = jnp.sum(grad.astype(F32), 0, keepdims=True)
        bias_ref[:, lanes] = bias + before[1][:, lanes] if before else bias
        part = dot(grad, up_weight_ref[layer], 1, 1)
        total = part if total is None else total + part
    part_ref[...] = total.astype(BF16)


def context_back_kernel(
    layer,
    place,
    second_ref,
    share_ref,
    recv_ref,
    unit_ref,
    inverse_ref,
    vec_ref,
    out_weight_ref,
    *rest,
):
    before = rest[:-4]
    total_ref, low_ref, grad_ref, sums_ref = rest[-4:]
    added = share_ref[...].astype(F32) + recv_ref[...].astype(F32)
    upstream = second_ref[...] + added
    unit = unit_ref[...]
    first = norm_back(upstream, unit, inverse_ref[...], vec_ref[layer, 1:2, :])
    sums_ref[...] = before[0][...] if before else jnp.zeros_like(sums_ref)
    sums_ref[0:1, :] += jnp.sum(upstream * unit, 0, keepdims=True)
    sums_ref[1:2, :] += jnp.sum(upstream, 0, keepdims=True)
    sums_ref[2:3, :] += jnp.sum(first, 0, keepdims=True)
    total_ref[...] = first
    low = first.astype(BF16)
    low_ref[...] = low
    grad_ref[...] = dot(low, out_weight_ref[layer], 1, 1).astype(BF16)


def joint_back_kernel(
    layer,
    place,
    core_ref,
    *refs,
):
    pairs = (len(refs) - 6) // 3
    q_refs, own_refs, recv_refs = (refs[k * pairs : (k + 1) * pairs] for k in range(3))
    q_weight_ref, kv_weight_ref, mine_ref, theirs_ref, bias_ref, part_ref = refs[3 * pairs :]
    span = slice(place * CHUNK, (place + 1) * CHUNK)
    width = 128 * pairs
    local = width // 2
    q_grad = jnp.concatenate([ref[span, :] for ref in q_refs], 1)
    both = [
        (own[place] + recv[place].astype(F32)).astype(BF16)
        for own, recv in zip(own_refs, recv_refs)
    ]
    kv_grad = jnp.concatenate(
        [part[:, :128] for part in both] + [part[:, 128:] for part in both], 1
    )
    first = core_ref[0] == 0
    for member, value in enumerate((q_grad, kv_grad[:, :width], kv_grad[:, width:])):
        left, right = value[:, :local].astype(F32), value[:, local:].astype(F32)
        lanes = slice(member * local, (member + 1) * local)
        mine_ref[:, lanes] = jnp.where(first, left, right).astype(BF16)
        theirs_ref[:, lanes] = jnp.where(first, right, left).astype(BF16)
    bias_ref[...] = jnp.zeros_like(bias_ref)
    bias_ref[0:1, :] = jnp.sum(q_grad.astype(F32), 0, keepdims=True)
    bias_ref[1:2, :] = jnp.sum(kv_grad[:, width:].astype(F32), 0, keepdims=True)
    part_ref[...] = (
        dot(q_grad, q_weight_ref[layer]) + dot(kv_grad, kv_weight_ref[layer])
    ).astype(BF16)


def weights_kernel(core_ref, *refs):
    sources, vectors, small_ref, other_ref = refs[:8], refs[8:14], refs[14], refs[15]
    q_ref, kv_ref, out_ref, vec_ref, q_bias_ref, kv_bias_ref, unit_bias_ref = refs[16:]
    local = sources[0].shape[1]
    width = 2 * local
    own_row = pl.multiple_of(core_ref[0] * local, local)
    other_row = pl.multiple_of((1 - core_ref[0]) * local, local)
    for layer in range(LAYERS):
        for member, (target, start) in enumerate(
            ((q_ref, 0), (kv_ref, 0), (kv_ref, width), (out_ref, 0))
        ):
            target[layer, pl.ds(start + own_row, local), :] = sources[2 * member][layer]
            target[layer, pl.ds(start + other_row, local), :] = sources[2 * member + 1][layer]

    first = core_ref[0] == 0
    for layer in range(LAYERS):
        row = slice(layer, layer + 1)
        for member, vector in enumerate(vectors):
            vec_ref[layer, member : member + 1, :] = vector[...].astype(F32)[row]
        if layer == 0:
            vec_ref[layer, 6:7, :] = jnp.ones_like(vec_ref[layer, 6:7, :])
            vec_ref[layer, 7:8, :] = jnp.zeros_like(vec_ref[layer, 7:8, :])
        else:
            vec_ref[layer, 6:8, :] = vec_ref[layer - 1, 4:6, :]
        own = small_ref[...].astype(F32)[row]
        other = other_ref[...].astype(F32)[row]
        kv_bias_ref[layer] = jnp.zeros_like(kv_bias_ref[layer])
        for target, start, lanes in (
            (q_bias_ref, 0, slice(0, local)),
            (kv_bias_ref, width, slice(local, width)),
        ):
            left, right = own[:, lanes], other[:, lanes]
            target[layer, :, start : start + local] = jnp.where(first, left, right)
            target[layer, :, start + local : start + width] = jnp.where(first, right, left)
        units = own.shape[1] - width
        unit_bias_ref[layer, :, :units] = own[:, width:]
        unit_bias_ref[layer, :, units:] = other[:, width:]


def halve_kernel(bit, numbers_ref, *refs):
    parts, (sent_ref, kept_ref) = refs[:-2], refs[-2:]
    half = sent_ref.shape[0]
    for target, number in ((sent_ref, 1 - numbers_ref[bit]), (kept_ref, numbers_ref[bit])):
        rows = pl.ds(pl.multiple_of(number * half, half), half)
        target[...] = sum(part[rows, :].astype(F32) for part in parts).astype(target.dtype)


def add_kernel(kept_ref, recv_ref, piece_ref):
    piece_ref[0] = (kept_ref[...] + recv_ref[...].astype(F32)).astype(BF16)


def join_kernel(pieces_ref, recv_ref, joined_ref):
    count = pieces_ref.shape[0]
    joined_ref[:count] = pieces_ref[...]
    joined_ref[count:] = recv_ref[...]


def arrange(place, pieces_ref, recv_ref, full):
    count, rows = pieces_ref.shape[0], pieces_ref.shape[1]
    for number in range(2 * count):
        source = pieces_ref[number] if number < count else recv_ref[number - count]
        start = pl.multiple_of((number ^ place) * rows, rows)
        full[pl.ds(start, rows), :] = source.astype(F32)


def unpack_kernel(place, numbers_ref, pieces_ref, recv_ref, *refs):
    targets, full = refs[:-1], refs[-1]
    arrange(numbers_ref[place], pieces_ref, recv_ref, full)
    start = 0
    for target in targets:
        rows = target.shape[-2]
        value = full[start : start + rows, :]
        if len(target.shape) == 3:
            target[0] = value
        else:
            target[...] = value.astype(target.dtype)
        start += rows


def vectors_unpack_kernel(place, numbers_ref, pieces_ref, recv_ref, *refs):
    q_ref, table_ref, targets, full = refs[0], refs[1], refs[2:-1], refs[-1]
    arrange(numbers_ref[place], pieces_ref, recv_ref, full)
    local = q_ref.shape[1]
    half = table_ref.shape[0]
    q_ref[0] = full[:local, :]
    table_ref[...] = full[local : local + half, :].astype(BF16)
    for layer in range(LAYERS):
        start = local + half + 8 * layer
        row = slice(layer, layer + 1)
        for member in range(7):
            targets[member][row, :] = full[start + member : start + member + 1, :]
        last = full[start + 7 : start + 8, :]
        for member in range(2):
            targets[7 + member][row, :] = last[:, member * local : (member + 1) * local]


def table_kernel(chunks, share, numbers_ref, bucket_ref, *refs):
    joints, firsts = refs[:chunks], refs[chunks : 2 * chunks]
    vectors = refs[2 * chunks : -3]
    mine_ref, sent_ref, full = refs[-3:]
    buckets, half = full.shape[0], full.shape[0] // 2
    chip, core = numbers_ref[1], numbers_ref[0]
    numbers = lax.broadcasted_iota(jnp.int32, (buckets, CHUNK), 0)
    places = lax.broadcasted_iota(jnp.int32, (buckets, CHUNK), 1)
    total = None
    for place in range(chunks):
        hit = numbers == bucket_ref[place]
        rows = places + place * CHUNK
        mine = jnp.logical_and(rows >= chip * share, rows < (chip + 1) * share)
        every = jnp.where(hit, 1.0, 0.0).astype(BF16)
        own = jnp.where(jnp.logical_and(hit, mine), 1.0, 0.0).astype(BF16)
        first = firsts[place][...]
        high = first.astype(BF16)
        rest = (first - high.astype(F32)).astype(BF16)
        part = dot(every, joints[place][...]) + (dot(own, high) + dot(own, rest))
        total = part if total is None else total + part
    full[...] = total
    mine_ref[:half, :] = full[pl.ds(pl.multiple_of(core * half, half), half), :]
    sent_ref[:half, :] = full[pl.ds(pl.multiple_of((1 - core) * half, half), half), :].astype(BF16)
    for layer in range(LAYERS):
        rows = slice(half + 8 * layer, half + 8 * layer + 8)
        mine_ref[rows, :] = vectors[2 * layer][...]
        sent_ref[rows, :] = vectors[2 * layer + 1][...].astype(BF16)


def vectors_kernel(numbers_ref, second_ref, first_ref, unit_ref, *refs):
    mine_ref, sent_ref = refs[-2:]
    second, first, unit = second_ref[...], first_ref[...], unit_ref[...]
    bias = sum(ref[...] for ref in refs[:-2])
    units, local = unit.shape[1] // 2, bias.shape[1] // 2
    low = numbers_ref[0] == 0
    for target, lanes, flip in (
        (mine_ref, slice(0, units), False),
        (sent_ref, slice(units, 2 * units), True),
    ):
        target[0:3, :] = second[0:3, :]
        target[3:6, :] = first[0:3, :]
        target[6:7, :] = unit[:, lanes]
        target[7:8, :] = jnp.zeros_like(target[7:8, :])
        for member in range(2):
            left, right = bias[member : member + 1, :local], bias[member : member + 1, local:]
            if flip:
                left, right = right, left
            target[7:8, member * local : (member + 1) * local] = jnp.where(low, left, right)


def table_add_kernel(mine_ref, recv_ref, both_ref, sent_ref):
    total = mine_ref[...] + recv_ref[...].astype(F32)
    both_ref[...] = total
    sent_ref[...] = total[: sent_ref.shape[0], :].astype(BF16)


def pack_kernel(q_ref, both_ref, sent_ref, recv_ref, packed_ref):
    local, half, rows = q_ref.shape[0], sent_ref.shape[0], both_ref.shape[0]
    packed_ref[...] = jnp.zeros_like(packed_ref)
    packed_ref[:local, :] = q_ref[...]
    table = sent_ref[...].astype(F32) + recv_ref[...].astype(F32)
    packed_ref[local : local + half, :] = table.astype(BF16)
    packed_ref[local + half : local + rows, :] = both_ref[half:, :].astype(BF16)


def pile_kernel(*refs):
    sources, target = refs[:-1], refs[-1]
    start = 0
    for source in sources:
        rows = source.shape[0]
        target[start : start + rows, :] = source[...].astype(target.dtype)
        start += rows
    if start < target.shape[0]:
        target[start:, :] = jnp.zeros_like(target[start:, :])


def pick_rows(chip, chunk_refs, share, target):
    for number in range(2):

        @pl.when(chip == number)
        def _():
            start, end = number * share, (number + 1) * share
            for place, ref in enumerate(chunk_refs):
                low, high = max(start, place * CHUNK), min(end, (place + 1) * CHUNK)
                if low < high:
                    target[low - start : high - start, :] = ref[
                        low - place * CHUNK : high - place * CHUNK, :
                    ]


def own_rows_kernel(numbers_ref, *refs):
    pick_rows(numbers_ref[1], refs[:-1], refs[-1].shape[0], refs[-1])


def tokens_send_kernel(numbers_ref, *refs):
    pick_rows(1 - numbers_ref[1], refs[:-1], refs[-1].shape[0], refs[-1])


def tokens_kernel(chunks, numbers_ref, *refs):
    joints, firsts = refs[:chunks], refs[chunks : 2 * chunks]
    recv_ref, target, own = refs[2 * chunks :]
    share = target.shape[0]
    pick_rows(numbers_ref[1], joints, share, own)
    pick_rows(numbers_ref[1], firsts, share, target)
    target[...] += own[...].astype(F32) + recv_ref[...].astype(F32)


class Wide:
    BITS = {"y": (2, 1), "near": (3, 2), "far": (4, 4)}
    PLACES = {("y", "near", "far"): 5, ("near", "y", "far"): 6}

    def __init__(self, size, chip, core):
        self.small, self.size = size == 8, size
        index = lax.axis_index("wide")
        bits = {name: (index >> k) & 1 for k, name in enumerate(("y", "near", "far"))}
        places = [
            sum(bits[name] << (2 - k) for k, name in enumerate(order)) if self.small else 0
            for order in self.PLACES
        ]
        self.numbers = jnp.stack(
            [
                jnp.asarray(value, jnp.int32)
                for value in (core, chip, bits["y"], bits["near"], bits["far"], *places, 0)
            ]
        )

    def pairs(self, name):
        reach = self.BITS[name][1]
        return [(number, number ^ reach) for number in range(self.size)]


def gate(value, *later):
    return lax.optimization_barrier((value,) + later)[0] if later else value


SMEM = pl.BlockSpec(memory_space=pltpu.SMEM)


class Chain:
    def __init__(self, wide, value, order):
        self.wide, self.order, self.step = wide, order, 0
        self.parts, self.rows = [value], value.shape[0]

    def advance(self, *after):
        if not self.wide.small:
            if self.step == 0:
                value = self.parts[0]
                self.parts = lax.psum(value, "wide").reshape(2, 4, -1, value.shape[1])
            self.step = 6
            self.sent = self.parts[0]
            return self.parts[0]
        self.step += 1
        parts = [(part, ON_CHIP) for part in self.parts]
        columns = self.parts[0].shape[-1]
        if self.step <= 3:
            name = self.order[self.step - 1]
            half = (self.parts[0].shape[0] // 2, columns)
            sent, kept = call(
                functools.partial(halve_kernel, Wide.BITS[name][0]),
                None,
                [(self.wide.numbers, SMEM)] + parts,
                [(half, BF16, ON_CHIP, None), (half, F32, ON_CHIP, None)],
                after=after,
            )
            self.parts = [kept, lax.ppermute(sent, "wide", self.wide.pairs(name))]
            self.sent = sent
            return sent
        kernel = add_kernel if self.step == 4 else join_kernel
        shape = self.parts[0].shape
        shape = (1,) + shape if self.step == 4 else (2 * shape[0],) + shape[1:]
        (sent,) = call(kernel, None, parts, [(shape, BF16, ON_CHIP, None)], after=after)
        name = self.order[6 - self.step]
        self.parts = [sent, lax.ppermute(sent, "wide", self.wide.pairs(name))]
        return sent

    def finish(self):
        while self.step < 6:
            self.advance()
        return [self.parts[0], self.parts[1]]


def on_device(wide, *arguments):
    (
        tokens,
        buckets,
        lengths,
        type_table,
        query_weight,
        query_bias,
        key_weight,
        value_weight,
        value_bias,
        output_weight,
        output_bias,
        attention_gain,
        attention_shift,
        up_weight,
        up_bias,
        down_weight,
        down_bias,
        feed_gain,
        feed_shift,
        cotangent,
    ) = arguments
    share, model = tokens.shape
    lane = 2 * share
    chunks = lane // CHUNK
    local = query_weight.shape[2]
    width = 2 * local
    head_count = width // HEAD_DIM
    units = up_weight.shape[2]
    place = lax.axis_index("narrow")
    chip, core = place // 2, place % 2
    first_chip, first_core = chip == 0, core == 0

    def by_core(own, other, axis):
        return jnp.where(
            first_core,
            jnp.concatenate([own, other], axis),
            jnp.concatenate([other, own], axis),
        )

    def by_chip(own, other):
        return jnp.where(
            first_chip, jnp.concatenate([own, other], 0), jnp.concatenate([other, own], 0)
        )

    def own_rows(rows):
        return jnp.where(first_chip, rows[:share], rows[share:])

    def other_rows(rows):
        return jnp.where(first_chip, rows[share:], rows[:share])

    lane_tokens = by_chip(tokens, over_chip(tokens))
    lane_buckets = by_chip(buckets, over_chip(buckets))
    lane_cotangent = by_chip(cotangent, over_chip(cotangent))

    smem = pl.BlockSpec(memory_space=pltpu.SMEM)
    sums = Wide(wide, chip, core)
    core_number = sums.numbers
    shards = []
    turned_weights = [
        jnp.swapaxes(weight, 1, 2) for weight in (query_weight, key_weight, value_weight)
    ]
    for weight in turned_weights + [output_weight]:
        shards += [(weight, ON_CHIP), (over_core(weight), ON_CHIP)]

    small = jnp.concatenate([query_bias, value_bias, up_bias], 1)
    vectors = [
        output_bias,
        attention_gain,
        attention_shift,
        down_bias,
        feed_gain,
        feed_shift,
        small,
        over_core(small),
    ]
    qw, kvw, ow, vec, q_bias, kv_bias, unit_bias = call(
        weights_kernel,
        None,
        [(core_number, smem)] + shards + [(vector, ON_CHIP) for vector in vectors],
        [
            (shape, dtype, ON_CHIP, None)
            for shape, dtype in (
                ((LAYERS, width, model), BF16),
                ((LAYERS, 2 * width, model), BF16),
                ((LAYERS, width, model), BF16),
                ((LAYERS, 8, model), F32),
                ((LAYERS, 1, width), F32),
                ((LAYERS, 1, 2 * width), F32),
                ((LAYERS, 1, 2 * units), F32),
            )
        ],
    )
    up_other = over_core(up_weight)
    down_other = over_core(down_weight)

    ends = jnp.cumsum(lengths[0], dtype=jnp.int32)
    offsets = lax.iota(jnp.int32, share)
    spots = jnp.concatenate(
        [
            offsets + (block * 2 + which) * share
            for which in (core, 1 - core)
            for block in range(2)
        ]
    )
    labels = jnp.sum((spots[:, None] >= ends[None, :]).astype(jnp.int32), 1, dtype=jnp.int32)
    tiles = 2 * chunks
    tile_labels = labels.reshape(tiles, CHUNK)
    present = jnp.any(
        tile_labels[:, :, None] == lax.iota(jnp.int32, lengths.shape[1])[None, None, :], axis=1
    )
    bits = jnp.sum(
        jnp.where(present, jnp.left_shift(1, lax.iota(jnp.int32, lengths.shape[1]))[None, :], 0),
        axis=1,
        dtype=jnp.int32,
    )
    bits = jnp.concatenate([bits, bits[:chunks]])
    k_labels = tile_labels[:, :, None]
    q_labels = tile_labels[:chunks, None, :]

    block = (CHUNK, model)

    def layer_spec(layer, shape):
        return pl.BlockSpec((1,) + shape, lambda *ids: (layer,) + (0,) * len(shape))

    selector = (lane_buckets[:, None] == lax.iota(jnp.int32, type_table.shape[0])[None, :]).astype(
        BF16
    )
    stream = lane_tokens.astype(F32) + dot(selector, type_table)
    low_first = stream.astype(BF16)
    state = [stream[CHUNK * i : CHUNK * (i + 1)] for i in range(chunks)]
    kept = []
    for layer in range(LAYERS):
        keep = {}
        if layer == 0:
            kv = (dot(low_first, kvw[0], 1, 1) + kv_bias[0]).astype(BF16)
            queries = ((dot(low_first, qw[0], 1, 1) + q_bias[0]) * HEAD_DIM**-0.5).astype(BF16)
            low_in, kv, queries = (
                [value[CHUNK * i : CHUNK * (i + 1)] for i in range(chunks)]
                for value in (low_first, kv, queries)
            )
            kv_other = [over_core(part) for part in kv]
        else:
            low_in, queries, kv, kv_other = [], [], [], []
            units_now, inverses = [], []
            for i in range(chunks):
                outs = call(
                    functools.partial(project_kernel, layer, i),
                    None,
                    [
                        (value, ON_CHIP)
                        for value in (
                            state[i],
                            feed_share[i],
                            feed_recv[i],
                            vec,
                            qw,
                            kvw,
                            q_bias,
                            kv_bias,
                        )
                    ],
                    [
                        (block, F32, ON_CHIP, None),
                        ((CHUNK, 1), F32, ON_CHIP, None),
                        (block, BF16, ON_CHIP, None),
                        ((CHUNK, width), BF16, ON_CHIP, None),
                        ((CHUNK, 2 * width), BF16, ON_CHIP, None),
                    ],
                    cost=2,
                )
                units_now.append(outs[0])
                inverses.append(outs[1])
                low_in.append(outs[2])
                queries.append(outs[3])
                kv.append(outs[4])
                kv_other.append(over_core(outs[4]))
            state = units_now
            kept[layer - 1]["second_unit"] = units_now
            kept[layer - 1]["second_inverse"] = inverses
        kv_all, turned = call(
            gather_kernel,
            None,
            [(part, ON_CHIP) for part in kv + kv_other],
            [
                ((tiles, CHUNK, 2 * width), BF16, ON_CHIP, None),
                ((tiles, 2 * width, CHUNK), BF16, ON_CHIP, None),
            ],
            cost=2,
        )
        context, exact, logsum, shares = [], [], [], []
        for i in range(chunks):
            outs = call(
                functools.partial(attend_kernel, head_count, layer, i),
                None,
                [(bits, smem)]
                + [
                    (value, ON_CHIP)
                    for value in (queries[i], kv_all, turned, q_labels, k_labels, ow)
                ],
                [
                    ((CHUNK, width), BF16, ON_CHIP, None),
                    ((CHUNK, width), F32, ON_CHIP, None),
                    ((8, CHUNK), F32, ON_CHIP, None),
                    (block, BF16, ON_CHIP, None),
                ],
                scratch=[
                    pltpu.VMEM((head_count * CHUNK, 128), BF16),
                    pltpu.VMEM((width, CHUNK), F32),
                    pltpu.VMEM((head_count // 2, 8, 2 * CHUNK), F32),
                    pltpu.VMEM((head_count // 2, 8, 2 * CHUNK), F32),
                    pltpu.VMEM((head_count // 2, tiles, CHUNK, 2 * CHUNK), F32),
                ],
                cost=6,
                limit=20,
            )
            for target, value in zip((context, exact, logsum, shares), outs):
                target.append(value)
        received = [over_chip(part) for part in shares]
        low_middle, act, slope, first_unit, first_inverse, feed_share = [], [], [], [], [], []
        for i in range(chunks):
            outs = call(
                functools.partial(feed_kernel, layer, i),
                None,
                [
                    (value, ON_CHIP)
                    for value in (
                        state[i],
                        shares[i],
                        received[i],
                        vec,
                        up_weight,
                        up_other,
                        unit_bias,
                        down_weight,
                        down_other,
                    )
                ],
                [
                    (block, F32, ON_CHIP, None),
                    ((CHUNK, 1), F32, ON_CHIP, None),
                    (block, BF16, ON_CHIP, None),
                    ((CHUNK, 2 * units), BF16, ON_CHIP, None),
                    ((CHUNK, 2 * units), BF16, ON_CHIP, None),
                    (block, BF16, ON_CHIP, None),
                ],
                cost=8,
            )
            for target, value in zip(
                (first_unit, first_inverse, low_middle, act, slope, feed_share), outs
            ):
                target.append(value)
        feed_recv = [over_chip(part) for part in feed_share]
        state = first_unit
        keep.update(
            low_in=low_in,
            queries=queries,
            kv_all=kv_all,
            turned=turned,
            context=context,
            exact=exact,
            logsum=logsum,
            first_unit=first_unit,
            first_inverse=first_inverse,
            low_middle=low_middle,
            act=act,
            slope=slope,
        )
        kept.append(keep)

    pair_order, other_order = ("y", "near", "far"), ("near", "y", "far")

    def unpacked(kernel, layer, sources, shapes, buffers, scratch=(), after=()):
        return call(
            kernel,
            (1,),
            [(source, smem if source is sums.numbers else whole(source.shape)) for source in sources],
            [
                ((LAYERS,) + shape, F32, layer_spec(layer, shape), buffer)
                for shape, buffer in zip(shapes, buffers)
            ],
            scratch,
            after=after,
        )

    def unpacked_rows(layer, chain, shapes, buffers, after=()):
        return unpacked(
            functools.partial(unpack_kernel, Wide.PLACES[chain.order]),
            layer,
            [sums.numbers] + chain.finish(),
            shapes,
            buffers,
            [pltpu.VMEM((chain.rows, model), F32)],
            after,
        )

    def piled(rows, *values):
        return call(
            pile_kernel,
            None,
            [(value, ON_CHIP) for value in values],
            [((rows, model), BF16, ON_CHIP, None)],
        )[0]

    vector_sums = [None] * LAYERS
    encoded = []
    for layer in reversed(range(LAYERS)):
        keep = kept[layer]
        top_layer = layer == LAYERS - 1
        second, low_second, up_grad, unit_sums, second_sums, parts = [], [], [], [], [], []
        for i in range(chunks):
            if top_layer:
                upstream = lane_cotangent
                unit = keep["first_unit"][i]
                inverse = keep["first_inverse"][i]
                added = (feed_share[i], feed_recv[i])
            else:
                upstream = first_total[i]
                unit = keep["second_unit"][i]
                inverse = keep["second_inverse"][i]
                added = (joint_share[i], joint_recv[i])
            outs = call(
                functools.partial(feed_back_kernel, layer, i, top_layer),
                None,
                [
                    (value, ON_CHIP)
                    for value in (
                        upstream,
                        unit,
                        inverse,
                        added[0],
                        added[1],
                        vec,
                        keep["slope"][i],
                        up_weight,
                        up_other,
                        down_weight,
                        down_other,
                        *second_sums[-1:],
                        *unit_sums[-1:],
                    )
                ],
                [
                    (block if top_layer else (8, 128), BF16, ON_CHIP, None),
                    (block, F32, ON_CHIP, None),
                    (block, BF16, ON_CHIP, None),
                    ((CHUNK, 2 * units), BF16, ON_CHIP, None),
                    ((1, 2 * units), F32, ON_CHIP, None),
                    ((8, model), F32, ON_CHIP, None),
                    (block, BF16, ON_CHIP, None),
                ],
                cost=0,
                after=(
                    []
                    if top_layer or i == 1
                    else [upper.advance(), feed_chain.advance(joint_share[2]), vector_sums[1][0]]
                    if i == 0
                    else []
                ),
            )
            if top_layer:
                encoded.append(outs[0])
            for target, value in zip(
                (second, low_second, up_grad, unit_sums, second_sums, parts), outs[1:]
            ):
                target.append(value)
        received = [over_chip(part) for part in parts]

        def weight_grad(lefts, rights, shape, left_start=0, right_start=0, received=()):
            return call(
                functools.partial(weight_grad_kernel, chunks, left_start, right_start),
                None,
                [(value, ON_CHIP) for value in [*lefts, *rights, *received]],
                [(shape, BF16, ON_CHIP, None)],
                cost=0,
            )[0]

        square = (model, units)
        down_other_grad = over_core(
            weight_grad(keep["act"], low_second, square[::-1], left_start=units)
        )
        up_other_grad = over_core(
            weight_grad(keep["low_middle"], up_grad, square, right_start=units)
        )
        down_grad = weight_grad(
            keep["act"], low_second, square[::-1], received=[down_other_grad]
        )
        up_weight_grad = weight_grad(
            keep["low_middle"], up_grad, square, received=[up_other_grad]
        )
        first_total, low_total, context_grad, first_sums = [], [], [], []
        if top_layer:
            (own_encoded,) = call(
                own_rows_kernel,
                (1,),
                [(sums.numbers, smem)] + [(part, whole(block)) for part in encoded],
                [((share, model), BF16, whole((share, model)), None)],
            )
        for i in range(chunks):
            outs = call(
                functools.partial(context_back_kernel, layer, i),
                None,
                [
                    (value, ON_CHIP)
                    for value in (
                        second[i],
                        parts[i],
                        received[i],
                        keep["first_unit"][i],
                        keep["first_inverse"][i],
                        vec,
                        ow,
                        *first_sums[-1:],
                    )
                ],
                [
                    (block, F32, ON_CHIP, None),
                    (block, BF16, ON_CHIP, None),
                    ((CHUNK, width), BF16, ON_CHIP, None),
                    ((8, model), F32, ON_CHIP, None),
                ],
                after=(
                    [own_encoded] * (top_layer and i == 0)
                    if top_layer or i != 1
                    else [upper.advance(second_sums[2]), feed_chain.advance(second_sums[2])]
                ),
            )
            for target, value in zip((first_total, low_total, context_grad, first_sums), outs):
                target.append(value)
        own, other = call(
            functools.partial(out_grad_kernel, chunks),
            None,
            [(core_number, smem)]
            + [(value, ON_CHIP) for value in keep["context"] + low_total],
            [((local, model), F32, ON_CHIP, None), ((local, model), BF16, ON_CHIP, None)],
            scratch=[pltpu.VMEM((width, model), F32)],
        )
        out_grad = (own + over_core(other).astype(F32)).astype(BF16)
        pending = [out_grad, up_weight_grad, down_grad]
        if top_layer:
            feed_chain = Chain(sums, piled(2 * units, up_weight_grad, down_grad), pair_order)
            pending = [out_grad, feed_chain.advance()]
        else:
            strands = [
                Chain(sums, up_weight_grad, pair_order),
                Chain(sums, down_grad, other_order),
            ]
            pending = [
                out_grad,
                upper.advance(first_sums[2]),
                feed_chain.advance(first_sums[2]),
                *[strand.advance() for strand in strands],
            ]
        half_shape = (chunks, CHUNK, 256)
        q_grads, kv_owns, kv_recvs = [], [], []
        for pair in range(head_count // 2):
            q_grad, kv_grad, kv_grad_other = call(
                functools.partial(attend_back_kernel, pair, head_count, chunks),
                None,
                [(bits, smem)]
                + [
                    (value, ON_CHIP)
                    for value in [keep["kv_all"], keep["turned"], q_labels, k_labels]
                    + keep["queries"]
                    + context_grad
                    + keep["exact"]
                    + keep["logsum"]
                ],
                [
                    ((lane, 128), BF16, ON_CHIP, None),
                    (half_shape, F32, ON_CHIP, None),
                    (half_shape, BF16, ON_CHIP, None),
                ],
                scratch=[
                    pltpu.VMEM((2 * CHUNK, 128), BF16),
                    pltpu.VMEM((2 * CHUNK, 128), BF16),
                    pltpu.VMEM((8, 2 * CHUNK), F32),
                    pltpu.VMEM((128, CHUNK), F32),
                    pltpu.VMEM((tiles, CHUNK, 256), F32),
                ],
                cost=0,
                limit=16,
                after=pending + q_grads[-1:],
            )
            pending = []
            if not top_layer:
                pending = [upper.advance(q_grad)]
                if pair == 0:
                    pending.append(feed_chain.advance(q_grad))
                if pair == 2:
                    up_out, down_out = unpacked_rows(
                        1, feed_chain, [square, square[::-1]], [None] * 2, after=[q_grad]
                    )
                    pending.append(up_out)
                if pair > 0:
                    pending += [strand.advance(q_grad) for strand in strands]
            elif pair == 2:
                pending = [feed_chain.advance(q_grad)]
            q_grads.append(q_grad)
            kv_owns.append(kv_grad)
            kv_recvs.append(over_core(gate(kv_grad_other, *pending)))
        joint_own, joint_other, bias_sums, joint_share = [], [], [], []
        for i in range(chunks):
            outs = call(
                functools.partial(joint_back_kernel, layer, i),
                None,
                [(core_number, smem)]
                + [(value, ON_CHIP) for value in q_grads + kv_owns + kv_recvs + [qw, kvw]],
                [
                    ((CHUNK, 3 * local), BF16, ON_CHIP, None),
                    ((CHUNK, 3 * local), BF16, ON_CHIP, None),
                    ((8, width), F32, ON_CHIP, None),
                    (block, BF16, ON_CHIP, None),
                ],
                cost=0,
            )
            for target, value in zip((joint_own, joint_other, bias_sums, joint_share), outs):
                target.append(value)
        vector_sums[layer] = call(
            vectors_kernel,
            None,
            [(sums.numbers, smem)]
            + [(value, ON_CHIP) for value in second_sums[-1:] + first_sums[-1:] + unit_sums[-1:] + bias_sums],
            [((8, model), F32, ON_CHIP, None), ((8, model), F32, ON_CHIP, None)],
        )
        if layer > 0:
            joint_recv = [over_chip(part) for part in joint_share]
        joint_other_grad = weight_grad(joint_other, keep["low_in"], (3 * local, model))
        if layer == 0:
            buckets_total = type_table.shape[0]
            half_table = buckets_total // 2
            table_mine, table_sent = call(
                functools.partial(table_kernel, chunks, share),
                None,
                [
                    (value, smem if value is sums.numbers else ON_CHIP)
                    for value in [sums.numbers, lane_buckets.reshape(chunks, 1, CHUNK)]
                    + joint_share
                    + first_total
                    + [*vector_sums[0], *vector_sums[1]]
                ],
                [
                    ((half_table + 16, model), F32, ON_CHIP, None),
                    ((half_table + 16, model), BF16, ON_CHIP, None),
                ],
                scratch=[pltpu.VMEM((buckets_total, model), F32)],
                cost=0,
                after=[joint_other_grad],
            )
            table_recv = over_core(table_sent)
        joint_recv_grad = over_core(joint_other_grad)
        if layer == 0:
            table_both, table_low = call(
                table_add_kernel,
                None,
                [(table_mine, ON_CHIP), (table_recv, ON_CHIP)],
                [
                    ((half_table + 16, model), F32, ON_CHIP, None),
                    ((half_table, model), BF16, ON_CHIP, None),
                ],
            )
        joint_grad = weight_grad(
            joint_own, keep["low_in"], (3 * local, model), received=[joint_recv_grad]
        )
        flat = [(local, model)] * 4
        if layer > 0:
            upper = Chain(sums, piled(4 * local, joint_grad, out_grad), other_order)

    second_chain = Chain(
        sums, piled(10 * half_table // 2, joint_grad[local:], out_grad), other_order
    )
    second_sent = second_chain.advance()
    table_other = over_chip(table_low)
    (tokens_sent,) = call(
        tokens_send_kernel,
        None,
        [(sums.numbers, smem)] + [(part, ON_CHIP) for part in joint_share],
        [((share, model), BF16, ON_CHIP, None)],
        after=[table_low],
    )
    tokens_recv = over_chip(tokens_sent)
    (packed,) = call(
        pack_kernel,
        None,
        [(value, ON_CHIP) for value in (joint_grad[:local], table_both, table_low, table_other)],
        [((3 * half_table, model), BF16, ON_CHIP, None)],
    )
    first_chain = Chain(sums, packed, pair_order)
    token = first_chain.advance()
    for step in range(5):
        for strand in strands:
            if strand.step < 6:
                token = strand.advance(token)
        token = second_chain.advance(token)
        if upper.step < 6:
            token = upper.advance(token)
        token = first_chain.advance(token)
        if step == 0:
            turned_out = unpacked_rows(1, upper, flat, [None] * 4, after=[token])
            token = strands[0].advance(turned_out[0])
        if step == 3:
            (tokens_grad,) = call(
                functools.partial(tokens_kernel, chunks),
                (1,),
                [(sums.numbers, smem)]
                + [
                    (value, whole(value.shape))
                    for value in joint_share + first_total + [tokens_recv]
                ],
                [((share, model), F32, whole((share, model)), None)],
                scratch=[pltpu.VMEM((share, model), BF16)],
                after=[token],
            )
            token = tokens_grad
            (down_out,) = unpacked_rows(0, strands[1], [square[::-1]], [down_out], after=[token])
            token = down_out
        if step == 4:
            (up_out,) = unpacked_rows(0, strands[0], [square], [up_out], after=[token])
    k_out, v_out, o_out = unpacked_rows(0, second_chain, flat[:3], turned_out[1:])
    shapes = [(LAYERS, model)] * 7 + [(LAYERS, local)] * 2
    q_out, table_half, *vector_out = call(
        functools.partial(vectors_unpack_kernel, Wide.PLACES[pair_order]),
        (1,),
        [(sums.numbers, smem)] + [(value, whole(value.shape)) for value in first_chain.finish()],
        [
            ((LAYERS, local, model), F32, layer_spec(0, (local, model)), turned_out[0]),
            ((half_table, model), BF16, whole((half_table, model)), None),
        ]
        + [(shape, F32, whole(shape), None) for shape in shapes],
        scratch=[pltpu.VMEM((first_chain.rows, model), F32)],
    )
    table_grad = by_core(table_half, over_core(table_half), 0).astype(F32)

    return (
        own_encoded,
        tokens_grad,
        table_grad,
        jnp.swapaxes(q_out, 1, 2),
        vector_out[7],
        jnp.swapaxes(k_out, 1, 2),
        jnp.swapaxes(v_out, 1, 2),
        vector_out[8],
        o_out,
        vector_out[5],
        vector_out[3],
        vector_out[4],
        up_out,
        vector_out[6],
        down_out,
        vector_out[2],
        vector_out[0],
        vector_out[1],
    )


def solution(mesh):
    rows = P(("wide", "narrow"), None)
    third = P(None, None, "narrow")
    second = P(None, "narrow")
    middle = P(None, "narrow", None)
    in_specs = (
        rows,
        P(("wide", "narrow")),
        P("wide", None),
        P(),
        third,
        second,
        third,
        third,
        second,
        middle,
        P(),
        P(),
        P(),
        third,
        second,
        middle,
        P(),
        P(),
        P(),
        rows,
    )
    out_specs = (
        rows,
        rows,
        P(),
        third,
        second,
        third,
        third,
        second,
        middle,
        P(),
        P(),
        P(),
        third,
        second,
        middle,
        P(),
        P(),
        P(),
    )
    return jax.shard_map(
        functools.partial(on_device, mesh.shape["wide"]),
        mesh=mesh,
        in_specs=in_specs,
        out_specs=out_specs,
        check_vma=False,
    )
```
